32 devices in a mesh: dp: 2 (over y), row: 4 (over x, core), col: 4 (over z).
Axes of the slice: x: 2, y: 2, z: 4, core: 2. Of those that a mesh axis runs over, the one named last changes fastest.
Arguments:
- tokens: bfloat16 [8192, 768], P(('dp', 'col', 'row')), may hold values from -6 to 6
- cotangent: bfloat16 [8192, 768], P(('dp', 'col', 'row')), may hold values from -6 to 6
- lengths: int32 [2], P('dp'), may hold values from 1024 to 4096, as said below
- query_weight: float32 [768, 768], P(('row', 'col')), may hold values from -0.21875 to 0.21875
- key_weight: float32 [768, 768], P(('row', 'col')), may hold values from -0.21875 to 0.21875
- value_weight: float32 [768, 768], P(('row', 'col')), may hold values from -0.21875 to 0.21875
- query_bias: float32 [768], P('col'), may hold values from -3 to 3
- value_bias: float32 [768], P('col'), may hold values from -0.1875 to 0.1875
- out_weight: float32 [768, 768], P(('col', 'row')), may hold values from -6 to 6
- out_bias: float32 [768], P('row'), may hold values from -1.75 to 1.75
- norm1_gain: float32 [768], P('row'), may hold values from 0.5 to 1.5
- norm1_shift: float32 [768], P('row'), may hold values from -1.75 to 1.75
- up_weight: float32 [768, 3072], P('row', 'col'), may hold values from -0.21875 to 0.21875
- up_bias: float32 [3072], P('col'), may hold values from -3 to 3
- down_weight: float32 [3072, 768], P(('col', 'row')), may hold values from -0.109375 to 0.109375
- down_bias: float32 [768], P('row'), may hold values from -1.75 to 1.75
- norm2_gain: float32 [768], P('row'), may hold values from 0.5 to 1.5
- norm2_shift: float32 [768], P('row'), may hold values from -1.75 to 1.75
Outputs:
- output: bfloat16 [8192, 768], P(('dp', 'col', 'row'))
- grad_tokens: float32 [8192, 768], P(('dp', 'col', 'row'))
- grad_query_weight: float32 [768, 768], P(('row', 'col'))
- grad_key_weight: float32 [768, 768], P(('row', 'col'))
- grad_value_weight: float32 [768, 768], P(('row', 'col'))
- grad_query_bias: float32 [768], P('col')
- grad_value_bias: float32 [768], P('col')
- grad_out_weight: float32 [768, 768], P(('col', 'row'))
- grad_out_bias: float32 [768], P('row')
- grad_norm1_gain: float32 [768], P('row')
- grad_norm1_shift: float32 [768], P('row')
- grad_up_weight: float32 [768, 3072], P('row', 'col')
- grad_up_bias: float32 [3072], P('col')
- grad_down_weight: float32 [3072, 768], P(('col', 'row'))
- grad_down_bias: float32 [768], P('row')
- grad_norm2_gain: float32 [768], P('row')
- grad_norm2_shift: float32 [768], P('row')
The draws below stay inside these ranges and needn't reach their ends.
Inputs may be any that keep to these rules, and one draw needn't show every extreme that they name: `lengths`: one sequence is exactly 4096 long.
All inputs are finite; a program needn't handle non-finite values.
Results may differ from the reference program's by a relative error of at most 0.024.
Values may be sent and summed in bfloat16 or wider, within the bound.
No kernel may reach another device: no remote copies, remote signals or barrier semaphores. Data moves between devices by JAX's collectives and lax.ppermute only.
A program may use at most 256 MiB of HBM per device.

```python
import math
import jax
import jax.numpy as jnp
from jax import lax

D = 768
HEADS = 12
HD = 64
FF = 3072
SEQ = 4096
SEQS = 2
TOKENS = 8192


def draw_lengths(key, part):
    drawn_lengths = jax.random.randint(key, (SEQS,), SEQ // 4, SEQ + 1)
    longest_at = jax.random.randint(jax.random.fold_in(key, 7), (), 0, SEQS)
    placed = jnp.where(jnp.arange(SEQS) == longest_at, SEQ, drawn_lengths)
    return placed.astype(jnp.int32)


def level_of(own_key, shape, cuts, smallest, top_value):
    loudness = 1.0
    for position, blocks in cuts:
        steps = jax.random.uniform(jax.random.fold_in(jax.random.fold_in(own_key, 6), position), (blocks,), jnp.float32, smallest / len(cuts), top_value / len(cuts))
        loudness = loudness * jnp.repeat(jnp.exp(steps), shape[position] // blocks).reshape((-1,) + (1,) * (len(shape) - 1 - position))
    return loudness


def noise(stream_key, shape, spread, limit, split=(), kind=jnp.bfloat16):
    loudness = level_of(stream_key, shape, split, -0.22, 0.18) if split else 1.0
    entries = jax.random.normal(stream_key, shape, jnp.float32) * spread * loudness
    return jnp.minimum(jnp.maximum(entries, -limit), limit).astype(kind)


def setup_inputs(seed: int = 0) -> dict:
    key_of = jax.random.split(jax.random.key(seed), 19)
    tokens = noise(key_of[0], (TOKENS, D), 1.0, 6.0, ((0, 32),))
    cotangent = noise(key_of[1], (TOKENS, D), 1.0, 6.0, ((0, 32),))
    lengths = draw_lengths(jax.random.fold_in(key_of[18], 71), 0)
    query_weight = noise(key_of[3], (D, D), D ** -0.5, 0.21875, ((0, 16),), jnp.float32)
    key_weight = noise(key_of[4], (D, D), D ** -0.5, 0.21875, ((0, 16),), jnp.float32)
    value_weight = noise(key_of[5], (D, D), D ** -0.5, 0.21875, ((0, 16),), jnp.float32)
    query_bias = noise(key_of[6], (D,), 0.5, 3.0, ((0, 4),), jnp.float32)
    value_bias = noise(key_of[7], (D,), 0.03, 0.1875, ((0, 4),), jnp.float32)
    out_weight = noise(key_of[8], (D, D), (max(1, D // 512)) ** -0.5, 6.0, ((0, 16),), jnp.float32)
    out_bias = noise(key_of[9], (D,), 0.3, 1.75, ((0, 4),), jnp.float32)
    norm1_gain = jnp.clip(1.0 + 0.1 * jax.random.normal(key_of[10], (D,), jnp.float32), 0.5, 1.5)
    norm1_shift = noise(key_of[11], (D,), 0.3, 1.75, ((0, 4),), jnp.float32)
    up_weight = noise(key_of[12], (D, FF), D ** -0.5, 0.21875, ((0, 4), (1, 4)), jnp.float32)
    up_bias = noise(key_of[13], (FF,), 0.5, 3.0, ((0, 4),), jnp.float32)
    down_weight = noise(key_of[14], (FF, D), FF ** -0.5, 0.109375, ((0, 16),), jnp.float32)
    down_bias = noise(key_of[15], (D,), 0.3, 1.75, ((0, 4),), jnp.float32)
    norm2_gain = jnp.clip(1.0 + 0.1 * jax.random.normal(key_of[16], (D,), jnp.float32), 0.5, 1.5)
    norm2_shift = noise(key_of[17], (D,), 0.3, 1.75, ((0, 4),), jnp.float32)
    return {"tokens": tokens, "cotangent": cotangent, "lengths": lengths, "query_weight": query_weight, "key_weight": key_weight, "value_weight": value_weight, "query_bias": query_bias, "value_bias": value_bias, "out_weight": out_weight, "out_bias": out_bias, "norm1_gain": norm1_gain, "norm1_shift": norm1_shift, "up_weight": up_weight, "up_bias": up_bias, "down_weight": down_weight, "down_bias": down_bias, "norm2_gain": norm2_gain, "norm2_shift": norm2_shift}


@jax.custom_vjp
def low(v):
    return lax.optimization_barrier(v.astype(jnp.bfloat16)).astype(jnp.float32)

@jax.custom_vjp
def low_back(v):
    return v

def low_keep(v):
    return (low(v), None)

def low_pass(kept, grad):
    return (grad,)

def back_keep(v):
    return (v, None)

def back_low(kept, grad):
    return (low(grad),)
low.defvjp(low_keep, low_pass)
low_back.defvjp(back_keep, back_low)
highest = lax.Precision.HIGHEST
eps_norm = 1e-05

def matmul(left_mat, right_mat):
    return jnp.dot(left_mat, right_mat, precision=highest, preferred_element_type=jnp.float32)

def layer_norm(resid, norm_gain, norm_shift):
    row_mean = lax.optimization_barrier(jnp.mean(resid, axis=-1, keepdims=True))
    centered = resid - row_mean
    row_var = lax.optimization_barrier(jnp.mean(centered * centered, axis=-1, keepdims=True))
    return centered * lax.rsqrt(row_var + eps_norm) * norm_gain + norm_shift

def attend(queries, key_rows, values, key_ok):
    scores = low_back(matmul(queries, key_rows.T) * (1.0 / math.sqrt(HD)))
    scores = jnp.where(key_ok[None, :], scores, -1e+30)
    attn_weights = jax.nn.softmax(scores, axis=-1)
    return matmul(low(attn_weights), values)

def split_heads(matrix):
    return matrix.reshape(SEQ, HEADS, HD).transpose(1, 0, 2)

def forward(inputs, params, valid_rows, key_ok):
    query_weight, key_weight, value_weight, query_bias, value_bias, out_weight, out_bias, norm1_gain, norm1_shift, up_weight, up_bias, down_weight, down_bias, norm2_gain, norm2_shift = params
    queries = low_back(low(matmul(inputs, low(query_weight)) + query_bias))
    key_rows = low_back(low(matmul(inputs, low(key_weight))))
    values = low_back(low(matmul(inputs, low(value_weight)) + value_bias))

    def one_head(triple):
        return attend(triple[0], triple[1], triple[2], key_ok)
    per_head = lax.map(jax.checkpoint(one_head), (split_heads(queries), split_heads(key_rows), split_heads(values)))
    mixed = low_back(low(per_head.transpose(1, 0, 2).reshape(SEQ, D)))
    attended = low_back(matmul(mixed, low(out_weight)) + out_bias)
    hidden = layer_norm(inputs + attended, norm1_gain, norm1_shift)
    preact = low_back(matmul(low(hidden), low(up_weight)) + up_bias)
    active = low(jax.nn.gelu(preact, approximate=False))
    branch = low_back(matmul(active, low(down_weight)) + down_bias)
    return layer_norm(hidden + branch, norm2_gain, norm2_shift) * valid_rows[:, None]

def add_pair(left_sum, right_sum):
    return left_sum + right_sum

def reference(tokens, cotangent, lengths, query_weight, key_weight, value_weight, query_bias, value_bias, out_weight, out_bias, norm1_gain, norm1_shift, up_weight, up_bias, down_weight, down_bias, norm2_gain, norm2_shift):
    params = (query_weight, key_weight, value_weight, query_bias, value_bias, out_weight, out_bias, norm1_gain, norm1_shift, up_weight, up_bias, down_weight, down_bias, norm2_gain, norm2_shift)
    positions = jnp.arange(SEQ, dtype=jnp.int32)

    def per_sequence(running, sequence):
        seq_tokens, seq_cot, seq_length = sequence
        key_ok = positions < seq_length.astype(jnp.int32)
        valid_rows = key_ok.astype(jnp.float32)

        def run_layer(inputs, weights):
            return forward(inputs, weights, valid_rows, key_ok)
        result, pullback = jax.vjp(run_layer, seq_tokens.astype(jnp.float32), params)
        grad_inputs, grad_params = pullback(seq_cot.astype(jnp.float32))
        running = jax.tree.map(add_pair, running, grad_params)
        return (running, (result.astype(jnp.bfloat16), grad_inputs))
    initial = jax.tree.map(jnp.zeros_like, params)
    totals, (outputs, grads_in) = lax.scan(per_sequence, initial, (tokens.reshape(SEQS, SEQ, D), cotangent.reshape(SEQS, SEQ, D), lengths))
    g_query_weight, g_key_weight, g_value_weight, g_query_bias, g_value_bias, g_out_weight, g_out_bias, g_norm1_gain, g_norm1_shift, g_up_weight, g_up_bias, g_down_weight, g_down_bias, g_norm2_gain, g_norm2_shift = totals
    return (outputs.reshape(TOKENS, D), grads_in.reshape(TOKENS, D), g_query_weight, g_key_weight, g_value_weight, g_query_bias, g_value_bias, g_out_weight, g_out_bias, g_norm1_gain, g_norm1_shift, g_up_weight, g_up_bias, g_down_weight, g_down_bias, g_norm2_gain, g_norm2_shift)
```

```python
import functools
import math

import jax
import jax.numpy as jnp
from jax import lax
from jax.experimental import pallas as pl
from jax.experimental.pallas import tpu as pltpu
from jax.sharding import PartitionSpec as P

HD = 64
LANES = 256
EPS = 1e-05
BF = jnp.bfloat16
F32 = jnp.float32
VMEM_BYTES = 60 * 1024 * 1024


def nn(a, b):
    return jnp.dot(a, b, preferred_element_type=F32)


def tn(a, b):
    return lax.dot_general(a, b, (((0,), (0,)), ((), ())), preferred_element_type=F32)


def nt(a, b):
    return lax.dot_general(a, b, (((1,), (1,)), ((), ())), preferred_element_type=F32)


CORE = [(0, 1), (1, 0), (2, 3), (3, 2)]
CROSS = [(0, 2), (2, 0), (1, 3), (3, 1)]


def core_swap(x):
    return lax.ppermute(x, "row", CORE)


def cross_swap(x):
    return lax.ppermute(x, "row", CROSS)


def shift_col(x, step):
    n = lax.axis_size("col")
    return lax.ppermute(x, "col", [(i, (i + step) % n) for i in range(n)])


def gather_row_rel(x):
    near = core_swap(x)
    far = cross_swap(x)
    return [x, near, far, core_swap(far)]


def natural_row(blocks):
    r = lax.axis_index("row")
    low = (r & 1) == 0
    b0, b1, b2, b3 = blocks
    left = jnp.where(low, jnp.concatenate([b0, b1]), jnp.concatenate([b1, b0]))
    right = jnp.where(low, jnp.concatenate([b2, b3]), jnp.concatenate([b3, b2]))
    return jnp.where(r < 2, jnp.concatenate([left, right]), jnp.concatenate([right, left]))


def reduce_row_rel(own, near, far, diag):
    got = core_swap(jnp.stack([near, diag]).astype(BF))
    own = own + got[0].astype(F32)
    far = far + got[1].astype(F32)
    return own + cross_swap(far.astype(BF)).astype(F32)


def gather_col(x):
    n = lax.axis_size("col")
    z = lax.axis_index("col")
    out = jnp.zeros((n,) + x.shape, x.dtype)
    block = x
    out = lax.dynamic_update_index_in_dim(out, block, z, 0)
    for step in range(1, n):
        block = shift_col(block, 1)
        out = lax.dynamic_update_index_in_dim(out, block, (z + n - step) % n, 0)
    return out


def reduce_col(parts):
    n = lax.axis_size("col")
    z = lax.axis_index("col")

    def part(k):
        return lax.dynamic_index_in_dim(parts, (z + n - k) % n, 0, keepdims=False)

    total = part(1)
    for step in range(2, n + 1):
        total = part(step) + shift_col(total.astype(BF), 1).astype(F32)
    return total


def sum_dp(x):
    n = lax.axis_size("dp")
    if n == 2:
        return x + lax.ppermute(x, "dp", [(0, 1), (1, 0)])
    return lax.psum(x, "dp")


def split3(x):
    hi = lax.reduce_precision(x, 8, 7)
    mid = lax.reduce_precision(x - hi, 8, 7)
    low = x - hi - mid
    return hi.astype(BF), mid.astype(BF), low.astype(BF)


def head_lanes(shape, head, width):
    lane = lax.broadcasted_iota(jnp.int32, shape, 1)
    mine = (lane >= head * HD) & (lane < (head + 1) * HD)
    return mine | (lane == width) | ((lane >= width + 1 + 3 * head) & (lane < width + 4 + 3 * head))


def attn_fwd_kernel(q_ref, k_ref, v_ref, o_ref, lse_ref, *, heads, chunk):
    width = heads * HD
    q = q_ref[...]
    out = jnp.zeros(o_ref.shape, F32)
    lse = jnp.zeros(lse_ref.shape, F32)
    lane = lax.broadcasted_iota(jnp.int32, lse_ref.shape, 1)
    for head in range(heads):
        mine = head_lanes(q.shape, head, width)
        qh = jnp.where(mine, q, jnp.zeros_like(q))
        acc = None
        for j in range(k_ref.shape[0] // chunk):
            rows = slice(j * chunk, (j + 1) * chunk)
            s = nt(qh, k_ref[rows, :])
            top = jnp.max(s, axis=1, keepdims=True)
            if acc is None:
                peak = top
                acc = nn(jnp.exp(s - peak).astype(BF), v_ref[rows, :])
            else:
                new = jnp.maximum(peak, top)
                acc = acc * jnp.exp(peak - new) + nn(jnp.exp(s - new).astype(BF), v_ref[rows, :])
                peak = new
        total = acc[:, width : width + 1]
        out = jnp.where(mine, acc / total, out)
        lse = jnp.where(lane == head, peak + jnp.log(total), lse)
    o_ref[...] = out.astype(o_ref.dtype)
    lse_ref[...] = lse


def attn_fwd(q, k, v, heads, block=256, chunk=2048):
    rows = q.shape[0]
    keys = k.shape[0]
    whole = pl.BlockSpec((keys, LANES), lambda i: (0, 0))
    return pl.pallas_call(
        functools.partial(attn_fwd_kernel, heads=heads, chunk=min(chunk, keys)),
        grid=(rows // block,),
        in_specs=[pl.BlockSpec((block, LANES), lambda i: (i, 0)), whole, whole],
        out_specs=[
            pl.BlockSpec((block, LANES), lambda i: (i, 0)),
            pl.BlockSpec((block, 128), lambda i: (i, 0)),
        ],
        out_shape=[
            jax.ShapeDtypeStruct((rows, LANES), BF),
            jax.ShapeDtypeStruct((rows, 128), F32),
        ],
        compiler_params=pltpu.CompilerParams(vmem_limit_bytes=VMEM_BYTES),
        cost_estimate=pl.CostEstimate(
            flops=4 * rows * keys * LANES * heads,
            bytes_accessed=4 * (rows + keys) * LANES,
            transcendentals=heads * rows * keys,
        ),
        name="attn_fwd",
    )(q, k, v)


def attn_bwd_kernel(q_ref, do_ref, k_ref, v_ref, dq_ref, dk_ref, dv_ref, dq_acc, *, heads, block):
    width = heads * HD
    step = pl.program_id(0)
    k = k_ref[...]
    v = v_ref[...]

    @pl.when(step == 0)
    def _():
        dq_acc[...] = jnp.zeros_like(dq_acc)

    dk = jnp.zeros(dk_ref.shape, F32)
    dv = jnp.zeros(dv_ref.shape, F32)
    for i in range(q_ref.shape[0] // block):
        rows = slice(i * block, (i + 1) * block)
        q_all = q_ref[rows, :]
        do_all = do_ref[rows, :]
        dq = jnp.zeros((block, LANES), F32)
        for head in range(heads):
            mine = head_lanes((block, LANES), head, width)
            q = jnp.where(mine, q_all, jnp.zeros_like(q_all))
            do = jnp.where(mine, do_all, jnp.zeros_like(do_all))
            p = jnp.exp(nt(k, q))
            ds = (p * nt(v, do)).astype(BF)
            dv = dv + nn(p.astype(BF), do)
            dk = dk + nn(ds, q)
            dq = jnp.where(mine, tn(ds, k), dq)
        dq_acc[rows, :] += dq
    dk_ref[...] = dk.astype(dk_ref.dtype)
    dv_ref[...] = dv.astype(dv_ref.dtype)

    @pl.when(step == pl.num_programs(0) - 1)
    def _():
        dq_ref[...] = dq_acc[...].astype(dq_ref.dtype)


def attn_bwd(q, do, k, v, heads, block=256, chunk=1024):
    rows = q.shape[0]
    keys = k.shape[0]
    whole = pl.BlockSpec((rows, LANES), lambda i: (0, 0))
    part = pl.BlockSpec((chunk, LANES), lambda i: (i, 0))
    return pl.pallas_call(
        functools.partial(attn_bwd_kernel, heads=heads, block=block),
        grid=(keys // chunk,),
        in_specs=[whole, whole, part, part],
        out_specs=[whole, part, part],
        out_shape=[
            jax.ShapeDtypeStruct((rows, LANES), F32),
            jax.ShapeDtypeStruct((keys, LANES), F32),
            jax.ShapeDtypeStruct((keys, LANES), F32),
        ],
        scratch_shapes=[pltpu.VMEM((rows, LANES), F32)],
        compiler_params=pltpu.CompilerParams(vmem_limit_bytes=VMEM_BYTES),
        cost_estimate=pl.CostEstimate(
            flops=10 * rows * keys * LANES * heads,
            bytes_accessed=8 * (rows + keys) * LANES,
            transcendentals=heads * rows * keys,
        ),
        name="attn_bwd",
    )(q, do, k, v)


def gelu_exact(x):
    return jax.nn.gelu(x, approximate=False)


def norm_forward(resid, gain, shift):
    mean = jnp.mean(resid, axis=1, keepdims=True)
    centered = resid - mean
    inv = lax.rsqrt(jnp.mean(centered * centered, axis=1, keepdims=True) + EPS)
    normal = centered * inv
    return normal * gain + shift, normal, inv


def norm_backward(grad_out, normal, inv, gain):
    scaled = grad_out * gain
    mean_e = jnp.mean(scaled, axis=1, keepdims=True)
    mean_en = jnp.mean(scaled * normal, axis=1, keepdims=True)
    grad_in = inv * (scaled - mean_e - normal * mean_en)
    return grad_in, jnp.sum(grad_out * normal, axis=0), jnp.sum(grad_out, axis=0)


def per_device(
    tokens,
    cotangent,
    lengths,
    query_weight,
    key_weight,
    value_weight,
    query_bias,
    value_bias,
    out_weight,
    out_bias,
    norm1_gain,
    norm1_shift,
    up_weight,
    up_bias,
    down_weight,
    down_bias,
    norm2_gain,
    norm2_shift,
):
    rows_n = lax.axis_size("row")
    cols_n = lax.axis_size("col")
    r = lax.axis_index("row")
    z = lax.axis_index("col")
    local, width = tokens.shape
    block_len = local * cols_n
    length = lengths[0]
    hw = width // cols_n
    heads = hw // HD
    feat = width // rows_n
    scale = 1.0 / math.sqrt(HD)

    x_col = gather_col(tokens).reshape(block_len, width)

    qkv = jnp.stack([query_weight, key_weight, value_weight], axis=1).astype(BF)
    sub = qkv.shape[0]
    qkv = qkv.reshape(sub, 3, cols_n, hw).transpose(2, 0, 1, 3).reshape(cols_n, sub, 3 * hw)
    qkv = lax.all_to_all(qkv, "col", split_axis=0, concat_axis=0, tiled=True)
    qkv = qkv.reshape(cols_n * sub, 3 * hw)
    vecs = jnp.stack([out_bias, norm1_gain, norm1_shift, down_bias, norm2_gain, norm2_shift])
    vec_parts = jnp.stack(split3(vecs)).reshape(-1)
    vec_rows = 16
    vec_parts = jnp.pad(vec_parts, (0, vec_rows * 3 * hw - vec_parts.shape[0]))
    message = jnp.concatenate([qkv, vec_parts.reshape(vec_rows, 3 * hw)])
    got = natural_row([b[None] for b in gather_row_rel(message)])
    w_qkv = got[:, : cols_n * sub].reshape(width, 3 * hw)
    vec_all = got[:, cols_n * sub :].reshape(rows_n, -1)[:, : 3 * 6 * feat]
    vec_all = jnp.sum(vec_all.reshape(rows_n, 3, 6, feat).astype(F32), axis=1)
    vec_all = vec_all.transpose(1, 0, 2).reshape(6, width)
    out_bias_all, gain1, shift1, down_bias_all, gain2, shift2 = [vec_all[i] for i in range(6)]

    up_t = up_weight.astype(BF).T
    units = up_t.shape[0] // rows_n
    up_t = up_t.reshape(rows_n, units, feat)
    up_t = lax.all_to_all(up_t, "row", split_axis=0, concat_axis=0, tiled=True)
    up_t = up_t.transpose(1, 0, 2).reshape(units, width)
    bias_mine = lax.dynamic_slice_in_dim(up_bias, r * units, units, 0)
    bias_rows = jnp.pad(jnp.stack(split3(bias_mine)), ((0, 13), (0, width - units)))
    sub_out = out_weight.shape[0]
    pack = jnp.concatenate([up_t, down_weight.astype(BF), out_weight.astype(BF), bias_rows])
    pack = lax.all_gather(pack, "col", axis=0, tiled=False)
    up_r = pack[:, :units].reshape(cols_n * units, width)
    down_r = pack[:, units : 2 * units].reshape(cols_n * units, width)
    out_r = pack[:, 2 * units : 2 * units + sub_out]
    up_bias_r = jnp.sum(pack[:, 2 * units + sub_out :][:, :3, :units].astype(F32), axis=1)
    up_bias_r = up_bias_r.reshape(1, cols_n * units)

    proj = nn(x_col, w_qkv)
    proj_bias = jnp.concatenate([query_bias, jnp.zeros_like(query_bias), value_bias])
    proj = (proj + proj_bias).astype(BF)
    queries = proj[:, :hw]
    kv = jnp.concatenate(gather_row_rel(proj[:, hw:]))
    keys_n = kv.shape[0]
    place = jnp.arange(keys_n, dtype=jnp.int32)
    owner = r ^ (place // block_len)
    inner = place % block_len
    position = (inner // local) * (local * rows_n) + owner * local + inner % local
    key_mask = jnp.where(position < length, 0.0, -1e30).astype(BF)[:, None]
    pad_n = LANES - hw - 1
    key_rows = jnp.concatenate([kv[:, :hw], key_mask, jnp.ones((keys_n, pad_n), BF)], axis=1)
    value_rows = jnp.concatenate([kv[:, hw:], jnp.ones((keys_n, pad_n + 1), BF)], axis=1)
    q_scaled = queries * jnp.asarray(scale, BF)
    ones_q = jnp.ones((block_len, 1), BF)
    q_rows = jnp.concatenate([q_scaled, ones_q, jnp.zeros((block_len, pad_n), BF)], axis=1)
    mixed_wide, lse = attn_fwd(q_rows, key_rows, value_rows, heads)
    mixed_part = mixed_wide[:, :hw]
    mixed = lax.all_to_all(mixed_part, "col", split_axis=0, concat_axis=1, tiled=True)

    out_full = natural_row([b[None] for b in gather_row_rel(out_r)])
    out_full = out_full.transpose(1, 0, 2, 3).reshape(width, width)
    attended = nn(mixed, out_full) + out_bias_all
    hidden, normal1, inv1 = norm_forward(tokens.astype(F32) + attended, gain1, shift1)

    hidden_all = jnp.concatenate(gather_row_rel(hidden.astype(BF)))
    preact = nt(hidden_all, up_r) + up_bias_r
    active = gelu_exact(preact).astype(BF)
    part = nn(active, down_r).reshape(rows_n, local, width)
    branch = reduce_row_rel(part[0], part[1], part[2], part[3]) + down_bias_all
    normed, normal2, inv2 = norm_forward(hidden + branch, gain2, shift2)
    my_pos = z * (local * rows_n) + r * local + jnp.arange(local, dtype=jnp.int32)
    valid = (my_pos < length).astype(F32)[:, None]
    output = (normed * valid).astype(BF)

    grad_y = cotangent.astype(F32) * valid
    grad_resid2, g_gain2, g_shift2 = norm_backward(grad_y, normal2, inv2, gain2)
    grad_branch = grad_resid2.astype(BF)
    g_down_bias = jnp.sum(grad_branch.astype(F32), axis=0)
    grad_branch_all = jnp.concatenate(gather_row_rel(grad_branch))
    grad_active = nt(grad_branch_all, down_r)
    grad_preact = jax.vjp(gelu_exact, preact)[1](grad_active)[0].astype(BF)
    part = nn(grad_preact, up_r).reshape(rows_n, local, width)
    grad_hidden = reduce_row_rel(part[0], part[1], part[2], part[3]) + grad_resid2
    g_down = tn(active, grad_branch_all).astype(BF).reshape(cols_n, units, width)
    g_up = tn(grad_preact, hidden_all).astype(BF).reshape(cols_n, units, width)
    g_up_bias = jnp.sum(grad_preact.astype(F32), axis=0)
    grad_resid1, g_gain1, g_shift1 = norm_backward(grad_hidden, normal1, inv1, gain1)
    grad_attended = grad_resid1.astype(BF)
    g_out_bias = jnp.sum(grad_attended.astype(F32), axis=0)
    grad_mixed_local = nt(grad_attended, out_full).astype(BF)
    grad_mixed = lax.all_to_all(grad_mixed_local, "col", split_axis=1, concat_axis=0, tiled=True)

    g_out = tn(mixed, grad_attended).reshape(cols_n, rows_n, sub_out, width)
    g_out = [lax.dynamic_index_in_dim(g_out, r ^ k, 1, keepdims=False) for k in range(4)]
    g_out = reduce_row_rel(*g_out).astype(BF)
    g_pack = jnp.concatenate([g_up, g_down, g_out], axis=1)
    g_pack = lax.psum_scatter(g_pack, "col", scatter_dimension=0, tiled=True)[0]
    g_pack = sum_dp(g_pack)
    g_up = g_pack[:units].reshape(units, rows_n, feat)
    g_up = lax.all_to_all(g_up, "row", split_axis=1, concat_axis=0, tiled=True)
    g_up_weight = g_up.reshape(rows_n * units, feat).T.astype(F32)
    g_down_weight = g_pack[units : 2 * units].astype(F32)
    g_out_weight = g_pack[2 * units :].astype(F32)

    lse_parts = jnp.stack(split3(-lse[:, :heads]), axis=2).reshape(block_len, 3 * heads)
    tail = jnp.zeros((block_len, pad_n - 3 * heads), BF)
    qb_rows = jnp.concatenate([q_scaled, ones_q, lse_parts, tail], axis=1)
    delta = mixed_part.astype(F32) * grad_mixed.astype(F32)
    delta = -jnp.sum(delta.reshape(block_len, heads, HD), axis=2)
    delta_parts = jnp.stack(split3(delta), axis=2).reshape(block_len, 3 * heads)
    do_rows = jnp.concatenate(
        [grad_mixed, jnp.zeros((block_len, 1), BF), delta_parts, tail], axis=1
    )
    dq, dk, dv = attn_bwd(qb_rows, do_rows, key_rows, value_rows, heads)
    grad_q = (dq[:, :hw] * scale).astype(BF)
    grad_kv = jnp.concatenate([dk[:, :hw], dv[:, :hw]], axis=1)
    grad_kv = grad_kv.reshape(rows_n, block_len, 2 * hw)
    grad_kv = reduce_row_rel(*[grad_kv[i] for i in range(4)]).astype(BF)
    grad_qkv = jnp.concatenate([grad_q, grad_kv], axis=1)

    back = nt(grad_qkv, w_qkv).reshape(cols_n, local, width)
    grad_tokens = grad_resid1 + reduce_col(back)

    g_qkv = tn(x_col, grad_qkv).reshape(rows_n, feat, 3 * hw)
    g_bias = jnp.sum(grad_qkv.astype(F32), axis=0)
    g_qkv = [lax.dynamic_index_in_dim(g_qkv, r ^ k, 0, keepdims=False) for k in range(4)]
    g_qkv = sum_dp(reduce_row_rel(*g_qkv).astype(BF))
    g_qkv = lax.all_to_all(
        g_qkv.reshape(cols_n, sub, 3 * hw), "col", split_axis=0, concat_axis=0, tiled=True
    )
    g_qkv = g_qkv.reshape(cols_n, sub, 3, hw).transpose(2, 1, 0, 3).reshape(3, sub, width)
    g_qkv = g_qkv.astype(F32)

    up_place = jnp.zeros((cols_n, rows_n, units), F32)
    up_place = lax.dynamic_update_slice(
        up_place, g_up_bias.reshape(cols_n, 1, units), (0, r, 0)
    ).reshape(-1, width)
    bias_place = jnp.zeros((2, width), F32)
    bias_place = lax.dynamic_update_slice(
        bias_place, jnp.stack([g_bias[:hw], g_bias[2 * hw :]]), (0, z * hw)
    )
    sums = jnp.concatenate(
        [jnp.stack([g_gain1, g_shift1, g_gain2, g_shift2, g_down_bias, g_out_bias]), up_place, bias_place]
    )
    sums = sums + core_swap(sums)
    sums = sums + cross_swap(sums)
    sums = sum_dp(sums)
    sums = sums + lax.ppermute(sums, "col", [(i, i ^ 1) for i in range(cols_n)])
    sums = sums + lax.ppermute(sums, "col", [(i, i ^ 2) for i in range(cols_n)])
    mine = lax.dynamic_slice_in_dim(sums[:6], r * feat, feat, 1)
    g_up_bias = lax.dynamic_index_in_dim(
        sums[6:-2].reshape(cols_n, rows_n * units), z, 0, keepdims=False
    )
    g_bias = lax.dynamic_slice_in_dim(sums[-2:], z * hw, hw, 1)
    return (
        output,
        grad_tokens,
        g_qkv[0],
        g_qkv[1],
        g_qkv[2],
        g_bias[0],
        g_bias[1],
        g_out_weight,
        mine[5],
        mine[0],
        mine[1],
        g_up_weight,
        g_up_bias,
        g_down_weight,
        mine[4],
        mine[2],
        mine[3],
    )


def solution(mesh):
    token_spec = P(("dp", "col", "row"), None)
    placed = (
        token_spec,
        token_spec,
        P("dp"),
        P(("row", "col"), None),
        P(("row", "col"), None),
        P(("row", "col"), None),
        P("col"),
        P("col"),
        P(("col", "row"), None),
        P("row"),
        P("row"),
        P("row"),
        P("row", "col"),
        P("col"),
        P(("col", "row"), None),
        P("row"),
        P("row"),
        P("row"),
    )
    return jax.shard_map(
        per_device,
        mesh=mesh,
        in_specs=placed,
        out_specs=(token_spec, token_spec) + placed[3:],
        check_vma=False,
    )
```

```python
import functools
import math

import jax
import jax.numpy as jnp
from jax import lax
from jax.experimental import pallas as pl
from jax.experimental.pallas import tpu as pltpu
from jax.sharding import PartitionSpec as P

HD = 64
LANES = 256
EPS = 1e-05
BF = jnp.bfloat16
F32 = jnp.float32
VMEM_BYTES = 60 * 1024 * 1024


def nn(a, b):
    return jnp.dot(a, b, preferred_element_type=F32)


def tn(a, b):
    return lax.dot_general(a, b, (((0,), (0,)), ((), ())), preferred_element_type=F32)


def nt(a, b):
    return lax.dot_general(a, b, (((1,), (1,)), ((), ())), preferred_element_type=F32)


def head_lanes(shape, head, width):
    lane = lax.broadcasted_iota(jnp.int32, shape, 1)
    mine = (lane >= head * HD) & (lane < (head + 1) * HD)
    return mine | (lane == width) | ((lane >= width + 1 + 3 * head) & (lane < width + 4 + 3 * head))


def three_parts(x):
    hi = x.astype(BF).astype(F32)
    mid = (x - hi).astype(BF).astype(F32)
    return hi, mid, x - hi - mid


def widen_keys(kv, owner, length, keys_out, values_out, at, width, shift, rows_n):
    n = kv.shape[0]
    keys_out[at : at + n, :width] = kv[:, :width]
    values_out[at : at + n, :width] = kv[:, width:]
    shape = (n, LANES - width)
    t = lax.broadcasted_iota(jnp.int32, shape, 0)
    lane = lax.broadcasted_iota(jnp.int32, shape, 1)
    low = t & ((1 << shift) - 1)
    position = (((t >> shift) * rows_n + owner) << shift) + low
    mask = jnp.where((lane == 0) & (position >= length), -1e30, jnp.where(lane == 0, 0.0, 1.0))
    keys_out[at : at + n, width:] = mask.astype(BF)
    values_out[at : at + n, width:] = jnp.ones(shape, BF)


def attn_fwd_kernel(*refs, heads, first, pair, shift, rows_n):
    if first:
        meta, q_ref, kv0, kv1, acc_out, stat_out, k_out, v_out = refs
    else:
        meta, q_ref, kv0, kv1, acc_in, stat_in, o_ref, qb_ref, k_out, v_out = refs
    width = heads * HD
    half = kv0.shape[0]

    @pl.when(pl.program_id(0) == 0)
    def _():
        widen_keys(kv0[...], meta[1] ^ pair[0], meta[0], k_out, v_out, 0, width, shift, rows_n)
        widen_keys(kv1[...], meta[1] ^ pair[1], meta[0], k_out, v_out, half, width, shift, rows_n)

    q = q_ref[...]
    rows = q.shape[0]
    lane = lax.broadcasted_iota(jnp.int32, (rows, LANES), 1)
    slot = lax.broadcasted_iota(jnp.int32, (rows, 128), 1)
    wide = jnp.zeros((rows, LANES), F32)
    stat = jnp.zeros((rows, 128), F32)
    extra = q.astype(F32)
    if not first:
        old = stat_in[...]
        old_acc = jnp.concatenate([acc_in[...], jnp.zeros((rows, LANES - acc_in.shape[1]), F32)], axis=1)
    for head in range(heads):
        mine = head_lanes(q.shape, head, width)
        qh = jnp.where(mine, q, jnp.zeros_like(q))
        s = nt(qh, k_out[...])
        peak = jnp.max(s, axis=1, keepdims=True)
        if first:
            p = jnp.exp(s - peak).astype(BF)
            acc = nn(p, v_out[...])
            wide = jnp.where(mine, acc, wide)
            total = acc[:, width : width + 1]
            stat = jnp.where(slot == head, peak, stat)
            stat = jnp.where(slot == head + 8, total, stat)
        else:
            old_peak = old[:, head : head + 1]
            new = jnp.maximum(old_peak, peak)
            keep = jnp.exp(old_peak - new)
            p = jnp.exp(s - new).astype(BF)
            acc = nn(p, v_out[...])
            total = old[:, head + 8 : head + 9] * keep + acc[:, width : width + 1]
            wide = jnp.where(mine, (old_acc * keep + acc) / total, wide)
            hi, mid, low = three_parts(-(new + jnp.log(total)))
            at = width + 1 + 3 * head
            extra = jnp.where(lane == at, hi, extra)
            extra = jnp.where(lane == at + 1, mid, extra)
            extra = jnp.where(lane == at + 2, low, extra)
    if first:
        acc_out[...] = wide[:, :width]
        stat_out[...] = stat
    else:
        o_ref[...] = wide[:, :width].astype(BF)
        qb_ref[...] = extra.astype(BF)


def attn_fwd(meta, q, kv_pair, pair, heads, local, rows_n, state=None, block=256):
    rows = q.shape[0]
    half, double = kv_pair[0].shape
    width = double // 2
    first = state is None

    def whole(shape):
        return pl.BlockSpec(shape, lambda i: (0,) * len(shape))

    def tile(lanes):
        return pl.BlockSpec((block, lanes), lambda i: (i, 0))

    in_specs = [pl.BlockSpec(memory_space=pltpu.SMEM), tile(LANES)] + [whole((half, double))] * 2
    args = [meta, q, *kv_pair]
    wide_keys = jax.ShapeDtypeStruct((2 * half, LANES), BF)
    if first:
        out_specs = [tile(width), tile(128)]
        out_shape = [jax.ShapeDtypeStruct((rows, width), F32), jax.ShapeDtypeStruct((rows, 128), F32)]
    else:
        in_specs += [tile(width), tile(128)]
        args += list(state)
        out_specs = [tile(width), tile(LANES)]
        out_shape = [jax.ShapeDtypeStruct((rows, width), BF), jax.ShapeDtypeStruct((rows, LANES), BF)]
    return pl.pallas_call(
        functools.partial(
            attn_fwd_kernel,
            heads=heads,
            first=first,
            pair=pair,
            shift=local.bit_length() - 1,
            rows_n=rows_n,
        ),
        grid=(rows // block,),
        in_specs=in_specs,
        out_specs=out_specs + [whole((2 * half, LANES))] * 2,
        out_shape=out_shape + [wide_keys, wide_keys],
        compiler_params=pltpu.CompilerParams(vmem_limit_bytes=VMEM_BYTES),
        cost_estimate=pl.CostEstimate(
            flops=8 * rows * half * LANES * heads,
            bytes_accessed=8 * (rows + half) * LANES,
            transcendentals=2 * heads * rows * half,
        ),
        name="attn_fwd_near" if first else "attn_fwd_far",
    )(*args)


def attn_bwd_kernel(*refs, heads, first, block, scale):
    if first:
        q_ref, g_ref, o_ref, k_ref, v_ref, keep_ref, send_ref, dq_out, do_ref, dq_acc = refs
    else:
        q_ref, do_ref, dq_in, k_ref, v_ref, keep_ref, send_ref, dq_out, dq_acc = refs
    width = heads * HD
    step = pl.program_id(0)
    rows = q_ref.shape[0]

    @pl.when(step == 0)
    def _():
        if first:
            dq_acc[...] = jnp.zeros_like(dq_acc)
            g = g_ref[...]
            do_ref[:, :width] = g
            prod = g.astype(F32) * o_ref[...].astype(F32)
            shape = (rows, LANES - width)
            lane = lax.broadcasted_iota(jnp.int32, shape, 1)
            column = lax.broadcasted_iota(jnp.int32, prod.shape, 1)
            tail = jnp.zeros(shape, F32)
            for head in range(heads):
                mine = (column >= head * HD) & (column < (head + 1) * HD)
                parts = three_parts(-jnp.sum(jnp.where(mine, prod, 0.0), axis=1, keepdims=True))
                for i in range(3):
                    tail = jnp.where(lane == 1 + 3 * head + i, parts[i], tail)
            do_ref[:, width:] = tail.astype(BF)
        else:
            dq_acc[:, :width] = dq_in[...]

    k = k_ref[...]
    v = v_ref[...]
    dk = jnp.zeros((k.shape[0], LANES), F32)
    dv = jnp.zeros((k.shape[0], LANES), F32)
    for i in range(rows // block):
        at = slice(i * block, (i + 1) * block)
        q_all = q_ref[at, :]
        do_all = do_ref[at, :]
        dq = jnp.zeros((block, LANES), F32)
        for head in range(heads):
            mine = head_lanes((block, LANES), head, width)
            q = jnp.where(mine, q_all, jnp.zeros_like(q_all))
            do = jnp.where(mine, do_all, jnp.zeros_like(do_all))
            p = jnp.exp(nt(k, q))
            ds = (p * nt(v, do)).astype(BF)
            dv = dv + nn(p.astype(BF), do)
            dk = dk + nn(ds, q)
            dq = jnp.where(mine, tn(ds, k), dq)
        dq_acc[at, :] += dq

    @pl.when(step == 0)
    def _():
        keep_ref[:, :width] = dk[:, :width]
        keep_ref[:, width:] = dv[:, :width]

    @pl.when(step == 1)
    def _():
        send_ref[:, :width] = dk[:, :width].astype(BF)
        send_ref[:, width:] = dv[:, :width].astype(BF)
        if first:
            dq_out[...] = dq_acc[:, :width]
        else:
            dq_out[...] = (dq_acc[:, :width] * scale).astype(BF)


def attn_bwd(q, grads, k, v, heads, scale, dq=None, block=256):
    rows = q.shape[0]
    half = k.shape[0] // 2
    width = heads * HD
    first = dq is None

    def whole(shape):
        return pl.BlockSpec(shape, lambda i: (0,) * len(shape))

    part = pl.BlockSpec((half, LANES), lambda i: (i, 0))
    args = [q, *grads] if first else [q, grads, dq]
    out_specs = [whole((half, 2 * width)), whole((half, 2 * width)), whole((rows, width))]
    out_shape = [
        jax.ShapeDtypeStruct((half, 2 * width), F32),
        jax.ShapeDtypeStruct((half, 2 * width), BF),
        jax.ShapeDtypeStruct((rows, width), F32 if first else BF),
    ]
    if first:
        out_specs.append(whole((rows, LANES)))
        out_shape.append(jax.ShapeDtypeStruct((rows, LANES), BF))
    return pl.pallas_call(
        functools.partial(attn_bwd_kernel, heads=heads, first=first, block=block, scale=scale),
        grid=(2,),
        in_specs=[whole(a.shape) for a in args] + [part, part],
        out_specs=out_specs,
        out_shape=out_shape,
        scratch_shapes=[pltpu.VMEM((rows, LANES), F32)],
        compiler_params=pltpu.CompilerParams(vmem_limit_bytes=VMEM_BYTES),
        cost_estimate=pl.CostEstimate(
            flops=20 * rows * half * LANES * heads,
            bytes_accessed=16 * (rows + half) * LANES,
            transcendentals=2 * heads * rows * half,
        ),
        name="attn_bwd_far" if first else "attn_bwd_near",
    )(*args, k, v)


def small_call(kernel, out_shape, flops, name):
    return pl.pallas_call(
        kernel,
        out_shape=out_shape,
        compiler_params=pltpu.CompilerParams(vmem_limit_bytes=VMEM_BYTES),
        cost_estimate=pl.CostEstimate(flops=flops, bytes_accessed=4 << 20, transcendentals=0),
        name=name,
    )


def row_mean(x):
    return jnp.mean(x, axis=1, keepdims=True)


def col_sum(x):
    return jnp.sum(x, axis=0, keepdims=True)


def norm_forward(resid, gain, shift):
    centered = resid - row_mean(resid)
    inv = lax.rsqrt(row_mean(centered * centered) + EPS)
    normal = centered * inv
    return normal * gain + shift, normal, inv


def norm_backward(grad_out, normal, inv, gain):
    scaled = grad_out * gain
    return inv * (scaled - row_mean(scaled) - normal * row_mean(scaled * normal))


def project_kernel(mixed_ref, w_ref, x_ref, vec_ref, hid_ref, low_ref, normal_ref, inv_ref):
    total = x_ref[...].astype(F32) + vec_ref[0:1, :]
    step = mixed_ref.shape[2]
    for j in range(mixed_ref.shape[0]):
        total = total + nn(mixed_ref[j], w_ref[j * step : (j + 1) * step, :])
    hidden, normal, inv = norm_forward(total, vec_ref[1:2, :], vec_ref[2:3, :])
    hid_ref[...] = hidden
    low_ref[...] = hidden.astype(BF)
    normal_ref[...] = normal
    inv_ref[...] = jnp.broadcast_to(inv, inv_ref.shape)


def project(mixed, w, x, vecs):
    rows, width = x.shape
    return small_call(
        project_kernel,
        [
            jax.ShapeDtypeStruct((rows, width), F32),
            jax.ShapeDtypeStruct((rows, width), BF),
            jax.ShapeDtypeStruct((rows, width), F32),
            jax.ShapeDtypeStruct((rows, 128), F32),
        ],
        2 * rows * width * width,
        "project_norm1",
    )(mixed, w, x, vecs)


def ffn_fwd_kernel(h0_ref, h1_ref, up_ref, bias_ref, down_ref, keep_ref, send_ref, act_ref, slope_ref):
    rows = h0_ref.shape[0]
    for i, (h_ref, out_ref) in enumerate(((h0_ref, keep_ref), (h1_ref, send_ref))):
        x = nt(h_ref[...], up_ref[...]) + bias_ref[...]
        cdf = 0.5 * (1.0 + lax.erf(x * math.sqrt(0.5)))
        act = (x * cdf).astype(BF)
        slope = cdf + x * (math.sqrt(0.5 / math.pi) * jnp.exp(-0.5 * x * x))
        act_ref[i * rows : (i + 1) * rows, :] = act
        slope_ref[i * rows : (i + 1) * rows, :] = slope.astype(BF)
        out_ref[...] = nn(act, down_ref[...]).astype(out_ref.dtype)


def ffn_fwd(h0, h1, up, bias, down):
    rows, width = h0.shape
    units = up.shape[0]
    return small_call(
        ffn_fwd_kernel,
        [
            jax.ShapeDtypeStruct((rows, width), F32),
            jax.ShapeDtypeStruct((rows, width), BF),
            jax.ShapeDtypeStruct((2 * rows, units), BF),
            jax.ShapeDtypeStruct((2 * rows, units), BF),
        ],
        8 * rows * width * units,
        "ffn_fwd",
    )(h0, h1, up, bias, down)


def ffn_bwd_kernel(g0_ref, g1_ref, up_ref, down_ref, slope_ref, keep_ref, send_ref, pre_ref):
    rows = g0_ref.shape[0]
    for i, (g_ref, out_ref) in enumerate(((g0_ref, keep_ref), (g1_ref, send_ref))):
        at = slice(i * rows, (i + 1) * rows)
        pre = (nt(g_ref[...], down_ref[...]) * slope_ref[at, :].astype(F32)).astype(BF)
        pre_ref[at, :] = pre
        out_ref[...] = nn(pre, up_ref[...]).astype(out_ref.dtype)


def ffn_bwd(g0, g1, up, down, slope):
    rows, width = g0.shape
    units = up.shape[0]
    return small_call(
        ffn_bwd_kernel,
        [
            jax.ShapeDtypeStruct((rows, width), F32),
            jax.ShapeDtypeStruct((rows, width), BF),
            jax.ShapeDtypeStruct((2 * rows, units), BF),
        ],
        8 * rows * width * units,
        "ffn_bwd",
    )(g0, g1, up, down, slope)


def norm2_kernel(
    meta, hid_ref, keep_ref, near_ref, far_ref, cot_ref, vec_ref, out_ref, grad_ref, low_ref, sum_ref
):
    branch = keep_ref[...] + near_ref[...].astype(F32) + far_ref[...].astype(F32) + vec_ref[3:4, :]
    gain = vec_ref[4:5, :]
    normed, normal, inv = norm_forward(hid_ref[...] + branch, gain, vec_ref[5:6, :])
    row = lax.broadcasted_iota(jnp.int32, (out_ref.shape[0], 1), 0)
    valid = (meta[2] + row < meta[0]).astype(F32)
    out_ref[...] = (normed * valid).astype(BF)
    grad_y = cot_ref[...].astype(F32) * valid
    grad = norm_backward(grad_y, normal, inv, gain)
    grad_ref[...] = grad
    low = grad.astype(BF)
    low_ref[...] = low
    sum_ref[...] = jnp.zeros_like(sum_ref)
    sum_ref[0:1, :] = col_sum(grad_y * normal)
    sum_ref[1:2, :] = col_sum(grad_y)
    sum_ref[2:3, :] = col_sum(low.astype(F32))


def norm2(meta, hidden, keep, near, far, cot, vecs):
    rows, width = hidden.shape
    vmem = pl.BlockSpec(memory_space=pltpu.VMEM)
    return pl.pallas_call(
        norm2_kernel,
        in_specs=[pl.BlockSpec(memory_space=pltpu.SMEM)] + [vmem] * 6,
        out_specs=[vmem] * 4,
        out_shape=[
            jax.ShapeDtypeStruct((rows, width), BF),
            jax.ShapeDtypeStruct((rows, width), F32),
            jax.ShapeDtypeStruct((rows, width), BF),
            jax.ShapeDtypeStruct((8, width), F32),
        ],
        compiler_params=pltpu.CompilerParams(vmem_limit_bytes=VMEM_BYTES),
        cost_estimate=pl.CostEstimate(flops=1 << 22, bytes_accessed=4 << 20, transcendentals=0),
        name="norm2_both",
    )(meta, hidden, keep, near, far, cot, vecs)


def norm1_back_kernel(
    keep_ref, near_ref, far_ref, add_ref, normal_ref, inv_ref, vec_ref, w_ref, out_ref, low_ref, mixed_ref, sum_ref
):
    grad = keep_ref[...] + near_ref[...].astype(F32) + far_ref[...].astype(F32) + add_ref[...]
    normal = normal_ref[...]
    resid = norm_backward(grad, normal, inv_ref[:, 0:1], vec_ref[1:2, :])
    out_ref[...] = resid
    low = resid.astype(BF)
    low_ref[...] = low
    step = mixed_ref.shape[2]
    for j in range(mixed_ref.shape[0]):
        mixed_ref[j] = nt(low, w_ref[j * step : (j + 1) * step, :]).astype(BF)
    sum_ref[...] = jnp.zeros_like(sum_ref)
    sum_ref[0:1, :] = col_sum(grad * normal)
    sum_ref[1:2, :] = col_sum(grad)
    sum_ref[2:3, :] = col_sum(low.astype(F32))


def norm1_back(keep, near, far, add, normal, inv, vecs, w, cols_n):
    rows, width = add.shape
    return small_call(
        norm1_back_kernel,
        [
            jax.ShapeDtypeStruct((rows, width), F32),
            jax.ShapeDtypeStruct((rows, width), BF),
            jax.ShapeDtypeStruct((cols_n, rows, width // cols_n), BF),
            jax.ShapeDtypeStruct((8, width), F32),
        ],
        2 * rows * width * width,
        "norm1_back",
    )(keep, near, far, add, normal, inv, vecs, w)


CORE = [(0, 1), (1, 0), (2, 3), (3, 2)]
CROSS = [(0, 2), (2, 0), (1, 3), (3, 1)]


def core_swap(x):
    return lax.ppermute(x, "row", CORE)


def cross_swap(x):
    return lax.ppermute(x, "row", CROSS)


def shift_col(x, step):
    n = lax.axis_size("col")
    return lax.ppermute(x, "col", [(i, (i + step) % n) for i in range(n)])


def gather_row_rel(x):
    far = cross_swap(x)
    near = core_swap(x)
    return [x, near, far, core_swap(far)]


def natural_row(blocks):
    r = lax.axis_index("row")
    low = (r & 1) == 0
    b0, b1, b2, b3 = blocks
    left = jnp.where(low, jnp.concatenate([b0, b1]), jnp.concatenate([b1, b0]))
    right = jnp.where(low, jnp.concatenate([b2, b3]), jnp.concatenate([b3, b2]))
    return jnp.where(r < 2, jnp.concatenate([left, right]), jnp.concatenate([right, left]))


def reduce_row_rel(own, near, far, diag):
    got = core_swap(jnp.stack([near, diag]).astype(BF))
    own = own + got[0].astype(F32)
    far = far + got[1].astype(F32)
    return own + cross_swap(far.astype(BF)).astype(F32)


def gather_col(x):
    n = lax.axis_size("col")
    z = lax.axis_index("col")
    out = jnp.zeros((n,) + x.shape, x.dtype)
    block = x
    out = lax.dynamic_update_index_in_dim(out, block, z, 0)
    for step in range(1, n):
        block = shift_col(block, 1)
        out = lax.dynamic_update_index_in_dim(out, block, (z + n - step) % n, 0)
    return out


def reduce_col(parts):
    n = lax.axis_size("col")
    z = lax.axis_index("col")

    def part(k):
        return lax.dynamic_index_in_dim(parts, (z + n - k) % n, 0, keepdims=False).astype(F32)

    total = part(1)
    for step in range(2, n + 1):
        total = part(step) + shift_col(total.astype(BF), 1).astype(F32)
    return total


def sum_dp(x):
    n = lax.axis_size("dp")
    if n == 2:
        return x + lax.ppermute(x, "dp", [(0, 1), (1, 0)])
    return lax.psum(x, "dp")


def split3(x):
    hi = lax.reduce_precision(x, 8, 7)
    mid = lax.reduce_precision(x - hi, 8, 7)
    low = x - hi - mid
    return hi.astype(BF), mid.astype(BF), low.astype(BF)


def per_device(
    tokens,
    cotangent,
    lengths,
    query_weight,
    key_weight,
    value_weight,
    query_bias,
    value_bias,
    out_weight,
    out_bias,
    norm1_gain,
    norm1_shift,
    up_weight,
    up_bias,
    down_weight,
    down_bias,
    norm2_gain,
    norm2_shift,
):
    rows_n = lax.axis_size("row")
    cols_n = lax.axis_size("col")
    r = lax.axis_index("row")
    z = lax.axis_index("col")
    local, width = tokens.shape
    block_len = local * cols_n
    length = lengths[0]
    hw = width // cols_n
    heads = hw // HD
    feat = width // rows_n
    scale = 1.0 / math.sqrt(HD)
    meta = jnp.stack([length, r, z * (local * rows_n) + r * local]).astype(jnp.int32)

    x_col = gather_col(tokens).reshape(block_len, width)

    qkv = jnp.stack([query_weight, key_weight, value_weight], axis=1).astype(BF)
    sub = qkv.shape[0]
    qkv = qkv.reshape(sub, 3, cols_n, hw).transpose(2, 0, 1, 3).reshape(cols_n, sub, 3 * hw)
    qkv = lax.all_to_all(qkv, "col", split_axis=0, concat_axis=0, tiled=True)
    qkv = qkv.reshape(cols_n * sub, 3 * hw)
    vecs = jnp.stack([out_bias, norm1_gain, norm1_shift, down_bias, norm2_gain, norm2_shift])
    vec_parts = jnp.stack(split3(vecs)).reshape(-1)
    vec_rows = 16
    vec_parts = jnp.pad(vec_parts, (0, vec_rows * 3 * hw - vec_parts.shape[0]))
    message = jnp.concatenate([qkv, vec_parts.reshape(vec_rows, 3 * hw)])
    got = natural_row([b[None] for b in gather_row_rel(message)])
    w_qkv = got[:, : cols_n * sub].reshape(width, 3 * hw)
    vec_all = got[:, cols_n * sub :].reshape(rows_n, -1)[:, : 3 * 6 * feat]
    vec_all = jnp.sum(vec_all.reshape(rows_n, 3, 6, feat).astype(F32), axis=1)
    vec_all = vec_all.transpose(1, 0, 2).reshape(6, width)
    vecs = jnp.concatenate([vec_all, jnp.zeros((2, width), F32)])

    up_t = up_weight.astype(BF).T
    units = up_t.shape[0] // rows_n
    up_t = up_t.reshape(rows_n, units, feat)
    up_t = lax.all_to_all(up_t, "row", split_axis=0, concat_axis=0, tiled=True)
    up_t = up_t.transpose(1, 0, 2).reshape(units, width)
    bias_mine = lax.dynamic_slice_in_dim(up_bias, r * units, units, 0)
    bias_rows = jnp.pad(jnp.stack(split3(bias_mine)), ((0, 13), (0, width - units)))
    sub_out = out_weight.shape[0]
    pack = jnp.concatenate([up_t, down_weight.astype(BF), out_weight.astype(BF), bias_rows])
    pack, x_col = lax.optimization_barrier((pack, x_col))
    pack = gather_col(pack)
    up_r = pack[:, :units].reshape(cols_n * units, width)
    down_r = pack[:, units : 2 * units].reshape(cols_n * units, width)
    out_r = pack[:, 2 * units : 2 * units + sub_out]
    up_bias_r = jnp.sum(pack[:, 2 * units + sub_out :][:, :3, :units].astype(F32), axis=1)
    up_bias_r = up_bias_r.reshape(1, cols_n * units)

    kv_bias = jnp.concatenate([jnp.zeros_like(value_bias), value_bias])
    kv = (nn(x_col, w_qkv[:, hw:]) + kv_bias).astype(BF)
    pad = LANES - hw
    q_weight = jnp.pad(w_qkv[:, :hw], ((0, 0), (0, pad)))
    q_bias = jnp.concatenate([query_bias, jnp.full((1,), 1.0 / scale, F32), jnp.zeros((pad - 1,), F32)])
    q_rows = ((nn(x_col, q_weight) + q_bias) * scale).astype(BF)
    kv_own, kv_near, kv_far, kv_diag = gather_row_rel(kv)
    acc, stat, k_near, v_near = attn_fwd(meta, q_rows, (kv_own, kv_near), (0, 1), heads, local, rows_n)
    mixed_part, qb_rows, k_far, v_far = attn_fwd(
        meta, q_rows, (kv_far, kv_diag), (2, 3), heads, local, rows_n, state=(acc, stat)
    )
    mixed = lax.all_to_all(
        mixed_part.reshape(cols_n, local, hw), "col", split_axis=0, concat_axis=0, tiled=True
    )

    out_full = natural_row([b[None] for b in gather_row_rel(out_r)])
    out_full = out_full.transpose(1, 0, 2, 3).reshape(width, width)
    hidden, hidden_low, normal1, inv1 = project(mixed, out_full, tokens, vecs)

    h_own, h_near, h_far, h_diag = gather_row_rel(hidden_low)
    keep0, send0, act0, slope0 = ffn_fwd(h_own, h_near, up_r, up_bias_r, down_r)
    keep1, send1, act1, slope1 = ffn_fwd(h_far, h_diag, up_r, up_bias_r, down_r)
    got = core_swap(jnp.stack([send0, send1]))
    got_far = cross_swap((keep1 + got[1].astype(F32)).astype(BF))
    output, grad_resid2, grad_branch, sums2 = norm2(meta, hidden, keep0, got[0], got_far, cotangent, vecs)

    g_own, g_near, g_far, g_diag = gather_row_rel(grad_branch)
    keep0, send0, pre0 = ffn_bwd(g_own, g_near, up_r, down_r, slope0)
    keep1, send1, pre1 = ffn_bwd(g_far, g_diag, up_r, down_r, slope1)
    got = core_swap(jnp.stack([send0, send1]))
    got_far = cross_swap((keep1 + got[1].astype(F32)).astype(BF))
    active = jnp.concatenate([act0, act1])
    grad_preact = jnp.concatenate([pre0, pre1])
    grad_branch_all = jnp.concatenate([g_own, g_near, g_far, g_diag])
    hidden_all = jnp.concatenate([h_own, h_near, h_far, h_diag])
    g_down = tn(active, grad_branch_all).astype(BF).reshape(cols_n, units, width)
    g_up = tn(grad_preact, hidden_all).astype(BF).reshape(cols_n, units, width)
    g_up_bias = jnp.sum(grad_preact.astype(F32), axis=0)
    grad_resid1, grad_attended, grad_mixed_local, sums1 = norm1_back(
        keep0, got[0], got_far, grad_resid2, normal1, inv1, vecs, out_full, cols_n
    )
    grad_mixed = lax.all_to_all(grad_mixed_local, "col", split_axis=0, concat_axis=0, tiled=True)
    grad_mixed = grad_mixed.reshape(block_len, hw)

    g_out = jnp.stack([tn(mixed[j], grad_attended) for j in range(cols_n)])
    g_out = g_out.reshape(cols_n, rows_n, sub_out, width)
    g_out = [lax.dynamic_index_in_dim(g_out, r ^ k, 1, keepdims=False) for k in range(4)]
    g_out = reduce_row_rel(*g_out).astype(BF)
    g_pack = jnp.concatenate([g_up, g_down, g_out], axis=1)
    g_pack = sum_dp(reduce_col(g_pack).astype(BF))
    g_up = g_pack[:units].reshape(units, rows_n, feat)
    g_up = lax.all_to_all(g_up, "row", split_axis=1, concat_axis=0, tiled=True)
    g_up_weight = g_up.reshape(rows_n * units, feat).T.astype(F32)
    g_down_weight = g_pack[units : 2 * units].astype(F32)
    g_out_weight = g_pack[2 * units :].astype(F32)

    far_keep, far_send, dq, do_rows = attn_bwd(qb_rows, (grad_mixed, mixed_part), k_far, v_far, heads, scale)
    far_got = cross_swap((far_keep + core_swap(far_send).astype(F32)).astype(BF))
    near_keep, near_send, grad_q = attn_bwd(qb_rows, do_rows, k_near, v_near, heads, scale, dq=dq)
    grad_kv = near_keep + core_swap(near_send).astype(F32) + far_got.astype(F32)
    grad_qkv = jnp.concatenate([grad_q, grad_kv.astype(BF)], axis=1)

    back = nt(grad_qkv, w_qkv).reshape(cols_n, local, width)
    grad_tokens = grad_resid1 + reduce_col(back)

    g_qkv = tn(x_col, grad_qkv).reshape(rows_n, feat, 3 * hw)
    g_bias = jnp.sum(grad_qkv.astype(F32), axis=0)
    g_qkv = [lax.dynamic_index_in_dim(g_qkv, r ^ k, 0, keepdims=False) for k in range(4)]
    g_qkv = sum_dp(reduce_row_rel(*g_qkv).astype(BF))
    g_qkv = lax.all_to_all(
        g_qkv.reshape(cols_n, sub, 3 * hw), "col", split_axis=0, concat_axis=0, tiled=True
    )
    g_qkv = g_qkv.reshape(cols_n, sub, 3, hw).transpose(2, 1, 0, 3).reshape(3, sub, width)
    g_qkv = g_qkv.astype(F32)

    up_place = jnp.zeros((cols_n, rows_n, units), F32)
    up_place = lax.dynamic_update_slice(
        up_place, g_up_bias.reshape(cols_n, 1, units), (0, r, 0)
    ).reshape(-1, width)
    bias_place = jnp.zeros((2, width), F32)
    bias_place = lax.dynamic_update_slice(
        bias_place, jnp.stack([g_bias[:hw], g_bias[2 * hw :]]), (0, z * hw)
    )
    sums = jnp.concatenate([sums1[:3], sums2[:3], up_place, bias_place])
    sums = sums + core_swap(sums)
    sums = sums + cross_swap(sums)
    sums = sum_dp(sums)
    sums = sums + lax.ppermute(sums, "col", [(i, i ^ 1) for i in range(cols_n)])
    sums = sums + lax.ppermute(sums, "col", [(i, i ^ 2) for i in range(cols_n)])
    mine = lax.dynamic_slice_in_dim(sums[:6], r * feat, feat, 1)
    g_up_bias = lax.dynamic_index_in_dim(
        sums[6:-2].reshape(cols_n, rows_n * units), z, 0, keepdims=False
    )
    g_bias = lax.dynamic_slice_in_dim(sums[-2:], z * hw, hw, 1)
    return (
        output,
        grad_tokens,
        g_qkv[0],
        g_qkv[1],
        g_qkv[2],
        g_bias[0],
        g_bias[1],
        g_out_weight,
        mine[2],
        mine[0],
        mine[1],
        g_up_weight,
        g_up_bias,
        g_down_weight,
        mine[5],
        mine[3],
        mine[4],
    )


def solution(mesh):
    token_spec = P(("dp", "col", "row"), None)
    placed = (
        token_spec,
        token_spec,
        P("dp"),
        P(("row", "col"), None),
        P(("row", "col"), None),
        P(("row", "col"), None),
        P("col"),
        P("col"),
        P(("col", "row"), None),
        P("row"),
        P("row"),
        P("row"),
        P("row", "col"),
        P("col"),
        P(("col", "row"), None),
        P("row"),
        P("row"),
        P("row"),
    )
    return jax.shard_map(
        per_device,
        mesh=mesh,
        in_specs=placed,
        out_specs=(token_spec, token_spec) + placed[3:],
        check_vma=False,
    )
```

```python
import functools
import math

import jax
import jax.numpy as jnp
from jax import lax
from jax.experimental import pallas as pl
from jax.experimental.pallas import tpu as pltpu
from jax.sharding import PartitionSpec as P

HD = 64
LANES = 256
EPS = 1e-05
BF = jnp.bfloat16
F32 = jnp.float32
VMEM_BYTES = 60 * 1024 * 1024
TURNED = HD + 16
SMALL_BYTES = 24 * 1024 * 1024


def nn(a, b):
    return jnp.dot(a, b, preferred_element_type=F32)


def tn(a, b):
    return lax.dot_general(a, b, (((0,), (0,)), ((), ())), preferred_element_type=F32)


def nt(a, b):
    return lax.dot_general(a, b, (((1,), (1,)), ((), ())), preferred_element_type=F32)


def cost(us):
    return pl.CostEstimate(flops=int(us * 0.6e9), bytes_accessed=1000, transcendentals=0)


def head_lanes(shape, head, width):
    lane = lax.broadcasted_iota(jnp.int32, shape, 1)
    mine = (lane >= head * HD) & (lane < (head + 1) * HD)
    return mine | (lane == width) | ((lane >= width + 1 + 3 * head) & (lane < width + 4 + 3 * head))


def three_parts(x):
    hi = x.astype(BF).astype(F32)
    mid = (x - hi).astype(BF).astype(F32)
    return hi, mid, x - hi - mid


def tail_rows(parts, ones, n):
    row = lax.broadcasted_iota(jnp.int32, (n, parts[0].shape[1]), 0)
    out = jnp.where(row == 0, ones, 0.0)
    for head, value in enumerate(parts):
        for i, piece in enumerate(three_parts(value)):
            out = jnp.where(row == 1 + 3 * head + i, piece, out)
    return out


def widen_keys(kv, owner, meta, keys_out, values_out, turned, at, width, shift, sizes):
    n = kv.shape[0]
    rows_n, cols_n = sizes
    keys_out[at : at + n, :width] = kv[:, :width]
    values_out[at : at + n, :width] = kv[:, width:]
    shape = (n, LANES - width)
    t = lax.broadcasted_iota(jnp.int32, shape, 0)
    lane = lax.broadcasted_iota(jnp.int32, shape, 1)
    source = meta[3] - (t >> shift)
    source = jnp.where(source < 0, source + cols_n, source)
    position = ((source * rows_n + owner) << shift) + (t & ((1 << shift) - 1))
    mask = jnp.where(lane == 0, jnp.where(position >= meta[0], -1e30, 0.0), 1.0)
    keys_out[at : at + n, width:] = mask.astype(BF)
    values_out[at : at + n, width:] = jnp.ones(shape, BF)
    flat = values_out[at : at + n, :].T
    for head in range(width // HD):
        first = head * TURNED
        turned[first : first + HD, at : at + n] = flat[head * HD : (head + 1) * HD, :]
        turned[first + HD : first + TURNED, at : at + n] = jnp.ones((TURNED - HD, n), BF)


def attn_fwd_kernel(*refs, heads, first, pair, shift, sizes, chunk, blocks):
    if first:
        meta, q_ref, kv0, kv1, acc_out, stat_out, k_out, v_out, turned = refs
    else:
        meta, q_ref, kv0, kv1, acc_in, stat_in = refs[:6]
        outs = refs[6 : 6 + blocks]
        qb_ref, k_out, v_out, turned = refs[6 + blocks :]
    width = heads * HD
    half = kv0.shape[0]
    keys = 2 * half
    for i, ref in enumerate((kv0, kv1)):
        widen_keys(
            ref[...], meta[1] ^ pair[i], meta, k_out, v_out, turned, i * half, width, shift, sizes
        )
    q = q_ref[...]
    rows = q.shape[0]
    slot = lax.broadcasted_iota(jnp.int32, (16, rows), 0)
    stat = jnp.zeros((16, rows), F32)
    logs = []
    for head in range(heads):
        qh = jnp.where(head_lanes(q.shape, head, width), q, jnp.zeros_like(q))
        scores = [nt(k_out[i : i + chunk, :], qh) for i in range(0, keys, chunk)]
        peak = functools.reduce(
            jnp.maximum, [jnp.max(s, axis=0, keepdims=True) for s in scores]
        )
        if not first:
            old = stat_in[head : head + 1, :]
            peak = jnp.maximum(peak, old)
        acc = None
        for i, s in enumerate(scores):
            p = jnp.exp(s - peak).astype(BF)
            at = head * TURNED
            part = nn(turned[at : at + TURNED, i * chunk : (i + 1) * chunk], p)
            acc = part if acc is None else acc + part
        total = acc[HD : HD + 1]
        mine = slice(head * HD, (head + 1) * HD)
        if first:
            acc_out[mine, :] = acc[:HD]
            stat = jnp.where(slot == head, peak, stat)
            stat = jnp.where(slot == head + 8, total, stat)
        else:
            keep = jnp.exp(old - peak)
            total = total + stat_in[head + 8 : head + 9, :] * keep
            out = ((acc[:HD] + acc_in[mine, :] * keep) * (1.0 / total)).astype(BF)
            each = rows // blocks
            for b in range(blocks):
                outs[b][mine, :] = out[:, b * each : (b + 1) * each]
            logs.append(-(peak + jnp.log(total)))
    if first:
        stat_out[...] = stat
    else:
        qb_ref[:, :width] = q[:, :width]
        qb_ref[:, width:] = tail_rows(logs, 1.0, LANES - width).T.astype(BF)


def attn_fwd(meta, q, kv_pair, pair, heads, local, sizes, state=None, chunk=512):
    rows = q.shape[0]
    half, double = kv_pair[0].shape
    width = double // 2
    first = state is None
    blocks = rows // local
    vmem = pl.BlockSpec(memory_space=pltpu.VMEM)
    args = [meta, q, *kv_pair]
    if first:
        out_shape = [jax.ShapeDtypeStruct((width, rows), F32), jax.ShapeDtypeStruct((16, rows), F32)]
    else:
        args += list(state)
        out_shape = [jax.ShapeDtypeStruct((width, local), BF)] * blocks
        out_shape += [jax.ShapeDtypeStruct((rows, LANES), BF)]
    out_shape += [jax.ShapeDtypeStruct((2 * half, LANES), BF)] * 2
    return pl.pallas_call(
        functools.partial(
            attn_fwd_kernel,
            heads=heads,
            first=first,
            pair=pair,
            shift=local.bit_length() - 1,
            sizes=sizes,
            chunk=chunk,
            blocks=blocks,
        ),
        in_specs=[pl.BlockSpec(memory_space=pltpu.SMEM)] + [vmem] * (len(args) - 1),
        out_specs=[vmem] * len(out_shape),
        out_shape=out_shape,
        scratch_shapes=[pltpu.VMEM((heads * TURNED, 2 * half), BF)],
        compiler_params=pltpu.CompilerParams(vmem_limit_bytes=VMEM_BYTES),
        cost_estimate=cost(4),
        name="attn_fwd_near" if first else "attn_fwd_far",
    )(*args)


def grad_rows_kernel(*refs, heads, blocks):
    outs, grads, wide = refs[:blocks], refs[blocks : 2 * blocks], refs[2 * blocks]
    width = heads * HD
    for b in range(blocks):
        g = grads[b][...].astype(F32)
        prod = g * outs[b][...].astype(F32)
        each = g.shape[1]
        parts = [
            -jnp.sum(prod[head * HD : (head + 1) * HD], axis=0, keepdims=True) for head in range(heads)
        ]
        tall = jnp.concatenate([g, tail_rows(parts, 0.0, LANES - width)], axis=0)
        wide[b * each : (b + 1) * each, :] = tall.T.astype(BF)


def grad_rows(outs, grads, heads):
    each = outs[0].shape[1]
    return small_call(
        functools.partial(grad_rows_kernel, heads=heads, blocks=len(outs)),
        jax.ShapeDtypeStruct((each * len(outs), LANES), BF),
        "grad_rows",
    )(*outs, *grads)


def attn_bwd_kernel(*refs, heads, first, last, block, scale):
    if first:
        q_ref, g_ref, k_ref, v_ref, out_ref, dq_out, dk, dv = refs
    else:
        q_ref, g_ref, k_ref, v_ref, dq_in, out_ref, dq_out, dk, dv = refs
    width = heads * HD
    dk[...] = jnp.zeros_like(dk)
    dv[...] = jnp.zeros_like(dv)

    def step(i, carry):
        at = pl.ds(pl.multiple_of(i * block, block), block)
        q_all = q_ref[at, :]
        g_all = g_ref[at, :]
        k = k_ref[...]
        dq = jnp.zeros((block, LANES), F32)
        for head in range(heads):
            mine = head_lanes((block, LANES), head, width)
            q = jnp.where(mine, q_all, jnp.zeros_like(q_all))
            g = jnp.where(mine, g_all, jnp.zeros_like(g_all))
            p = jnp.exp(nt(k, q))
            ds = (p * nt(v_ref[...], g)).astype(BF)
            dv[...] += nn(p.astype(BF), g)
            dk[...] += nn(ds, q)
            dq = jnp.where(mine, tn(ds, k), dq)
        dq = dq[:, :width]
        if not first:
            dq = dq + dq_in[at, :]
        dq_out[at, :] = (dq * scale).astype(dq_out.dtype) if last else dq
        return carry

    lax.fori_loop(0, q_ref.shape[0] // block, step, 0)
    out_ref[:, :width] = dk[:, :width].astype(out_ref.dtype)
    out_ref[:, width:] = dv[:, :width].astype(out_ref.dtype)


def attn_bwd(q, g, k, v, at, heads, scale, kind, dq=None, last=False, block=512):
    rows = q.shape[0]
    half = k.shape[0] // 2
    width = heads * HD
    first = dq is None

    def whole(shape):
        return pl.BlockSpec(shape, lambda i: (0,) * len(shape))

    part = pl.BlockSpec((half, LANES), lambda i: (at, 0))
    args = [q, g, k, v] + ([] if first else [dq])
    specs = [whole(q.shape), whole(g.shape), part, part] + ([] if first else [whole(dq.shape)])
    return pl.pallas_call(
        functools.partial(
            attn_bwd_kernel, heads=heads, first=first, last=last, block=block, scale=scale
        ),
        grid=(1,),
        in_specs=specs,
        out_specs=[whole((half, 2 * width)), whole((rows, width))],
        out_shape=[
            jax.ShapeDtypeStruct((half, 2 * width), kind),
            jax.ShapeDtypeStruct((rows, width), BF if last else F32),
        ],
        scratch_shapes=[pltpu.VMEM((half, LANES), F32)] * 2,
        compiler_params=pltpu.CompilerParams(vmem_limit_bytes=VMEM_BYTES),
        cost_estimate=cost(4),
        name="attn_bwd_%d" % at,
    )(*args)


def small_call(kernel, out_shape, name, scratch=(), us=1.4):
    return pl.pallas_call(
        kernel,
        out_shape=out_shape,
        scratch_shapes=scratch,
        compiler_params=pltpu.CompilerParams(vmem_limit_bytes=SMALL_BYTES),
        cost_estimate=cost(us),
        name=name,
    )


def meta_call(kernel, args, out_shape, name, scratch=(), us=1.2):
    vmem = pl.BlockSpec(memory_space=pltpu.VMEM)
    return pl.pallas_call(
        kernel,
        in_specs=[pl.BlockSpec(memory_space=pltpu.SMEM)] + [vmem] * (len(args) - 1),
        out_specs=[vmem] * len(out_shape),
        out_shape=out_shape,
        scratch_shapes=scratch,
        compiler_params=pltpu.CompilerParams(vmem_limit_bytes=SMALL_BYTES),
        cost_estimate=cost(us),
        name=name,
    )(*args)


def row_mean(x):
    return jnp.mean(x, axis=1, keepdims=True)


def col_sum(x):
    return jnp.sum(x, axis=0, keepdims=True)


def norm_forward(resid, gain, shift):
    centered = resid - row_mean(resid)
    inv = lax.rsqrt(row_mean(centered * centered) + EPS)
    normal = centered * inv
    return normal * gain + shift, normal, inv


def norm_backward(grad_out, normal, inv, gain):
    scaled = grad_out * gain
    return inv * (scaled - row_mean(scaled) - normal * row_mean(scaled * normal))


def project_qkv_kernel(meta, *refs, n, rows_n, feat, hw, scale):
    x = refs[:n]
    ws, bias_ref, vec_ref, q_ref, kv_ref, w_out, pack_ref, w_all = refs[n : n + rows_n], *refs[n + rows_n :]
    each = feat // n
    for k in range(rows_n):
        for m in range(n):
            source = meta[3] - m
            source = jnp.where(source < 0, source + n, source)
            at = pl.multiple_of((meta[1] ^ k) * feat + source * each, each)
            w_all[pl.ds(at, each), :] = ws[k][m * each : (m + 1) * each, :]
    w = w_all[...]
    w_out[...] = w.T
    each = q_ref.shape[0] // n
    for k in range(n):
        at = slice(k * each, (k + 1) * each)
        out = nn(x[k][:each, :], w) + bias_ref[0:1, :]
        q_ref[at, :hw] = (out[:, :hw].astype(BF).astype(F32) * scale).astype(BF)
        lane = lax.broadcasted_iota(jnp.int32, (each, LANES - hw), 1)
        q_ref[at, hw:] = jnp.where(lane == 0, 1.0, 0.0).astype(BF)
        kv_ref[at, :] = out[:, hw:].astype(BF)
        more = x[k].shape[0] - each
        pack_ref[k * more : (k + 1) * more, :] = x[k][each:, :]
    pack_ref[n * more :, :] = vec_ref[...]


def project_qkv(meta, x, ws, bias, vecs, local, scale):
    feat, wide = ws[0].shape
    hw = wide // 3
    rows = local * len(x)
    return meta_call(
        functools.partial(
            project_qkv_kernel, n=len(x), rows_n=len(ws), feat=feat, hw=hw, scale=scale
        ),
        [meta, *x, *ws, bias, vecs],
        [
            jax.ShapeDtypeStruct((rows, LANES), BF),
            jax.ShapeDtypeStruct((rows, 2 * hw), BF),
            jax.ShapeDtypeStruct((wide, feat * len(ws)), BF),
            jax.ShapeDtypeStruct(((x[0].shape[0] - local) * len(x) + vecs.shape[0], vecs.shape[1]), BF),
        ],
        "project_qkv",
        scratch=[pltpu.VMEM((feat * len(ws), wide), BF)],
    )


def project_kernel(meta, *refs, n, rows_n, sub, feat):
    mixed, packs = refs[:n], refs[n : n + rows_n]
    x_ref, hid_ref, low_ref, normal_ref, inv_ref, w_ref, vec_ref = refs[n + rows_n :]
    r = meta[1]
    for k in range(rows_n):
        at = pl.multiple_of((r ^ k) * sub, sub)
        for i in range(n):
            w_ref[i, pl.ds(at, sub), :] = packs[k][((n - i) % n) * sub : ((n - i) % n + 1) * sub, :]
    values = []
    for k in range(rows_n):
        part = packs[k][n * sub : n * sub + 32, :feat].astype(F32)
        values.append(part[0:8] + part[8:16] + part[16:24])
    pieces = []
    for owner in range(rows_n):
        value = values[0]
        for k in range(1, rows_n):
            value = jnp.where((r ^ k) == owner, values[k], value)
        pieces.append(value)
    vecs = jnp.concatenate(pieces, axis=1)
    vec_ref[...] = vecs
    total = x_ref[...].astype(F32) + vecs[0:1, :]
    for j in range(n):
        total = total + tn(mixed[j][...], w_ref[j])
    hidden, normal, inv = norm_forward(total, vecs[1:2, :], vecs[2:3, :])
    hid_ref[...] = hidden
    low_ref[...] = hidden.astype(BF)
    normal_ref[...] = normal
    inv_ref[...] = jnp.broadcast_to(inv, inv_ref.shape)


def project(meta, mixed, packs, x, sub):
    rows, width = x.shape
    feat = width // len(packs)
    return meta_call(
        functools.partial(
            project_kernel, n=len(mixed), rows_n=len(packs), sub=sub, feat=feat
        ),
        [meta, *mixed, *packs, x],
        [
            jax.ShapeDtypeStruct((rows, width), F32),
            jax.ShapeDtypeStruct((rows, width), BF),
            jax.ShapeDtypeStruct((rows, width), F32),
            jax.ShapeDtypeStruct((rows, 128), F32),
            jax.ShapeDtypeStruct((len(mixed), sub * len(packs), width), BF),
            jax.ShapeDtypeStruct((8, width), F32),
        ],
        "project_norm1",
    )


def stack_refs(refs, at, n):
    return jnp.concatenate([ref[at : at + n, :] for ref in refs], axis=0)


def ffn_fwd_kernel(*refs, n, units):
    h0, h1 = refs[:2]
    packs = refs[2 : 2 + n]
    bias_ref, keep_ref, send_ref, act_ref, slope_ref = refs[2 + n :]
    rows = h0.shape[0]
    h = jnp.concatenate([h0[...], h1[...]], axis=0)
    x = nt(h, stack_refs(packs, 0, units)) + bias_ref[...]
    cdf = 0.5 * (1.0 + lax.erf(x * math.sqrt(0.5)))
    act = (x * cdf).astype(BF)
    act_ref[...] = act
    slope = cdf + x * (math.sqrt(0.5 / math.pi) * jnp.exp(-0.5 * x * x))
    slope_ref[...] = slope.astype(BF)
    out = nn(act, stack_refs(packs, units, units))
    keep_ref[...] = out[:rows]
    send_ref[...] = out[rows:].astype(BF)


def ffn_fwd(h0, h1, packs, bias, units):
    rows, width = h0.shape
    wide = units * len(packs)
    return small_call(
        functools.partial(ffn_fwd_kernel, n=len(packs), units=units),
        [
            jax.ShapeDtypeStruct((rows, width), F32),
            jax.ShapeDtypeStruct((rows, width), BF),
            jax.ShapeDtypeStruct((2 * rows, wide), BF),
            jax.ShapeDtypeStruct((2 * rows, wide), BF),
        ],
        "ffn_fwd",
    )(h0, h1, *packs, bias)


def ffn_bwd_kernel(*refs, n, units):
    g0, g1 = refs[:2]
    packs = refs[2 : 2 + n]
    slope_ref, keep_ref, send_ref, pre_ref = refs[2 + n :]
    rows = g0.shape[0]
    g = jnp.concatenate([g0[...], g1[...]], axis=0)
    pre = (nt(g, stack_refs(packs, units, units)) * slope_ref[...].astype(F32)).astype(BF)
    pre_ref[...] = pre
    out = nn(pre, stack_refs(packs, 0, units))
    keep_ref[...] = out[:rows]
    send_ref[...] = out[rows:].astype(BF)


def ffn_bwd(g0, g1, packs, slope, units):
    rows, width = g0.shape
    wide = units * len(packs)
    return small_call(
        functools.partial(ffn_bwd_kernel, n=len(packs), units=units),
        [
            jax.ShapeDtypeStruct((rows, width), F32),
            jax.ShapeDtypeStruct((rows, width), BF),
            jax.ShapeDtypeStruct((2 * rows, wide), BF),
        ],
        "ffn_bwd",
    )(g0, g1, *packs, slope)


def ffn_grads_kernel(*refs, units, n):
    act0, act1, pre0, pre1 = refs[:4]
    h = jnp.concatenate([ref[...] for ref in refs[4:8]], axis=0)
    g = jnp.concatenate([ref[...] for ref in refs[8:12]], axis=0)
    outs, bias_ref = refs[12 : 12 + n], refs[12 + n]
    pre = jnp.concatenate([pre0[...], pre1[...]], axis=0)
    act = jnp.concatenate([act0[...], act1[...]], axis=0)
    g_up = tn(pre, h)
    g_down = tn(act, g)
    for k in range(n):
        at = slice(k * units, (k + 1) * units)
        outs[k][:units, :] = g_up[at].astype(BF)
        outs[k][units:, :] = g_down[at].astype(BF)
    bias_ref[...] = jnp.broadcast_to(col_sum(pre.astype(F32)), bias_ref.shape)


def ffn_grads(acts, pres, hiddens, grads, units, n):
    width = hiddens[0].shape[1]
    shapes = [jax.ShapeDtypeStruct((2 * units, width), BF)] * n
    shapes += [jax.ShapeDtypeStruct((8, units * n), F32)]
    out = small_call(
        functools.partial(ffn_grads_kernel, units=units, n=n), shapes, "ffn_grads"
    )(*acts, *pres, *hiddens, *grads)
    return out[:n], out[n]


def norm2_kernel(
    meta, hid_ref, keep_ref, near_ref, far_ref, cot_ref, vec_ref, out_ref, grad_ref, low_ref, sum_ref
):
    branch = keep_ref[...] + near_ref[...].astype(F32) + far_ref[...].astype(F32) + vec_ref[3:4, :]
    gain = vec_ref[4:5, :]
    normed, normal, inv = norm_forward(hid_ref[...] + branch, gain, vec_ref[5:6, :])
    row = lax.broadcasted_iota(jnp.int32, (out_ref.shape[0], 1), 0)
    valid = (meta[2] + row < meta[0]).astype(F32)
    out_ref[...] = (normed * valid).astype(BF)
    grad_y = cot_ref[...].astype(F32) * valid
    grad = norm_backward(grad_y, normal, inv, gain)
    grad_ref[...] = grad
    low = grad.astype(BF)
    low_ref[...] = low
    sum_ref[...] = jnp.zeros_like(sum_ref)
    sum_ref[0:1, :] = col_sum(grad_y * normal)
    sum_ref[1:2, :] = col_sum(grad_y)
    sum_ref[2:3, :] = col_sum(low.astype(F32))


def norm2(meta, hidden, keep, near, far, cot, vecs):
    rows, width = hidden.shape
    shapes = [
        jax.ShapeDtypeStruct((rows, width), BF),
        jax.ShapeDtypeStruct((rows, width), F32),
        jax.ShapeDtypeStruct((rows, width), BF),
        jax.ShapeDtypeStruct((8, width), F32),
    ]
    return meta_call(norm2_kernel, [meta, hidden, keep, near, far, cot, vecs], shapes, "norm2_both")


def norm1_back_kernel(
    keep_ref, near_ref, far_ref, add_ref, normal_ref, inv_ref, vec_ref, w_ref, out_ref, low_ref, sum_ref, *mixed
):
    grad = keep_ref[...] + near_ref[...].astype(F32) + far_ref[...].astype(F32) + add_ref[...]
    normal = normal_ref[...]
    resid = norm_backward(grad, normal, inv_ref[:, 0:1], vec_ref[1:2, :])
    out_ref[...] = resid
    low = resid.astype(BF)
    low_ref[...] = low
    for j, ref in enumerate(mixed):
        ref[...] = nt(w_ref[j], low).astype(BF)
    sum_ref[...] = jnp.zeros_like(sum_ref)
    sum_ref[0:1, :] = col_sum(grad * normal)
    sum_ref[1:2, :] = col_sum(grad)
    sum_ref[2:3, :] = col_sum(low.astype(F32))


def norm1_back(keep, near, far, add, normal, inv, vecs, w):
    rows, width = add.shape
    out = small_call(
        norm1_back_kernel,
        [
            jax.ShapeDtypeStruct((rows, width), F32),
            jax.ShapeDtypeStruct((rows, width), BF),
            jax.ShapeDtypeStruct((8, width), F32),
        ]
        + [jax.ShapeDtypeStruct((w.shape[1], rows), BF)] * w.shape[0],
        "norm1_back",
    )(keep, near, far, add, normal, inv, vecs, w)
    return out[0], out[1], out[2], out[3:]


def two_parts(x):
    hi = x.astype(BF).astype(F32)
    return jnp.concatenate([hi, x - hi], axis=0).astype(BF)


def both_parts(rows):
    n = rows.shape[0] // 2
    return rows[:n].astype(F32) + rows[n:].astype(F32)


def out_grads_kernel(meta, *refs, n, rows_n, sub):
    mixed, grad, s1, s2, bias = refs[:n], *refs[n : n + 4]
    keep, far, send, sums, total = refs[n + 4 :]
    g = grad[...]
    for j in range(n):
        total[j] = nn(mixed[j][...], g)
    count = n * sub
    for j in range(n):
        at = slice(j * sub, (j + 1) * sub)

        def rows(k):
            return total[j, pl.ds(pl.multiple_of((meta[1] ^ k) * sub, sub), sub), :]

        keep[at, :] = rows(0)
        far[at, :] = rows(2)
        send[at, :] = rows(1).astype(BF)
        send[count + j * sub : count + (j + 1) * sub, :] = rows(3).astype(BF)
    sums[...] = jnp.zeros_like(sums)
    sums[0:3, :] = s1[0:3, :]
    sums[3:6, :] = s2[0:3, :]
    units = bias.shape[1] // n
    for j in range(n):
        away = meta[3] - j
        away = jnp.where(away < 0, away + n, away)
        value = bias[0:1, :units]
        for k in range(1, n):
            value = jnp.where(away == k, bias[0:1, k * units : (k + 1) * units], value)
        zero = jnp.zeros_like(value)
        row = [jnp.where(meta[1] == owner, value, zero) for owner in range(rows_n)]
        sums[8 + j : 9 + j, :] = jnp.concatenate(row, axis=1)
    send[2 * count :, :] = two_parts(sums[...])


def out_grads(meta, mixed, grad, s1, s2, bias, sub, rows_n):
    n, heads, width = len(mixed), mixed[0].shape[0], grad.shape[1]
    shapes = [
        jax.ShapeDtypeStruct((n * sub, width), F32),
        jax.ShapeDtypeStruct((n * sub, width), F32),
        jax.ShapeDtypeStruct((2 * n * sub + 32, width), BF),
        jax.ShapeDtypeStruct((16, width), F32),
    ]
    return meta_call(
        functools.partial(out_grads_kernel, n=n, sub=sub, rows_n=rows_n),
        [meta, *mixed, grad, s1, s2, bias],
        shapes,
        "out_grads",
        scratch=[pltpu.VMEM((n, heads, width), F32)],
    )


def far_message_kernel(far, sums, got, out):
    n = far.shape[0]
    out[:n, :] = (far[...] + got[n : 2 * n, :].astype(F32)).astype(BF)
    out[n:, :] = two_parts(sums[...] + both_parts(got[2 * n :, :]))


def far_message(far, sums, got):
    n, width = far.shape
    shape = jax.ShapeDtypeStruct((n + 32, width), BF)
    return small_call(far_message_kernel, shape, "far_message", us=0.7)(far, sums, got)


def col_messages_kernel(*refs, n, sub):
    chunks, (keep, sums, near, far), outs = refs[:n], refs[n : n + 4], refs[n + 4 :]
    count = n * sub
    both = sums[...] + both_parts(near[2 * count :, :]) + both_parts(far[count:, :])
    parts = two_parts(both)
    own = keep[...] + near[:count, :].astype(F32) + far[:count, :].astype(F32)
    size = chunks[0].shape[0]
    for k in range(n):
        j = (n - k) % n
        outs[k][:size, :] = chunks[k][...]
        outs[k][size : size + sub, :] = own[j * sub : (j + 1) * sub].astype(BF)
        outs[k][size + sub :, :] = parts


def col_messages(chunks, keep, sums, near, far, sub):
    size, width = chunks[0].shape
    shapes = [jax.ShapeDtypeStruct((size + sub + 32, width), BF)] * len(chunks)
    return small_call(
        functools.partial(col_messages_kernel, n=len(chunks), sub=sub), shapes, "col_messages"
    )(*chunks, keep, sums, near, far)


def sum_messages_kernel(*refs):
    refs, out = refs[:-1], refs[-1]
    n = out.shape[0] - 32
    total = refs[0][:n, :].astype(F32)
    sums = both_parts(refs[0][n:, :])
    for ref in refs[1:]:
        total = total + ref[:n, :].astype(F32)
        sums = sums + both_parts(ref[n:, :])
    out[:n, :] = total.astype(BF)
    out[n:, :] = two_parts(sums)


def sum_messages(messages):
    shape = jax.ShapeDtypeStruct(messages[0].shape, BF)
    return small_call(sum_messages_kernel, shape, "sum_messages", us=0.7)(*messages)


def finish_kernel(meta, own, other, *refs, rows_n, units, sub):
    ups, (down, out, sums) = refs[:rows_n], refs[rows_n:]
    at = 2 * units + sub
    up = own[:units, :].astype(F32) + other[:units, :].astype(F32)
    feat = up.shape[1] // rows_n
    pieces = [up[:, k * feat : (k + 1) * feat] for k in range(rows_n)]
    for k in range(rows_n):
        value = pieces[0]
        for owner in range(1, rows_n):
            value = jnp.where((meta[1] ^ k) == owner, pieces[owner], value)
        ups[k][...] = value.T.astype(BF)
    down[...] = own[units : 2 * units, :].astype(F32) + other[units : 2 * units, :].astype(F32)
    out[...] = own[2 * units : at, :].astype(F32) + other[2 * units : at, :].astype(F32)
    sums[...] = both_parts(own[at:, :]) + both_parts(other[at:, :])


def finish(meta, own, other, rows_n, units, sub):
    width = own.shape[1]
    shapes = [jax.ShapeDtypeStruct((width // rows_n, units), BF)] * rows_n
    shapes += [jax.ShapeDtypeStruct((n, width), F32) for n in (units, sub, 16)]
    return meta_call(
        functools.partial(finish_kernel, rows_n=rows_n, units=units, sub=sub),
        [meta, own, other],
        shapes,
        "finish_grads",
    )


def up_grads_kernel(meta, *refs, n):
    pieces, out = refs[:n], refs[n]
    units = pieces[0].shape[1]
    values = [ref[...].astype(F32) for ref in pieces]
    for owner in range(n):
        value = values[0]
        for k in range(1, n):
            value = jnp.where((meta[1] ^ k) == owner, values[k], value)
        out[:, owner * units : (owner + 1) * units] = value


def up_grads(meta, pieces):
    feat, units = pieces[0].shape
    return meta_call(
        functools.partial(up_grads_kernel, n=len(pieces)),
        [meta, *pieces],
        [jax.ShapeDtypeStruct((feat, units * len(pieces)), F32)],
        "up_grads",
    )[0]


def join_kernel(keep, near, far, grad_q, w_ref, *outs):
    n = len(outs) // 2
    hw = grad_q.shape[1]
    each = outs[0].shape[0]
    for k in range(n):
        at = slice(k * each, (k + 1) * each)
        kv = (keep[at, :] + near[at, :].astype(F32) + far[at, :].astype(F32)).astype(BF)
        d = jnp.concatenate([grad_q[at, :], kv], axis=1)
        outs[k][...] = d
        outs[n + k][...] = nn(d, w_ref[...]).astype(outs[n + k].dtype)


def join_grads(keep, near, far, grad_q, w, n):
    rows, hw = grad_q.shape
    width = w.shape[1]
    shapes = [jax.ShapeDtypeStruct((rows // n, 3 * hw), BF)] * n
    shapes += [jax.ShapeDtypeStruct((rows // n, width), BF if k == 1 else F32) for k in range(n)]
    out = small_call(join_kernel, shapes, "join_grads")(keep, near, far, grad_q, w)
    return out[:n], out[n:]


def qkv_grads_kernel(meta, *refs, n, feat):
    x, grads, keep, far, send, total = refs[:n], refs[n : 2 * n], *refs[2 * n :]
    each = grads[0].shape[0]
    rows_of_x = jnp.concatenate([ref[:each, :] for ref in x], axis=0)
    g = jnp.concatenate([ref[...] for ref in grads], axis=0)
    total[...] = tn(rows_of_x, g)

    def rows(k):
        return total[pl.ds(pl.multiple_of((meta[1] ^ k) * feat, feat), feat), :]

    bias = col_sum(g.astype(F32))
    hi = bias.astype(BF).astype(F32)
    row = lax.broadcasted_iota(jnp.int32, (16, bias.shape[1]), 0)
    tail = jnp.where(row == 0, hi, jnp.where(row == 1, bias - hi, 0.0))
    keep[:feat, :] = rows(0)
    keep[feat:, :] = tail
    far[...] = rows(2)
    send[:feat, :] = rows(1).astype(BF)
    send[feat : 2 * feat, :] = rows(3).astype(BF)
    send[2 * feat :, :] = tail.astype(BF)


def qkv_grads(meta, x, grads, feat):
    wide = grads[0].shape[1]
    width = x[0].shape[1]
    return meta_call(
        functools.partial(qkv_grads_kernel, n=len(x), feat=feat),
        [meta, *x, *grads],
        [
            jax.ShapeDtypeStruct((feat + 16, wide), F32),
            jax.ShapeDtypeStruct((feat, wide), F32),
            jax.ShapeDtypeStruct((2 * feat + 16, wide), BF),
        ],
        "qkv_grads",
        scratch=[pltpu.VMEM((width, wide), F32)],
    )


def spread_kernel(meta, *refs, n):
    pieces, outs = refs[:n], refs[n:]
    hw = pieces[0].shape[1] // 3
    values = [ref[...].astype(F32) for ref in pieces]
    for j in range(n):
        away = meta[3] - j
        away = jnp.where(away < 0, away + n, away)
        value = values[0]
        for k in range(1, n):
            value = jnp.where(away == k, values[k], value)
        for i, out in enumerate(outs):
            out[:, j * hw : (j + 1) * hw] = value[:, i * hw : (i + 1) * hw]


def spread(meta, pieces):
    sub, wide = pieces[0].shape
    width = wide // 3 * len(pieces)
    return meta_call(
        functools.partial(spread_kernel, n=len(pieces)),
        [meta, *pieces],
        [jax.ShapeDtypeStruct((sub, width), F32)] * 3,
        "spread",
    )


CORE = [(0, 1), (1, 0), (2, 3), (3, 2)]
CROSS = [(0, 2), (2, 0), (1, 3), (3, 1)]


def core_swap(x):
    return lax.ppermute(x, "row", CORE)


def cross_swap(x):
    return lax.ppermute(x, "row", CROSS)


def shift_col(x, step):
    n = lax.axis_size("col")
    return lax.ppermute(x, "col", [(i, (i + step) % n) for i in range(n)])


def after(x, *others):
    return lax.optimization_barrier((x,) + others)[0]


def natural_row(blocks):
    r = lax.axis_index("row")
    low = (r & 1) == 0
    b0, b1, b2, b3 = blocks
    left = jnp.where(low, jnp.stack([b0, b1]), jnp.stack([b1, b0]))
    right = jnp.where(low, jnp.stack([b2, b3]), jnp.stack([b3, b2]))
    return jnp.where(r < 2, jnp.concatenate([left, right]), jnp.concatenate([right, left]))


def gather_row_rel(x):
    far = cross_swap(x)
    near = core_swap(x)
    return [x, near, far, core_swap(far)]


def sum_dp(x):
    n = lax.axis_size("dp")
    if n == 2:
        return x + lax.ppermute(x, "dp", [(0, 1), (1, 0)])
    return lax.psum(x, "dp")


def split3(x):
    hi = lax.reduce_precision(x, 8, 7)
    mid = lax.reduce_precision(x - hi, 8, 7)
    low = x - hi - mid
    return hi.astype(BF), mid.astype(BF), low.astype(BF)


def per_device(
    tokens,
    cotangent,
    lengths,
    query_weight,
    key_weight,
    value_weight,
    query_bias,
    value_bias,
    out_weight,
    out_bias,
    norm1_gain,
    norm1_shift,
    up_weight,
    up_bias,
    down_weight,
    down_bias,
    norm2_gain,
    norm2_shift,
):
    rows_n = lax.axis_size("row")
    cols_n = lax.axis_size("col")
    r = lax.axis_index("row")
    z = lax.axis_index("col")
    local, width = tokens.shape
    block_len = local * cols_n
    hw = width // cols_n
    heads = hw // HD
    feat = width // rows_n
    scale = 1.0 / math.sqrt(HD)
    meta = jnp.stack([lengths[0], r, z * (local * rows_n) + r * local, z]).astype(jnp.int32)

    sub_out = out_weight.shape[0]
    x_blocks = [jnp.concatenate([tokens, out_weight.astype(BF)])]
    x_blocks.append(shift_col(x_blocks[0], 1))

    up_t = up_weight.astype(BF).T
    units = up_t.shape[0] // rows_n
    up_t = up_t.reshape(rows_n, units, feat)
    pieces = [lax.dynamic_index_in_dim(up_t, r ^ k, 0, keepdims=False) for k in range(4)]
    up_blocks = [
        pieces[0],
        core_swap(pieces[1]),
        cross_swap(pieces[2]),
        lax.ppermute(pieces[3], "row", [(i, i ^ 3) for i in range(rows_n)]),
    ]

    qkv = jnp.stack([query_weight, key_weight, value_weight], axis=1).astype(BF)
    sub = qkv.shape[0]
    qkv = qkv.reshape(sub, 3, cols_n, hw).transpose(2, 0, 1, 3).reshape(cols_n, sub, 3 * hw)
    pieces = []
    for k in range(cols_n):
        piece = lax.dynamic_index_in_dim(qkv, (z + k) % cols_n, 0, keepdims=False)
        pieces.append(shift_col(piece, k) if k else piece)
    w_blocks = gather_row_rel(after(jnp.concatenate(pieces), *up_blocks))
    for _ in range(2, cols_n):
        x_blocks.append(shift_col(x_blocks[-1], 1))

    up_t = natural_row(up_blocks).transpose(1, 0, 2).reshape(units, width)
    bias_mine = lax.dynamic_slice_in_dim(up_bias, r * units, units, 0)
    bias_rows = jnp.pad(jnp.stack(split3(bias_mine)), ((0, 13), (0, width - units)))
    pack = jnp.concatenate([up_t, down_weight.astype(BF), bias_rows])
    packs = [pack, shift_col(after(pack, x_blocks[-1]), 1)]

    qkv_bias = jnp.concatenate([query_bias, jnp.zeros_like(value_bias), value_bias])
    qkv_bias = jnp.broadcast_to(qkv_bias[None], (8, 3 * hw))
    vecs = jnp.stack([out_bias, norm1_gain, norm1_shift, down_bias, norm2_gain, norm2_shift])
    vecs = jnp.pad(jnp.stack(split3(vecs)), ((0, 1), (0, 2), (0, width - feat))).reshape(32, width)
    q_rows, kv, w_qkv, out_pack = project_qkv(meta, x_blocks, w_blocks, qkv_bias, vecs, local, scale)
    kv_own, kv_far, kv_near = kv, cross_swap(kv), core_swap(kv)
    sizes = (rows_n, cols_n)
    acc, stat, k_near, v_near = attn_fwd(meta, q_rows, (kv_own, kv_near), (0, 1), heads, local, sizes)
    stat = after(stat, packs[1])
    state = (acc, stat)
    packs.append(shift_col(after(packs[1], stat), 1))
    kv_far = after(kv_far, stat)
    kv_diag = core_swap(kv_far)
    *mixed_part, qb_rows, k_far, v_far = attn_fwd(
        meta, q_rows, (kv_far, kv_diag), (2, 3), heads, local, sizes, state=state
    )
    mixed_part[1] = after(mixed_part[1], packs[2])
    mixed = [mixed_part[0]] + [shift_col(mixed_part[k], -k) for k in range(1, cols_n)]
    packs.append(shift_col(after(packs[2], *mixed), 1))

    out_pack = after(out_pack, stat)
    out_far, out_near = cross_swap(out_pack), core_swap(out_pack)
    out_far = after(out_far, qb_rows)
    out_packs = [out_pack, out_near, out_far, core_swap(out_far)]
    hidden, hidden_low, normal1, inv1, out_full, vecs = project(meta, mixed, out_packs, tokens, sub_out)

    up_bias_r = [
        jnp.sum(p[2 * units : 2 * units + 3, :units].astype(F32), axis=0) for p in packs
    ]
    up_bias_r = jnp.concatenate(up_bias_r)[None]
    h_own, h_far, h_near = hidden_low, cross_swap(hidden_low), core_swap(hidden_low)
    keep0, send0, act0, slope0 = ffn_fwd(h_own, h_near, packs, up_bias_r, units)
    h_far = after(h_far, send0)
    h_diag = core_swap(h_far)
    keep1, send1, act1, slope1 = ffn_fwd(h_far, h_diag, packs, up_bias_r, units)
    far = (keep1 + core_swap(send1).astype(F32)).astype(BF)
    got_far = cross_swap(far)
    got_near = core_swap(send0)
    output, grad_resid2, grad_branch, sums2 = norm2(
        meta, hidden, keep0, got_near, got_far, cotangent, vecs
    )

    g_own, g_far, g_near = grad_branch, cross_swap(grad_branch), core_swap(grad_branch)
    keep0, send0, pre0 = ffn_bwd(g_own, g_near, packs, slope0, units)
    g_far = after(g_far, send0)
    g_diag = core_swap(g_far)
    keep1, send1, pre1 = ffn_bwd(g_far, g_diag, packs, slope1, units)
    far = (keep1 + core_swap(send1).astype(F32)).astype(BF)
    got_far = cross_swap(far)
    got_near = core_swap(send0)
    chunks, g_up_bias = ffn_grads(
        (act0, act1),
        (pre0, pre1),
        (h_own, h_near, h_far, h_diag),
        (g_own, g_near, g_far, g_diag),
        units,
        cols_n,
    )
    keep0 = after(keep0, *chunks)
    grad_resid1, grad_attended, sums1, grad_mixed = norm1_back(
        keep0, got_near, got_far, grad_resid2, normal1, inv1, vecs, out_full
    )
    grad_mixed = [grad_mixed[0]] + [shift_col(grad_mixed[k], k) for k in range(1, cols_n)]

    out_keep, out_far, out_send, sums = out_grads(
        meta, mixed, grad_attended, sums1, sums2, g_up_bias, sub_out, rows_n
    )
    out_got = core_swap(out_send)
    out_got_far = cross_swap(far_message(out_far, sums, out_got))
    messages = col_messages(chunks, out_keep, sums, out_got, out_got_far, sub_out)

    grad_mixed[0] = after(grad_mixed[0], messages[0])
    grads = grad_rows(mixed_part, grad_mixed, heads)
    received = [shift_col(after(messages[k], grads), -k) for k in range(1, cols_n)]
    part3, dq = attn_bwd(qb_rows, grads, k_far, v_far, 1, heads, scale, BF)
    got3 = core_swap(part3)
    part2, dq = attn_bwd(qb_rows, grads, k_far, v_far, 0, heads, scale, F32, dq=dq)
    far_got = cross_swap((part2 + got3.astype(F32)).astype(BF))
    part1, dq = attn_bwd(qb_rows, grads, k_near, v_near, 1, heads, scale, BF, dq=dq)
    got1 = core_swap(part1)
    dq = after(dq, received[0], received[2])
    part0, grad_q = attn_bwd(
        qb_rows, grads, k_near, v_near, 0, heads, scale, F32, dq=dq, last=True
    )

    d_blocks, back = join_grads(part0, got1, far_got, grad_q, w_qkv, cols_n)
    total = back[1]
    ring = []
    for step in range(2, cols_n + 1):
        ring.append(shift_col(total.astype(BF), 1))
        total = back[step % cols_n] + ring[-1].astype(F32)
    grad_tokens = grad_resid1 + total

    mine = sum_messages([after(messages[0], back[1])] + received)
    if lax.axis_size("dp") == 2:
        other = lax.ppermute(mine, "dp", [(0, 1), (1, 0)])
    else:
        other = lax.psum(mine.astype(F32), "dp") - mine.astype(F32)
    other = after(other, ring[1])
    *g_up, g_down_weight, g_out_weight, sums = finish(meta, mine, other, rows_n, units, sub_out)
    g_up[1] = core_swap(g_up[1])
    g_up[2] = cross_swap(g_up[2])
    g_up[3] = lax.ppermute(g_up[3], "row", [(i, i ^ 3) for i in range(rows_n)])
    g_up_weight = up_grads(meta, g_up)
    vec_out = lax.dynamic_slice_in_dim(sums[:6], r * feat, feat, 1)
    g_up_bias = lax.dynamic_index_in_dim(sums[8 : 8 + cols_n], z, 0, keepdims=False)

    own, far, send = qkv_grads(meta, x_blocks, d_blocks, feat)
    g_bias = own[feat] + own[feat + 1]

    def with_bias(block, bias):
        hi = lax.reduce_precision(bias, 8, 7)
        rows = jnp.pad(jnp.stack([hi, bias - hi]), ((0, 14), (0, 0)))
        return jnp.concatenate([block, rows]).astype(BF)

    def bias_of(got):
        return got[-16].astype(F32) + got[-15].astype(F32)

    got = core_swap(send)
    g_bias = g_bias + bias_of(got)
    mine = own[:feat] + got[:feat].astype(F32)
    got = cross_swap(with_bias(far + got[feat : 2 * feat].astype(F32), g_bias))
    g_bias = g_bias + bias_of(got)
    mine = mine + got[:feat].astype(F32)
    if lax.axis_size("dp") == 2:
        got = lax.ppermute(after(with_bias(mine, g_bias), ring[0]), "dp", [(0, 1), (1, 0)])
        g_bias = g_bias + bias_of(got)
        g_qkv = mine + got[:feat].astype(F32)
    else:
        g_bias, g_qkv = lax.psum((g_bias, mine), "dp")
    g_qkv = g_qkv.astype(BF).reshape(cols_n, sub, 3 * hw)
    pieces = []
    for k in range(cols_n):
        piece = lax.dynamic_index_in_dim(g_qkv, (z + k) % cols_n, 0, keepdims=False)
        pieces.append(shift_col(piece, k) if k else piece)
    g_qkv = spread(meta, pieces)
    return (
        output,
        grad_tokens,
        g_qkv[0],
        g_qkv[1],
        g_qkv[2],
        g_bias[:hw],
        g_bias[2 * hw :],
        g_out_weight,
        vec_out[2],
        vec_out[0],
        vec_out[1],
        g_up_weight,
        g_up_bias,
        g_down_weight,
        vec_out[5],
        vec_out[3],
        vec_out[4],
    )


def solution(mesh):
    token_spec = P(("dp", "col", "row"), None)
    placed = (
        token_spec,
        token_spec,
        P("dp"),
        P(("row", "col"), None),
        P(("row", "col"), None),
        P(("row", "col"), None),
        P("col"),
        P("col"),
        P(("col", "row"), None),
        P("row"),
        P("row"),
        P("row"),
        P("row", "col"),
        P("col"),
        P(("col", "row"), None),
        P("row"),
        P("row"),
        P("row"),
    )
    return jax.shard_map(
        per_device,
        mesh=mesh,
        in_specs=placed,
        out_specs=(token_spec, token_spec) + placed[3:],
        check_vma=False,
    )
```

```python
import functools
import math

import jax
import jax.numpy as jnp
from jax import lax
from jax.experimental import pallas as pl
from jax.experimental.pallas import tpu as pltpu
from jax.sharding import PartitionSpec as P

HD = 64
LANES = 256
EPS = 1e-05
BF = jnp.bfloat16
F32 = jnp.float32
VMEM_BYTES = 60 * 1024 * 1024
TURNED = HD + 16
SMALL_BYTES = 24 * 1024 * 1024
ATTN_BYTES = 36 * 1024 * 1024
ATTN_COST = 4
C4 = 6


def nn(a, b):
    return jnp.dot(a, b, preferred_element_type=F32)


def tn(a, b):
    return lax.dot_general(a, b, (((0,), (0,)), ((), ())), preferred_element_type=F32)


def nt(a, b):
    return lax.dot_general(a, b, (((1,), (1,)), ((), ())), preferred_element_type=F32)


def cost(us):
    return pl.CostEstimate(flops=int(us * 0.6e9), bytes_accessed=1000, transcendentals=0)


def head_lanes(shape, head, width):
    lane = lax.broadcasted_iota(jnp.int32, shape, 1)
    mine = (lane >= head * HD) & (lane < (head + 1) * HD)
    return mine | (lane == width) | ((lane >= width + 1 + 3 * head) & (lane < width + 4 + 3 * head))


def three_parts(x):
    hi = x.astype(BF).astype(F32)
    mid = (x - hi).astype(BF).astype(F32)
    return hi, mid, x - hi - mid


def tail_rows(parts, ones, n):
    row = lax.broadcasted_iota(jnp.int32, (n, parts[0].shape[1]), 0)
    out = jnp.where(row == 0, ones, 0.0)
    for head, value in enumerate(parts):
        for i, piece in enumerate(three_parts(value)):
            out = jnp.where(row == 1 + 3 * head + i, piece, out)
    return out


def widen_keys(kv, owner, meta, keys_out, values_out, turned, at, width, shift, sizes):
    n = kv.shape[0]
    rows_n, cols_n = sizes
    keys_out[at : at + n, :width] = kv[:, :width]
    values_out[at : at + n, :width] = kv[:, width:]
    shape = (n, LANES - width)
    t = lax.broadcasted_iota(jnp.int32, shape, 0)
    lane = lax.broadcasted_iota(jnp.int32, shape, 1)
    source = meta[3] - (t >> shift)
    source = jnp.where(source < 0, source + cols_n, source)
    position = ((source * rows_n + owner) << shift) + (t & ((1 << shift) - 1))
    mask = jnp.where(lane == 0, jnp.where(position >= meta[0], -1e30, 0.0), 1.0)
    keys_out[at : at + n, width:] = mask.astype(BF)
    values_out[at : at + n, width:] = jnp.ones(shape, BF)
    flat = values_out[at : at + n, :].T
    for head in range(width // HD):
        first = head * TURNED
        turned[first : first + HD, at : at + n] = flat[head * HD : (head + 1) * HD, :]
        turned[first + HD : first + TURNED, at : at + n] = jnp.ones((TURNED - HD, n), BF)


def attn_fwd_kernel(*refs, heads, first, pair, shift, sizes, chunk, blocks):
    if first:
        meta, q_ref, kv0, kv1, acc_out, stat_out, k_out, v_out, turned, stat = refs
    else:
        meta, q_ref, kv0, kv1, acc_in, stat_in = refs[:6]
        outs = refs[6 : 6 + blocks]
        qb_ref, k_out, v_out, turned, stat = refs[6 + blocks :]
    width = heads * HD
    half = kv0.shape[0]
    keys = 2 * half
    for i, ref in enumerate((kv0, kv1)):
        widen_keys(
            ref[...], meta[1] ^ pair[i], meta, k_out, v_out, turned, i * half, width, shift, sizes
        )
    q = q_ref[...]
    rows = q.shape[0]
    slot = lax.broadcasted_iota(jnp.int32, (16, rows), 0)
    stat[...] = jnp.zeros_like(stat)

    def one(head, carry):
        qh = jnp.where(head_lanes(q.shape, head, width), q, jnp.zeros_like(q))
        scores = [nt(k_out[i : i + chunk, :], qh) for i in range(0, keys, chunk)]
        peak = functools.reduce(
            jnp.maximum, [jnp.max(s, axis=0, keepdims=True) for s in scores]
        )
        if not first:
            old = jnp.max(jnp.where(slot == head, stat_in[...], -3e38), axis=0, keepdims=True)
            count = jnp.sum(jnp.where(slot == head + 8, stat_in[...], 0.0), axis=0, keepdims=True)
            peak = jnp.maximum(peak, old)
        acc = None
        for i, s in enumerate(scores):
            p = jnp.exp(s - peak).astype(BF)
            at = pl.ds(pl.multiple_of(head * TURNED, 16), TURNED)
            part = nn(turned[at, i * chunk : (i + 1) * chunk], p)
            acc = part if acc is None else acc + part
        total = acc[HD : HD + 1]
        mine = pl.ds(pl.multiple_of(head * HD, HD), HD)
        if first:
            acc_out[mine, :] = acc[:HD]
            new = jnp.where(slot == head, peak, stat[...])
            stat[...] = jnp.where(slot == head + 8, total, new)
        else:
            keep = jnp.exp(old - peak)
            total = total + count * keep
            out = ((acc[:HD] + acc_in[mine, :] * keep) * (1.0 / total)).astype(BF)
            each = rows // blocks
            for b in range(blocks):
                outs[b][mine, :] = out[:, b * each : (b + 1) * each]
            stat[...] = jnp.where(slot == head, -(peak + jnp.log(total)), stat[...])
        return carry

    lax.fori_loop(0, heads, one, 0)
    if first:
        stat_out[...] = stat[...]
    else:
        logs = [stat[head : head + 1, :] for head in range(heads)]
        qb_ref[:, :width] = q[:, :width]
        qb_ref[:, width:] = tail_rows(logs, 1.0, LANES - width).T.astype(BF)


def attn_fwd(meta, q, kv_pair, pair, heads, local, sizes, state=None, chunk=512):
    rows = q.shape[0]
    half, double = kv_pair[0].shape
    width = double // 2
    first = state is None
    blocks = rows // local
    vmem = pl.BlockSpec(memory_space=pltpu.VMEM)
    args = [meta, q, *kv_pair]
    if first:
        out_shape = [jax.ShapeDtypeStruct((width, rows), F32), jax.ShapeDtypeStruct((16, rows), F32)]
    else:
        args += list(state)
        out_shape = [jax.ShapeDtypeStruct((width, local), BF)] * blocks
        out_shape += [jax.ShapeDtypeStruct((rows, LANES), BF)]
    out_shape += [jax.ShapeDtypeStruct((2 * half, LANES), BF)] * 2
    return pl.pallas_call(
        functools.partial(
            attn_fwd_kernel,
            heads=heads,
            first=first,
            pair=pair,
            shift=local.bit_length() - 1,
            sizes=sizes,
            chunk=chunk,
            blocks=blocks,
        ),
        in_specs=[pl.BlockSpec(memory_space=pltpu.SMEM)] + [vmem] * (len(args) - 1),
        out_specs=[vmem] * len(out_shape),
        out_shape=out_shape,
        scratch_shapes=[pltpu.VMEM((heads * TURNED, 2 * half), BF), pltpu.VMEM((16, rows), F32)],
        compiler_params=pltpu.CompilerParams(vmem_limit_bytes=ATTN_BYTES),
        cost_estimate=cost(ATTN_COST),
        name="attn_fwd_near" if first else "attn_fwd_far",
    )(*args)


def grad_rows_kernel(*refs, heads, blocks):
    outs, grads, wide = refs[:blocks], refs[blocks : 2 * blocks], refs[2 * blocks]
    width = heads * HD
    for b in range(blocks):
        g = grads[b][...].astype(F32)
        prod = g * outs[b][...].astype(F32)
        each = g.shape[1]
        parts = [
            -jnp.sum(prod[head * HD : (head + 1) * HD], axis=0, keepdims=True) for head in range(heads)
        ]
        tall = jnp.concatenate([g, tail_rows(parts, 0.0, LANES - width)], axis=0)
        wide[b * each : (b + 1) * each, :] = tall.T.astype(BF)


def grad_rows(outs, grads, heads):
    each = outs[0].shape[1]
    return small_call(
        functools.partial(grad_rows_kernel, heads=heads, blocks=len(outs)),
        jax.ShapeDtypeStruct((each * len(outs), LANES), BF),
        "grad_rows",
    )(*outs, *grads)


def attn_bwd_kernel(*refs, heads, first, last, block, scale, pieces):
    q_ref, g_ref, k_ref, v_ref, *refs = refs
    if not first:
        dq_in, *refs = refs
    outs, (dq_out, dk, dv, dq_acc) = refs[:pieces], refs[pieces:]
    width = heads * HD
    dk[...] = jnp.zeros_like(dk)
    dv[...] = jnp.zeros_like(dv)

    def step(i, carry):
        at = pl.ds(pl.multiple_of((i // heads) * block, block), block)
        mine = head_lanes((block, LANES), i % heads, width)
        q_all = q_ref[at, :]
        g_all = g_ref[at, :]
        k = k_ref[...]
        q = jnp.where(mine, q_all, jnp.zeros_like(q_all))
        g = jnp.where(mine, g_all, jnp.zeros_like(g_all))
        p = jnp.exp(nt(k, q))
        ds = (p * nt(v_ref[...], g)).astype(BF)
        dv[...] += nn(p.astype(BF), g)
        dk[...] += nn(ds, q)
        dq_acc[at, :] = jnp.where(mine, tn(ds, k), dq_acc[at, :])
        return carry

    lax.fori_loop(0, q_ref.shape[0] // block * heads, step, 0)
    dq = dq_acc[:, :width]
    if not first:
        dq = dq + dq_in[...]
    dq_out[...] = (dq * scale).astype(dq_out.dtype) if last else dq
    each = outs[0].shape[0]
    for i, out in enumerate(outs):
        at = slice(i * each, (i + 1) * each)
        out[:, :width] = dk[at, :width].astype(out.dtype)
        out[:, width:] = dv[at, :width].astype(out.dtype)


def attn_bwd(q, g, k, v, at, heads, scale, kind, us, dq=None, last=False, pieces=1, block=512):
    rows = q.shape[0]
    half = k.shape[0] // 2
    width = heads * HD
    first = dq is None

    def whole(shape):
        return pl.BlockSpec(shape, lambda i: (0,) * len(shape))

    part = pl.BlockSpec((half, LANES), lambda i: (at, 0))
    args = [q, g, k, v] + ([] if first else [dq])
    specs = [whole(q.shape), whole(g.shape), part, part] + ([] if first else [whole(dq.shape)])
    return pl.pallas_call(
        functools.partial(
            attn_bwd_kernel,
            heads=heads,
            first=first,
            last=last,
            block=block,
            scale=scale,
            pieces=pieces,
        ),
        grid=(1,),
        in_specs=specs,
        out_specs=[whole((half // pieces, 2 * width))] * pieces + [whole((rows, width))],
        out_shape=[jax.ShapeDtypeStruct((half // pieces, 2 * width), kind)] * pieces
        + [
            jax.ShapeDtypeStruct((rows, width), BF if last else F32),
        ],
        scratch_shapes=[pltpu.VMEM((half, LANES), F32)] * 2 + [pltpu.VMEM((rows, LANES), F32)],
        compiler_params=pltpu.CompilerParams(vmem_limit_bytes=ATTN_BYTES),
        cost_estimate=cost(us),
        name="attn_bwd_%d" % at,
    )(*args)


def small_call(kernel, out_shape, name, scratch=(), us=1.4):
    return pl.pallas_call(
        kernel,
        out_shape=out_shape,
        scratch_shapes=scratch,
        compiler_params=pltpu.CompilerParams(vmem_limit_bytes=SMALL_BYTES),
        cost_estimate=cost(us),
        name=name,
    )


def meta_call(kernel, args, out_shape, name, scratch=(), us=1.2):
    vmem = pl.BlockSpec(memory_space=pltpu.VMEM)
    return pl.pallas_call(
        kernel,
        in_specs=[pl.BlockSpec(memory_space=pltpu.SMEM)] + [vmem] * (len(args) - 1),
        out_specs=[vmem] * len(out_shape),
        out_shape=out_shape,
        scratch_shapes=scratch,
        compiler_params=pltpu.CompilerParams(vmem_limit_bytes=SMALL_BYTES),
        cost_estimate=cost(us),
        name=name,
    )(*args)


def row_mean(x):
    return jnp.mean(x, axis=1, keepdims=True)


def col_sum(x):
    return jnp.sum(x, axis=0, keepdims=True)


def norm_forward(resid, gain, shift):
    centered = resid - row_mean(resid)
    inv = lax.rsqrt(row_mean(centered * centered) + EPS)
    normal = centered * inv
    return normal * gain + shift, normal, inv


def norm_backward(grad_out, normal, inv, gain):
    scaled = grad_out * gain
    return inv * (scaled - row_mean(scaled) - normal * row_mean(scaled * normal))


def project_qkv_kernel(meta, *refs, n, rows_n, feat, hw, scale):
    x = refs[:n]
    ws, bias_ref, vec_ref, q_ref, kv_ref, w_out, pack_ref, w_all = refs[n : n + rows_n], *refs[n + rows_n :]
    each = feat // n
    for k in range(rows_n):
        for m in range(n):
            source = meta[3] - m
            source = jnp.where(source < 0, source + n, source)
            at = pl.multiple_of((meta[1] ^ k) * feat + source * each, each)
            w_all[pl.ds(at, each), :] = ws[k][m * each : (m + 1) * each, :]
    w = w_all[...]
    w_out[...] = w.T
    each = q_ref.shape[0] // n
    for k in range(n):
        at = slice(k * each, (k + 1) * each)
        out = nn(x[k][:each, :], w) + bias_ref[0:1, :]
        q_ref[at, :hw] = (out[:, :hw].astype(BF).astype(F32) * scale).astype(BF)
        lane = lax.broadcasted_iota(jnp.int32, (each, LANES - hw), 1)
        q_ref[at, hw:] = jnp.where(lane == 0, 1.0, 0.0).astype(BF)
        kv_ref[at, :] = out[:, hw:].astype(BF)
        more = x[k].shape[0] - each
        pack_ref[k * more : (k + 1) * more, :] = x[k][each:, :]
    pack_ref[n * more :, :] = vec_ref[...]


def project_qkv(meta, x, ws, bias, vecs, local, scale):
    feat, wide = ws[0].shape
    hw = wide // 3
    rows = local * len(x)
    return meta_call(
        functools.partial(
            project_qkv_kernel, n=len(x), rows_n=len(ws), feat=feat, hw=hw, scale=scale
        ),
        [meta, *x, *ws, bias, vecs],
        [
            jax.ShapeDtypeStruct((rows, LANES), BF),
            jax.ShapeDtypeStruct((rows, 2 * hw), BF),
            jax.ShapeDtypeStruct((wide, feat * len(ws)), BF),
            jax.ShapeDtypeStruct(((x[0].shape[0] - local) * len(x) + vecs.shape[0], vecs.shape[1]), BF),
        ],
        "project_qkv",
        scratch=[pltpu.VMEM((feat * len(ws), wide), BF)],
    )


def project_kernel(meta, *refs, n, rows_n, sub, feat):
    mixed, packs = refs[:n], refs[n : n + rows_n]
    x_ref, hid_ref, low_ref, normal_ref, inv_ref, w_ref, vec_ref = refs[n + rows_n :]
    r = meta[1]
    for k in range(rows_n):
        at = pl.multiple_of((r ^ k) * sub, sub)
        for i in range(n):
            w_ref[i, pl.ds(at, sub), :] = packs[k][((n - i) % n) * sub : ((n - i) % n + 1) * sub, :]
    values = []
    for k in range(rows_n):
        part = packs[k][n * sub : n * sub + 32, :feat].astype(F32)
        values.append(part[0:8] + part[8:16] + part[16:24])
    pieces = []
    for owner in range(rows_n):
        value = values[0]
        for k in range(1, rows_n):
            value = jnp.where((r ^ k) == owner, values[k], value)
        pieces.append(value)
    vecs = jnp.concatenate(pieces, axis=1)
    vec_ref[...] = vecs
    total = x_ref[...].astype(F32) + vecs[0:1, :]
    for j in range(n):
        total = total + tn(mixed[j][...], w_ref[j])
    hidden, normal, inv = norm_forward(total, vecs[1:2, :], vecs[2:3, :])
    hid_ref[...] = hidden
    low_ref[...] = hidden.astype(BF)
    normal_ref[...] = normal
    inv_ref[...] = jnp.broadcast_to(inv, inv_ref.shape)


def project(meta, mixed, packs, x, sub):
    rows, width = x.shape
    feat = width // len(packs)
    return meta_call(
        functools.partial(
            project_kernel, n=len(mixed), rows_n=len(packs), sub=sub, feat=feat
        ),
        [meta, *mixed, *packs, x],
        [
            jax.ShapeDtypeStruct((rows, width), F32),
            jax.ShapeDtypeStruct((rows, width), BF),
            jax.ShapeDtypeStruct((rows, width), F32),
            jax.ShapeDtypeStruct((rows, 128), F32),
            jax.ShapeDtypeStruct((len(mixed), sub * len(packs), width), BF),
            jax.ShapeDtypeStruct((8, width), F32),
        ],
        "project_norm1",
    )


def stack_refs(refs, at, n):
    return jnp.concatenate([ref[at : at + n, :] for ref in refs], axis=0)


def ffn_fwd_kernel(*refs, n, units):
    h0, h1 = refs[:2]
    packs = refs[2 : 2 + n]
    bias_ref, keep_ref, send_ref, act_ref, slope_ref = refs[2 + n :]
    rows = h0.shape[0]
    h = jnp.concatenate([h0[...], h1[...]], axis=0)
    x = nt(h, stack_refs(packs, 0, units)) + bias_ref[...]
    cdf = 0.5 * (1.0 + lax.erf(x * math.sqrt(0.5)))
    act = (x * cdf).astype(BF)
    act_ref[...] = act
    slope = cdf + x * (math.sqrt(0.5 / math.pi) * jnp.exp(-0.5 * x * x))
    slope_ref[...] = slope.astype(BF)
    out = nn(act, stack_refs(packs, units, units))
    keep_ref[...] = out[:rows]
    send_ref[...] = out[rows:].astype(BF)


def ffn_fwd(h0, h1, packs, bias, units):
    rows, width = h0.shape
    wide = units * len(packs)
    return small_call(
        functools.partial(ffn_fwd_kernel, n=len(packs), units=units),
        [
            jax.ShapeDtypeStruct((rows, width), F32),
            jax.ShapeDtypeStruct((rows, width), BF),
            jax.ShapeDtypeStruct((2 * rows, wide), BF),
            jax.ShapeDtypeStruct((2 * rows, wide), BF),
        ],
        "ffn_fwd",
    )(h0, h1, *packs, bias)


def ffn_bwd_kernel(*refs, n, units):
    g0, g1 = refs[:2]
    packs = refs[2 : 2 + n]
    slope_ref, keep_ref, send_ref, pre_ref = refs[2 + n :]
    rows = g0.shape[0]
    g = jnp.concatenate([g0[...], g1[...]], axis=0)
    pre = (nt(g, stack_refs(packs, units, units)) * slope_ref[...].astype(F32)).astype(BF)
    pre_ref[...] = pre
    out = nn(pre, stack_refs(packs, 0, units))
    keep_ref[...] = out[:rows]
    send_ref[...] = out[rows:].astype(BF)


def ffn_bwd(g0, g1, packs, slope, units):
    rows, width = g0.shape
    wide = units * len(packs)
    return small_call(
        functools.partial(ffn_bwd_kernel, n=len(packs), units=units),
        [
            jax.ShapeDtypeStruct((rows, width), F32),
            jax.ShapeDtypeStruct((rows, width), BF),
            jax.ShapeDtypeStruct((2 * rows, wide), BF),
        ],
        "ffn_bwd",
    )(g0, g1, *packs, slope)


def ffn_grads_kernel(meta, *refs):
    act0, act1, pre0, pre1 = refs[:4]
    h = jnp.concatenate([ref[...] for ref in refs[4:8]], axis=0)
    g = jnp.concatenate([ref[...] for ref in refs[8:12]], axis=0)
    keep_ref, send_ref, bias_ref = refs[12:]
    pre = jnp.concatenate([pre0[...], pre1[...]], axis=0)
    act = jnp.concatenate([act0[...], act1[...]], axis=0)
    g_up = tn(pre, h).astype(BF)
    g_down = tn(act, g).astype(BF)
    first = meta[4] == 0

    @pl.when(first)
    def _():
        keep_ref[...] = g_up
        send_ref[...] = g_down

    @pl.when(jnp.logical_not(first))
    def _():
        keep_ref[...] = g_down
        send_ref[...] = g_up

    bias_ref[...] = jnp.broadcast_to(col_sum(pre.astype(F32)), bias_ref.shape)


def ffn_grads(meta, acts, pres, hiddens, grads):
    width = hiddens[0].shape[1]
    wide = acts[0].shape[1]
    return meta_call(
        ffn_grads_kernel,
        [meta, *acts, *pres, *hiddens, *grads],
        [
            jax.ShapeDtypeStruct((wide, width), BF),
            jax.ShapeDtypeStruct((wide, width), BF),
            jax.ShapeDtypeStruct((8, wide), F32),
        ],
        "ffn_grads",
    )


def norm2_kernel(
    meta, hid_ref, keep_ref, near_ref, far_ref, cot_ref, vec_ref, out_ref, grad_ref, low_ref, sum_ref
):
    branch = keep_ref[...] + near_ref[...].astype(F32) + far_ref[...].astype(F32) + vec_ref[3:4, :]
    gain = vec_ref[4:5, :]
    normed, normal, inv = norm_forward(hid_ref[...] + branch, gain, vec_ref[5:6, :])
    row = lax.broadcasted_iota(jnp.int32, (out_ref.shape[0], 1), 0)
    valid = (meta[2] + row < meta[0]).astype(F32)
    out_ref[...] = (normed * valid).astype(BF)
    grad_y = cot_ref[...].astype(F32) * valid
    grad = norm_backward(grad_y, normal, inv, gain)
    grad_ref[...] = grad
    low = grad.astype(BF)
    low_ref[...] = low
    sum_ref[...] = jnp.zeros_like(sum_ref)
    sum_ref[0:1, :] = col_sum(grad_y * normal)
    sum_ref[1:2, :] = col_sum(grad_y)
    sum_ref[2:3, :] = col_sum(low.astype(F32))


def norm2(meta, hidden, keep, near, far, cot, vecs):
    rows, width = hidden.shape
    shapes = [
        jax.ShapeDtypeStruct((rows, width), BF),
        jax.ShapeDtypeStruct((rows, width), F32),
        jax.ShapeDtypeStruct((rows, width), BF),
        jax.ShapeDtypeStruct((8, width), F32),
    ]
    return meta_call(norm2_kernel, [meta, hidden, keep, near, far, cot, vecs], shapes, "norm2_both")


def norm1_back_kernel(
    keep_ref, near_ref, far_ref, add_ref, normal_ref, inv_ref, vec_ref, w_ref, out_ref, low_ref, sum_ref, *mixed
):
    grad = keep_ref[...] + near_ref[...].astype(F32) + far_ref[...].astype(F32) + add_ref[...]
    normal = normal_ref[...]
    resid = norm_backward(grad, normal, inv_ref[:, 0:1], vec_ref[1:2, :])
    out_ref[...] = resid
    low = resid.astype(BF)
    low_ref[...] = low
    for j, ref in enumerate(mixed):
        ref[...] = nt(w_ref[j], low).astype(BF)
    sum_ref[...] = jnp.zeros_like(sum_ref)
    sum_ref[0:1, :] = col_sum(grad * normal)
    sum_ref[1:2, :] = col_sum(grad)
    sum_ref[2:3, :] = col_sum(low.astype(F32))


def norm1_back(keep, near, far, add, normal, inv, vecs, w):
    rows, width = add.shape
    out = small_call(
        norm1_back_kernel,
        [
            jax.ShapeDtypeStruct((rows, width), F32),
            jax.ShapeDtypeStruct((rows, width), BF),
            jax.ShapeDtypeStruct((8, width), F32),
        ]
        + [jax.ShapeDtypeStruct((w.shape[1], rows), BF)] * w.shape[0],
        "norm1_back",
    )(keep, near, far, add, normal, inv, vecs, w)
    return out[0], out[1], out[2], out[3:]


def two_parts(x):
    hi = x.astype(BF).astype(F32)
    return jnp.concatenate([hi, x - hi], axis=0).astype(BF)


def both_parts(rows):
    n = rows.shape[0] // 2
    return rows[:n].astype(F32) + rows[n:].astype(F32)


def out_grads_kernel(meta, *refs, n, rows_n, sub):
    mixed, grad, s1, s2, bias = refs[:n], *refs[n : n + 4]
    keep, far, send, sums, total = refs[n + 4 :]
    g = grad[...]
    for j in range(n):
        total[j] = nn(mixed[j][...], g)
    count = n * sub
    for j in range(n):
        at = slice(j * sub, (j + 1) * sub)

        def rows(k):
            return total[j, pl.ds(pl.multiple_of((meta[1] ^ k) * sub, sub), sub), :]

        keep[at, :] = rows(0)
        far[at, :] = rows(2)
        send[at, :] = rows(1).astype(BF)
        send[count + j * sub : count + (j + 1) * sub, :] = rows(3).astype(BF)
    sums[...] = jnp.zeros_like(sums)
    sums[0:3, :] = s1[0:3, :]
    sums[3:6, :] = s2[0:3, :]
    units = bias.shape[1] // n
    for j in range(n):
        away = meta[3] - j
        away = jnp.where(away < 0, away + n, away)
        value = bias[0:1, :units]
        for k in range(1, n):
            value = jnp.where(away == k, bias[0:1, k * units : (k + 1) * units], value)
        zero = jnp.zeros_like(value)
        row = [jnp.where(meta[1] == owner, value, zero) for owner in range(rows_n)]
        sums[8 + j : 9 + j, :] = jnp.concatenate(row, axis=1)
    send[2 * count :, :] = two_parts(sums[...])


def out_grads(meta, mixed, grad, s1, s2, bias, sub, rows_n):
    n, heads, width = len(mixed), mixed[0].shape[0], grad.shape[1]
    shapes = [
        jax.ShapeDtypeStruct((n * sub, width), F32),
        jax.ShapeDtypeStruct((n * sub, width), F32),
        jax.ShapeDtypeStruct((2 * n * sub + 32, width), BF),
        jax.ShapeDtypeStruct((16, width), F32),
    ]
    return meta_call(
        functools.partial(out_grads_kernel, n=n, sub=sub, rows_n=rows_n),
        [meta, *mixed, grad, s1, s2, bias],
        shapes,
        "out_grads",
        scratch=[pltpu.VMEM((n, heads, width), F32)],
    )


def far_message_kernel(far, sums, got, out):
    n = far.shape[0]
    out[:n, :] = (far[...] + got[n : 2 * n, :].astype(F32)).astype(BF)
    out[n:, :] = two_parts(sums[...] + both_parts(got[2 * n :, :]))


def far_message(far, sums, got):
    n, width = far.shape
    shape = jax.ShapeDtypeStruct((n + 32, width), BF)
    return small_call(far_message_kernel, shape, "far_message", us=0.7)(far, sums, got)


def col_messages_kernel(*refs, n, sub, added):
    (one, two, keep, sums, near, far), outs = refs[:6], refs[6:]
    count = n * sub
    both = sums[...] + both_parts(near[2 * count :, :]) + both_parts(far[count:, :])
    parts = two_parts(both)
    own = keep[...] + near[:count, :].astype(F32) + far[:count, :].astype(F32)
    units = one.shape[0] // n
    size = units if added else 2 * units
    for k in range(n):
        j = (n - k) % n
        at = slice(k * units, (k + 1) * units)
        if added:
            outs[k][:units, :] = (one[at, :].astype(F32) + two[at, :].astype(F32)).astype(BF)
        else:
            outs[k][:units, :] = one[at, :]
            outs[k][units:size, :] = two[at, :]
        outs[k][size : size + sub, :] = own[j * sub : (j + 1) * sub].astype(BF)
        outs[k][size + sub :, :] = parts


def col_messages(one, two, keep, sums, near, far, sub, n, added):
    rows, width = one.shape
    size = rows // n * (1 if added else 2)
    shapes = [jax.ShapeDtypeStruct((size + sub + 32, width), BF)] * n
    return small_call(
        functools.partial(col_messages_kernel, n=n, sub=sub, added=added), shapes, "col_messages"
    )(one, two, keep, sums, near, far)


def sum_messages_kernel(*refs):
    refs, out = refs[:-1], refs[-1]
    n = out.shape[0] - 32
    total = refs[0][:n, :].astype(F32)
    sums = both_parts(refs[0][n:, :])
    for ref in refs[1:]:
        total = total + ref[:n, :].astype(F32)
        sums = sums + both_parts(ref[n:, :])
    out[:n, :] = total.astype(BF)
    out[n:, :] = two_parts(sums)


def sum_messages(messages):
    shape = jax.ShapeDtypeStruct(messages[0].shape, BF)
    return small_call(sum_messages_kernel, shape, "sum_messages", us=0.7)(*messages)


def finish_kernel(meta, own, other, *refs, rows_n, units, sub, paired):
    ups, (down, out, sums) = refs[:rows_n], refs[rows_n:]
    size = own.shape[0] - sub - 32
    a = own[:size, :].astype(F32)
    b = other[:size, :].astype(F32)
    if paired:
        first = meta[4] == 0
        up = jnp.where(first, a, b)
        down[...] = jnp.where(first, b, a)
    else:
        up = a[:units] + b[:units]
        down[...] = a[units:] + b[units:]
    feat = up.shape[1] // rows_n
    pieces = [up[:, k * feat : (k + 1) * feat] for k in range(rows_n)]
    for k in range(rows_n):
        value = pieces[0]
        for owner in range(1, rows_n):
            value = jnp.where((meta[1] ^ k) == owner, pieces[owner], value)
        ups[k][...] = value.T.astype(BF)
    at = size + sub
    out[...] = own[size:at, :].astype(F32) + other[size:at, :].astype(F32)
    sums[...] = both_parts(own[at:, :]) + both_parts(other[at:, :])


def finish(meta, own, other, rows_n, units, sub, paired):
    width = own.shape[1]
    shapes = [jax.ShapeDtypeStruct((width // rows_n, units), BF)] * rows_n
    shapes += [jax.ShapeDtypeStruct((n, width), F32) for n in (units, sub, 16)]
    return meta_call(
        functools.partial(finish_kernel, rows_n=rows_n, units=units, sub=sub, paired=paired),
        [meta, own, other],
        shapes,
        "finish_grads",
    )


def up_grads_kernel(meta, *refs, n):
    pieces, out = refs[:n], refs[n]
    units = pieces[0].shape[1]
    values = [ref[...].astype(F32) for ref in pieces]
    for owner in range(n):
        value = values[0]
        for k in range(1, n):
            value = jnp.where((meta[1] ^ k) == owner, values[k], value)
        out[:, owner * units : (owner + 1) * units] = value


def up_grads(meta, pieces):
    feat, units = pieces[0].shape
    return meta_call(
        functools.partial(up_grads_kernel, n=len(pieces)),
        [meta, *pieces],
        [jax.ShapeDtypeStruct((feat, units * len(pieces)), F32)],
        "up_grads",
    )[0]


def join_kernel(keep, near0, near1, far, grad_q, w_ref, *outs):
    n = len(outs) // 2
    hw = grad_q.shape[1]
    each = outs[0].shape[0]
    for k in range(n):
        at = slice(k * each, (k + 1) * each)
        near = (near0, near1)[2 * k // n]
        inside = slice(at.start % near0.shape[0], at.start % near0.shape[0] + each)
        kv = (keep[at, :] + near[inside, :].astype(F32) + far[at, :].astype(F32)).astype(BF)
        d = jnp.concatenate([grad_q[at, :], kv], axis=1)
        outs[k][...] = d
        outs[n + k][...] = nn(d, w_ref[...]).astype(outs[n + k].dtype)


def join_grads(keep, near0, near1, far, grad_q, w, n):
    rows, hw = grad_q.shape
    width = w.shape[1]
    shapes = [jax.ShapeDtypeStruct((rows // n, 3 * hw), BF)] * n
    shapes += [jax.ShapeDtypeStruct((rows // n, width), BF if k == 1 else F32) for k in range(n)]
    out = small_call(join_kernel, shapes, "join_grads")(keep, near0, near1, far, grad_q, w)
    return out[:n], out[n:]


def qkv_grads_kernel(meta, *refs, n, feat):
    x, grads, keep, far, send, send_far, total = refs[:n], refs[n : 2 * n], *refs[2 * n :]
    each = grads[0].shape[0]
    rows_of_x = jnp.concatenate([ref[:each, :] for ref in x], axis=0)
    g = jnp.concatenate([ref[...] for ref in grads], axis=0)
    total[...] = tn(rows_of_x, g)

    def rows(k):
        return total[pl.ds(pl.multiple_of((meta[1] ^ k) * feat, feat), feat), :]

    bias = col_sum(g.astype(F32))
    hi = bias.astype(BF).astype(F32)
    row = lax.broadcasted_iota(jnp.int32, (16, bias.shape[1]), 0)
    tail = jnp.where(row == 0, hi, jnp.where(row == 1, bias - hi, 0.0))
    keep[:feat, :] = rows(0)
    keep[feat:, :] = tail
    far[...] = rows(2)
    send[:feat, :] = rows(1).astype(BF)
    send[feat:, :] = tail.astype(BF)
    send_far[...] = rows(3).astype(BF)


def qkv_grads(meta, x, grads, feat):
    wide = grads[0].shape[1]
    width = x[0].shape[1]
    return meta_call(
        functools.partial(qkv_grads_kernel, n=len(x), feat=feat),
        [meta, *x, *grads],
        [
            jax.ShapeDtypeStruct((feat + 16, wide), F32),
            jax.ShapeDtypeStruct((feat, wide), F32),
            jax.ShapeDtypeStruct((feat + 16, wide), BF),
            jax.ShapeDtypeStruct((feat, wide), BF),
        ],
        "qkv_grads",
        scratch=[pltpu.VMEM((width, wide), F32)],
    )


def spread_kernel(meta, *refs, n):
    pieces, outs = refs[:n], refs[n:]
    hw = pieces[0].shape[1] // 3
    values = [ref[...].astype(F32) for ref in pieces]
    for j in range(n):
        away = meta[3] - j
        away = jnp.where(away < 0, away + n, away)
        value = values[0]
        for k in range(1, n):
            value = jnp.where(away == k, values[k], value)
        for i, out in enumerate(outs):
            out[:, j * hw : (j + 1) * hw] = value[:, i * hw : (i + 1) * hw]


def spread(meta, pieces):
    sub, wide = pieces[0].shape
    width = wide // 3 * len(pieces)
    return meta_call(
        functools.partial(spread_kernel, n=len(pieces)),
        [meta, *pieces],
        [jax.ShapeDtypeStruct((sub, width), F32)] * 3,
        "spread",
    )


def pack_kernel(meta, *refs, n):
    blocks, (down, bias, out) = refs[:n], refs[n:]
    units, feat = blocks[0].shape
    values = [ref[...].astype(F32) for ref in blocks]
    for owner in range(n):
        value = values[0]
        for k in range(1, n):
            value = jnp.where((meta[1] ^ k) == owner, values[k], value)
        out[:units, owner * feat : (owner + 1) * feat] = value.astype(BF)
    out[units : 2 * units, :] = down[...].astype(BF)
    out[2 * units :, :] = bias[...]


def pack_weights(meta, blocks, down, bias):
    rows, width = down.shape
    return meta_call(
        functools.partial(pack_kernel, n=len(blocks)),
        [meta, *blocks, down, bias],
        [jax.ShapeDtypeStruct((2 * rows + bias.shape[0], width), BF)],
        "pack_weights",
    )[0]


CORE = [(0, 1), (1, 0), (2, 3), (3, 2)]
CROSS = [(0, 2), (2, 0), (1, 3), (3, 1)]


def core_swap(x):
    return lax.ppermute(x, "row", CORE)


def cross_swap(x):
    return lax.ppermute(x, "row", CROSS)


def shift_col(x, step):
    n = lax.axis_size("col")
    return lax.ppermute(x, "col", [(i, (i + step) % n) for i in range(n)])


def after(x, *others):
    return lax.optimization_barrier((x,) + others)[0]


def natural_row(blocks):
    r = lax.axis_index("row")
    low = (r & 1) == 0
    b0, b1, b2, b3 = blocks
    left = jnp.where(low, jnp.stack([b0, b1]), jnp.stack([b1, b0]))
    right = jnp.where(low, jnp.stack([b2, b3]), jnp.stack([b3, b2]))
    return jnp.where(r < 2, jnp.concatenate([left, right]), jnp.concatenate([right, left]))


def gather_row_rel(x):
    far = cross_swap(x)
    near = core_swap(x)
    return [x, near, far, core_swap(far)]


def sum_dp(x):
    n = lax.axis_size("dp")
    if n == 2:
        return x + lax.ppermute(x, "dp", [(0, 1), (1, 0)])
    return lax.psum(x, "dp")


def split3(x):
    hi = lax.reduce_precision(x, 8, 7)
    mid = lax.reduce_precision(x - hi, 8, 7)
    low = x - hi - mid
    return hi.astype(BF), mid.astype(BF), low.astype(BF)


def per_device(
    tokens,
    cotangent,
    lengths,
    query_weight,
    key_weight,
    value_weight,
    query_bias,
    value_bias,
    out_weight,
    out_bias,
    norm1_gain,
    norm1_shift,
    up_weight,
    up_bias,
    down_weight,
    down_bias,
    norm2_gain,
    norm2_shift,
):
    rows_n = lax.axis_size("row")
    cols_n = lax.axis_size("col")
    r = lax.axis_index("row")
    z = lax.axis_index("col")
    local, width = tokens.shape
    block_len = local * cols_n
    hw = width // cols_n
    heads = hw // HD
    feat = width // rows_n
    scale = 1.0 / math.sqrt(HD)
    paired = lax.axis_size("dp") == 2
    pair = lax.axis_index("dp") if paired else jnp.zeros((), jnp.int32)
    meta = jnp.stack([lengths[0], r, z * (local * rows_n) + r * local, z, pair]).astype(jnp.int32)

    sub_out = out_weight.shape[0]
    x_blocks = [jnp.concatenate([tokens, out_weight.astype(BF)])]
    x_blocks.append(shift_col(x_blocks[0], 1))

    up_t = up_weight.astype(BF).T
    units = up_t.shape[0] // rows_n
    up_t = up_t.reshape(rows_n, units, feat)
    pieces = [lax.dynamic_index_in_dim(up_t, r ^ k, 0, keepdims=False) for k in range(4)]
    up_blocks = [
        pieces[0],
        core_swap(pieces[1]),
        cross_swap(pieces[2]),
        lax.ppermute(pieces[3], "row", [(i, i ^ 3) for i in range(rows_n)]),
    ]

    qkv = jnp.stack([query_weight, key_weight, value_weight], axis=1).astype(BF)
    sub = qkv.shape[0]
    qkv = qkv.reshape(sub, 3, cols_n, hw).transpose(2, 0, 1, 3).reshape(cols_n, sub, 3 * hw)
    pieces = []
    for k in range(cols_n):
        piece = lax.dynamic_index_in_dim(qkv, (z + k) % cols_n, 0, keepdims=False)
        pieces.append(shift_col(piece, k) if k else piece)
    x_blocks.append(shift_col(x_blocks[1], 1))
    w_blocks = gather_row_rel(after(jnp.concatenate(pieces), x_blocks[2]))
    for _ in range(3, cols_n):
        x_blocks.append(shift_col(x_blocks[-1], 1))

    bias_mine = lax.dynamic_slice_in_dim(up_bias, r * units, units, 0)
    bias_rows = jnp.pad(jnp.stack(split3(bias_mine)), ((0, 13), (0, width - units)))
    pack = pack_weights(meta, up_blocks, down_weight, bias_rows)
    packs = [pack, shift_col(after(pack, x_blocks[-1]), 1)]

    qkv_bias = jnp.concatenate([query_bias, jnp.zeros_like(value_bias), value_bias])
    qkv_bias = jnp.broadcast_to(qkv_bias[None], (8, 3 * hw))
    vecs = jnp.stack([out_bias, norm1_gain, norm1_shift, down_bias, norm2_gain, norm2_shift])
    vecs = jnp.pad(jnp.stack(split3(vecs)), ((0, 1), (0, 2), (0, width - feat))).reshape(32, width)
    vecs = after(vecs, pack)
    q_rows, kv, w_qkv, out_pack = project_qkv(meta, x_blocks, w_blocks, qkv_bias, vecs, local, scale)
    kv_own, kv_far, kv_near = kv, cross_swap(kv), core_swap(kv)
    sizes = (rows_n, cols_n)
    acc, stat, k_near, v_near = attn_fwd(meta, q_rows, (kv_own, kv_near), (0, 1), heads, local, sizes)
    stat = after(stat, packs[1])
    state = (acc, stat)
    packs.append(shift_col(after(packs[1], stat), 1))
    kv_far = after(kv_far, stat)
    kv_diag = core_swap(kv_far)
    *mixed_part, qb_rows, k_far, v_far = attn_fwd(
        meta, q_rows, (kv_far, kv_diag), (2, 3), heads, local, sizes, state=state
    )
    mixed_part[1] = after(mixed_part[1], packs[2])
    mixed = [mixed_part[0]] + [shift_col(mixed_part[k], -k) for k in range(1, cols_n)]
    packs.append(shift_col(after(packs[2], *mixed), 1))

    out_pack = after(out_pack, stat)
    out_far, out_near = cross_swap(out_pack), core_swap(out_pack)
    out_far = after(out_far, qb_rows)
    out_packs = [out_pack, out_near, out_far, core_swap(out_far)]
    hidden, hidden_low, normal1, inv1, out_full, vecs = project(meta, mixed, out_packs, tokens, sub_out)

    up_bias_r = [
        jnp.sum(p[2 * units : 2 * units + 3, :units].astype(F32), axis=0) for p in packs
    ]
    up_bias_r = jnp.concatenate(up_bias_r)[None]
    h_own, h_far, h_near = hidden_low, cross_swap(hidden_low), core_swap(hidden_low)
    keep0, send0, act0, slope0 = ffn_fwd(h_own, h_near, packs, up_bias_r, units)
    h_far = after(h_far, send0)
    h_diag = core_swap(h_far)
    keep1, send1, act1, slope1 = ffn_fwd(h_far, h_diag, packs, up_bias_r, units)
    far = (keep1 + core_swap(send1).astype(F32)).astype(BF)
    got_far = cross_swap(far)
    got_near = core_swap(send0)
    output, grad_resid2, grad_branch, sums2 = norm2(
        meta, hidden, keep0, got_near, got_far, cotangent, vecs
    )

    g_own, g_far, g_near = grad_branch, cross_swap(grad_branch), core_swap(grad_branch)
    keep0, send0, pre0 = ffn_bwd(g_own, g_near, packs, slope0, units)
    g_far = after(g_far, send0)
    g_diag = core_swap(g_far)
    keep1, send1, pre1 = ffn_bwd(g_far, g_diag, packs, slope1, units)
    far = (keep1 + core_swap(send1).astype(F32)).astype(BF)
    got_far = cross_swap(far)
    got_near = core_swap(send0)
    g_one, g_two, g_up_bias = ffn_grads(
        meta,
        (act0, act1),
        (pre0, pre1),
        (h_own, h_near, h_far, h_diag),
        (g_own, g_near, g_far, g_diag),
    )
    if paired:
        g_two = lax.ppermute(g_two, "dp", [(0, 1), (1, 0)])
    keep0 = after(keep0, g_one)
    grad_resid1, grad_attended, sums1, grad_mixed = norm1_back(
        keep0, got_near, got_far, grad_resid2, normal1, inv1, vecs, out_full
    )
    grad_mixed = [grad_mixed[0]] + [shift_col(grad_mixed[k], k) for k in range(1, cols_n)]

    out_keep, out_far, out_send, sums = out_grads(
        meta, mixed, grad_attended, sums1, sums2, g_up_bias, sub_out, rows_n
    )
    out_got = core_swap(out_send)
    out_got = after(out_got, grad_mixed[1])
    out_message = far_message(out_far, sums, out_got)
    out_got_far = cross_swap(out_message)
    messages = col_messages(
        g_one, g_two, out_keep, sums, out_got, out_got_far, sub_out, cols_n, paired
    )

    grads = after(grad_rows(mixed_part, grad_mixed, heads), out_message)
    part3, dq = attn_bwd(qb_rows, grads, k_far, v_far, 1, heads, scale, BF, 4)
    got3 = core_swap(part3)
    dq = after(dq, messages[1])
    packed = shift_col(after(messages[1], dq), 1)
    part2, dq = attn_bwd(qb_rows, grads, k_far, v_far, 0, heads, scale, F32, 4, dq=dq)
    far_sum = (part2 + got3.astype(F32)).astype(BF)
    far_got = cross_swap(far_sum)
    packed = sum_messages([messages[2], packed])
    dq = after(dq, far_sum, packed)
    packed = shift_col(after(packed, dq), 1)
    *part1, dq = attn_bwd(qb_rows, grads, k_near, v_near, 1, heads, scale, BF, 4, dq=dq, pieces=2)
    got1 = [core_swap(part) for part in part1]
    packed = sum_messages([messages[3], packed])
    dq = after(dq, packed)
    packed = shift_col(after(packed, dq), 1)
    part0, grad_q = attn_bwd(
        qb_rows, grads, k_near, v_near, 0, heads, scale, F32, C4, dq=dq, last=True
    )

    d_blocks, back = join_grads(part0, *got1, far_got, grad_q, w_qkv, cols_n)
    ring = [shift_col(back[1], 1)]

    d_blocks = [after(d_blocks[0], packed), *d_blocks[1:]]
    own, far, send, send_far = qkv_grads(meta, x_blocks, d_blocks, feat)
    packed = sum_messages([after(messages[0], back[1]), packed])
    got, got_far = core_swap(send), core_swap(send_far)
    ring[0], got, got_far, packed = lax.optimization_barrier((ring[0], got, got_far, packed))
    for step in range(2, cols_n + 1):
        total = back[step % cols_n] + ring[-1].astype(F32)
        if step < cols_n:
            ring.append(shift_col(total.astype(BF), 1))
    grad_tokens = grad_resid1 + total
    if paired:
        other = lax.ppermute(packed, "dp", [(0, 1), (1, 0)])
    else:
        other = lax.psum(packed.astype(F32), "dp") - packed.astype(F32)
    g_bias = own[feat] + own[feat + 1]

    def with_bias(block, bias):
        hi = lax.reduce_precision(bias, 8, 7)
        rows = jnp.pad(jnp.stack([hi, bias - hi]), ((0, 14), (0, 0)))
        return jnp.concatenate([block, rows]).astype(BF)

    def bias_of(got):
        return got[-16].astype(F32) + got[-15].astype(F32)

    g_bias = g_bias + bias_of(got)
    mine = own[:feat] + got[:feat].astype(F32)
    got_x = got = cross_swap(with_bias(far + got_far.astype(F32), g_bias))
    g_bias = g_bias + bias_of(got)
    mine = mine + got[:feat].astype(F32)
    if paired:
        got = lax.ppermute(after(with_bias(mine, g_bias), ring[0]), "dp", [(0, 1), (1, 0)])
        g_bias = g_bias + bias_of(got)
        g_qkv = mine + got[:feat].astype(F32)
    else:
        g_bias, g_qkv = lax.psum((g_bias, mine), "dp")
    g_qkv = g_qkv.astype(BF).reshape(cols_n, sub, 3 * hw)
    pieces = []
    for k in range(cols_n):
        piece = lax.dynamic_index_in_dim(g_qkv, (z + k) % cols_n, 0, keepdims=False)
        pieces.append(shift_col(piece, k) if k else piece)
    g_qkv = spread(meta, pieces)
    other = after(other, ring[1], got_x)
    *g_up, g_down_weight, g_out_weight, sums = finish(
        meta, packed, other, rows_n, units, sub_out, paired
    )
    g_up[1] = core_swap(g_up[1])
    g_up[2] = cross_swap(g_up[2])
    g_up[3] = lax.ppermute(g_up[3], "row", [(i, i ^ 3) for i in range(rows_n)])
    g_up_weight = up_grads(meta, g_up)
    vec_out = lax.dynamic_slice_in_dim(sums[:6], r * feat, feat, 1)
    g_up_bias = lax.dynamic_index_in_dim(sums[8 : 8 + cols_n], z, 0, keepdims=False)

    return (
        output,
        grad_tokens,
        g_qkv[0],
        g_qkv[1],
        g_qkv[2],
        g_bias[:hw],
        g_bias[2 * hw :],
        g_out_weight,
        vec_out[2],
        vec_out[0],
        vec_out[1],
        g_up_weight,
        g_up_bias,
        g_down_weight,
        vec_out[5],
        vec_out[3],
        vec_out[4],
    )


def solution(mesh):
    token_spec = P(("dp", "col", "row"), None)
    placed = (
        token_spec,
        token_spec,
        P("dp"),
        P(("row", "col"), None),
        P(("row", "col"), None),
        P(("row", "col"), None),
        P("col"),
        P("col"),
        P(("col", "row"), None),
        P("row"),
        P("row"),
        P("row"),
        P("row", "col"),
        P("col"),
        P(("col", "row"), None),
        P("row"),
        P("row"),
        P("row"),
    )
    return jax.shard_map(
        per_device,
        mesh=mesh,
        in_specs=placed,
        out_specs=(token_spec, token_spec) + placed[3:],
        check_vma=False,
    )
```

```python
import functools
import math

import jax
import jax.numpy as jnp
from jax import lax
from jax.experimental import pallas as pl
from jax.experimental.pallas import tpu as pltpu
from jax.sharding import PartitionSpec as P

HD = 64
LANES = 256
EPS = 1e-05
BF = jnp.bfloat16
F32 = jnp.float32
VMEM_BYTES = 60 * 1024 * 1024
TURNED = HD + 16
SMALL_BYTES = 24 * 1024 * 1024
ATTN_BYTES = 36 * 1024 * 1024
NEAR_COST = 4
C4 = 6


def nn(a, b):
    return jnp.dot(a, b, preferred_element_type=F32)


def tn(a, b):
    return lax.dot_general(a, b, (((0,), (0,)), ((), ())), preferred_element_type=F32)


def nt(a, b):
    return lax.dot_general(a, b, (((1,), (1,)), ((), ())), preferred_element_type=F32)


def cost(us):
    return pl.CostEstimate(flops=int(us * 0.6e9), bytes_accessed=1000, transcendentals=0)


def head_lanes(shape, head, width):
    lane = lax.broadcasted_iota(jnp.int32, shape, 1)
    mine = (lane >= head * HD) & (lane < (head + 1) * HD)
    return mine | (lane == width) | ((lane >= width + 1 + 3 * head) & (lane < width + 4 + 3 * head))


def three_parts(x):
    hi = x.astype(BF).astype(F32)
    mid = (x - hi).astype(BF).astype(F32)
    return hi, mid, x - hi - mid


def tail_rows(parts, ones, n):
    row = lax.broadcasted_iota(jnp.int32, (n, parts[0].shape[1]), 0)
    out = jnp.where(row == 0, ones, 0.0)
    for head, value in enumerate(parts):
        for i, piece in enumerate(three_parts(value)):
            out = jnp.where(row == 1 + 3 * head + i, piece, out)
    return out


def widen_keys(kv, owner, base, meta, keys_out, values_out, turned, at, width, shift, sizes):
    n = kv.shape[0]
    rows_n, cols_n = sizes
    keys_out[at : at + n, :width] = kv[:, :width]
    values_out[at : at + n, :width] = kv[:, width:]
    shape = (n, LANES - width)
    t = lax.broadcasted_iota(jnp.int32, shape, 0) + base
    lane = lax.broadcasted_iota(jnp.int32, shape, 1)
    source = meta[3] - (t >> shift)
    source = jnp.where(source < 0, source + cols_n, source)
    position = ((source * rows_n + owner) << shift) + (t & ((1 << shift) - 1))
    mask = jnp.where(lane == 0, jnp.where(position >= meta[0], -1e30, 0.0), 1.0)
    keys_out[at : at + n, width:] = mask.astype(BF)
    values_out[at : at + n, width:] = jnp.ones(shape, BF)
    flat = values_out[at : at + n, :].T
    for head in range(width // HD):
        first = head * TURNED
        turned[first : first + HD, at : at + n] = flat[head * HD : (head + 1) * HD, :]
        turned[first + HD : first + TURNED, at : at + n] = jnp.ones((TURNED - HD, n), BF)


def attn_fwd_kernel(*refs, heads, first, pair, shift, sizes, chunk, blocks, parts):
    meta, *refs = refs
    q_refs, refs = refs[:parts], refs[parts:]
    kvs, refs = refs[: 2 * parts], refs[2 * parts :]
    if first:
        acc_out, stat_out, k_out, v_out, turned = refs
    else:
        acc_in, stat_in = refs[:2]
        outs = refs[2 : 2 + blocks]
        qb_ref, k_out, v_out, turned = refs[2 + blocks :]
    width = heads * HD
    keys = k_out.shape[0]
    at = 0
    for i, ref in enumerate(kvs):
        base = at % (keys // 2)
        owner = meta[1] ^ pair[i // parts]
        widen_keys(ref[...], owner, base, meta, k_out, v_out, turned, at, width, shift, sizes)
        at += ref.shape[0]
    q = jnp.concatenate([ref[...] for ref in q_refs], axis=0)
    rows = q.shape[0]
    slot = lax.broadcasted_iota(jnp.int32, (16, rows), 0)
    stat = jnp.zeros((16, rows), F32)
    logs = []
    for head in range(heads):
        qh = jnp.where(head_lanes(q.shape, head, width), q, jnp.zeros_like(q))
        scores = [nt(k_out[i : i + chunk, :], qh) for i in range(0, keys, chunk)]
        peak = functools.reduce(
            jnp.maximum, [jnp.max(s, axis=0, keepdims=True) for s in scores]
        )
        if not first:
            old = stat_in[head : head + 1, :]
            peak = jnp.maximum(peak, old)
        acc = None
        for i, s in enumerate(scores):
            p = jnp.exp(s - peak).astype(BF)
            at = head * TURNED
            part = nn(turned[at : at + TURNED, i * chunk : (i + 1) * chunk], p)
            acc = part if acc is None else acc + part
        total = acc[HD : HD + 1]
        mine = slice(head * HD, (head + 1) * HD)
        if first:
            acc_out[mine, :] = acc[:HD]
            stat = jnp.where(slot == head, peak, stat)
            stat = jnp.where(slot == head + 8, total, stat)
        else:
            keep = jnp.exp(old - peak)
            total = total + stat_in[head + 8 : head + 9, :] * keep
            out = ((acc[:HD] + acc_in[mine, :] * keep) * (1.0 / total)).astype(BF)
            each = rows // blocks
            for b in range(blocks):
                outs[b][mine, :] = out[:, b * each : (b + 1) * each]
            logs.append(-(peak + jnp.log(total)))
    if first:
        stat_out[...] = stat
    else:
        qb_ref[:, :width] = q[:, :width]
        qb_ref[:, width:] = tail_rows(logs, 1.0, LANES - width).T.astype(BF)


def attn_fwd(meta, q, kvs, pair, heads, local, sizes, us, state=None, chunk=512):
    rows = sum(part.shape[0] for part in q)
    half = sum(kv.shape[0] for kv in kvs) // 2
    width = kvs[0].shape[1] // 2
    first = state is None
    blocks = rows // local
    vmem = pl.BlockSpec(memory_space=pltpu.VMEM)
    args = [meta, *q, *kvs]
    if first:
        out_shape = [jax.ShapeDtypeStruct((width, rows), F32), jax.ShapeDtypeStruct((16, rows), F32)]
    else:
        args += list(state)
        out_shape = [jax.ShapeDtypeStruct((width, local), BF)] * blocks
        out_shape += [jax.ShapeDtypeStruct((rows, LANES), BF)]
    out_shape += [jax.ShapeDtypeStruct((2 * half, LANES), BF)] * 2
    return pl.pallas_call(
        functools.partial(
            attn_fwd_kernel,
            heads=heads,
            first=first,
            pair=pair,
            shift=local.bit_length() - 1,
            sizes=sizes,
            chunk=chunk,
            blocks=blocks,
            parts=len(q),
        ),
        in_specs=[pl.BlockSpec(memory_space=pltpu.SMEM)] + [vmem] * (len(args) - 1),
        out_specs=[vmem] * len(out_shape),
        out_shape=out_shape,
        scratch_shapes=[pltpu.VMEM((heads * TURNED, 2 * half), BF)],
        compiler_params=pltpu.CompilerParams(vmem_limit_bytes=ATTN_BYTES),
        cost_estimate=cost(us),
        name="attn_fwd_near" if first else "attn_fwd_far",
    )(*args)


def grad_rows_kernel(*refs, heads, blocks):
    outs, grads, wide = refs[:blocks], refs[blocks : 2 * blocks], refs[2 * blocks]
    width = heads * HD
    for b in range(blocks):
        g = grads[b][...].astype(F32)
        prod = g * outs[b][...].astype(F32)
        each = g.shape[1]
        parts = [
            -jnp.sum(prod[head * HD : (head + 1) * HD], axis=0, keepdims=True) for head in range(heads)
        ]
        tall = jnp.concatenate([g, tail_rows(parts, 0.0, LANES - width)], axis=0)
        wide[b * each : (b + 1) * each, :] = tall.T.astype(BF)


def grad_rows(outs, grads, heads):
    each = outs[0].shape[1]
    return small_call(
        functools.partial(grad_rows_kernel, heads=heads, blocks=len(outs)),
        jax.ShapeDtypeStruct((each * len(outs), LANES), BF),
        "grad_rows",
    )(*outs, *grads)


def attn_bwd_kernel(at_ref, q_ref, g_ref, k_ref, v_ref, dq_in, *refs, heads, block, pieces):
    outs, (dq_out, dk, dv) = refs[:pieces], refs[pieces:]
    width = heads * HD
    half = dk.shape[0]
    keys = pl.ds(pl.multiple_of(at_ref[0] * half, half), half)
    dk[...] = jnp.zeros_like(dk)
    dv[...] = jnp.zeros_like(dv)

    def step(i, carry):
        at = pl.ds(pl.multiple_of(i * block, block), block)
        q_all = q_ref[at, :]
        g_all = g_ref[at, :]
        k = k_ref[keys, :]
        dq = jnp.zeros((block, LANES), F32)
        for head in range(heads):
            mine = head_lanes((block, LANES), head, width)
            q = jnp.where(mine, q_all, jnp.zeros_like(q_all))
            g = jnp.where(mine, g_all, jnp.zeros_like(g_all))
            p = jnp.exp(nt(k, q))
            ds = (p * nt(v_ref[keys, :], g)).astype(BF)
            dv[...] += nn(p.astype(BF), g)
            dk[...] += nn(ds, q)
            dq = jnp.where(mine, tn(ds, k), dq)
        dq_out[at, :] = dq_in[at, :] + dq
        return carry

    lax.fori_loop(0, q_ref.shape[0] // block, step, 0)
    each = outs[0].shape[0]
    for i, out in enumerate(outs):
        at = slice(i * each, (i + 1) * each)
        out[:, :width] = dk[at, :width].astype(out.dtype)
        out[:, width:] = dv[at, :width].astype(out.dtype)


def attn_bwd(at, q, g, k, v, dq, heads, us, pieces=2, block=512):
    rows = q.shape[0]
    half = k.shape[0] // 2
    width = heads * HD
    vmem = pl.BlockSpec(memory_space=pltpu.VMEM)
    out_shape = [jax.ShapeDtypeStruct((half // pieces, 2 * width), BF)] * pieces
    return pl.pallas_call(
        functools.partial(attn_bwd_kernel, heads=heads, block=block, pieces=pieces),
        in_specs=[pl.BlockSpec(memory_space=pltpu.SMEM)] + [vmem] * 5,
        out_specs=[vmem] * (pieces + 1),
        out_shape=out_shape + [jax.ShapeDtypeStruct((rows, LANES), F32)],
        scratch_shapes=[pltpu.VMEM((half, LANES), F32)] * 2,
        compiler_params=pltpu.CompilerParams(vmem_limit_bytes=ATTN_BYTES),
        cost_estimate=cost(us),
        name="attn_bwd",
    )(jnp.full((1,), at, jnp.int32), q, g, k, v, dq)


def small_call(kernel, out_shape, name, scratch=(), us=1.4):
    return pl.pallas_call(
        kernel,
        out_shape=out_shape,
        scratch_shapes=scratch,
        compiler_params=pltpu.CompilerParams(vmem_limit_bytes=SMALL_BYTES),
        cost_estimate=cost(us),
        name=name,
    )


def meta_call(kernel, args, out_shape, name, scratch=(), us=1.2):
    vmem = pl.BlockSpec(memory_space=pltpu.VMEM)
    return pl.pallas_call(
        kernel,
        in_specs=[pl.BlockSpec(memory_space=pltpu.SMEM)] + [vmem] * (len(args) - 1),
        out_specs=[vmem] * len(out_shape),
        out_shape=out_shape,
        scratch_shapes=scratch,
        compiler_params=pltpu.CompilerParams(vmem_limit_bytes=SMALL_BYTES),
        cost_estimate=cost(us),
        name=name,
    )(*args)


def row_mean(x):
    return jnp.mean(x, axis=1, keepdims=True)


def col_sum(x):
    return jnp.sum(x, axis=0, keepdims=True)


def norm_forward(resid, gain, shift):
    centered = resid - row_mean(resid)
    inv = lax.rsqrt(row_mean(centered * centered) + EPS)
    normal = centered * inv
    return normal * gain + shift, normal, inv


def norm_backward(grad_out, normal, inv, gain):
    scaled = grad_out * gain
    return inv * (scaled - row_mean(scaled) - normal * row_mean(scaled * normal))


def project_qkv_kernel(meta, *refs, n, blocks, last, rows_n, cols_n, feat, hw, scale):
    x, ws, bias_ref = refs[:n], refs[n : n + rows_n], refs[n + rows_n]
    if last:
        vec_ref, q_ref, kv_ref, w_out, pack_ref, w_all = refs[n + rows_n + 1 :]
    else:
        q_ref, kv_ref, w_all = refs[n + rows_n + 1 :]
    each = feat // cols_n
    for k in range(rows_n):
        for m in range(cols_n):
            source = meta[3] - m
            source = jnp.where(source < 0, source + cols_n, source)
            at = pl.multiple_of((meta[1] ^ k) * feat + source * each, each)
            w_all[pl.ds(at, each), :] = ws[k][m * each : (m + 1) * each, :]
    w = w_all[...]
    each = q_ref.shape[0] // len(blocks)
    for i, k in enumerate(blocks):
        at = slice(i * each, (i + 1) * each)
        out = nn(x[k][:each, :], w) + bias_ref[0:1, :]
        q_ref[at, :hw] = (out[:, :hw].astype(BF).astype(F32) * scale).astype(BF)
        lane = lax.broadcasted_iota(jnp.int32, (each, LANES - hw), 1)
        q_ref[at, hw:] = jnp.where(lane == 0, 1.0, 0.0).astype(BF)
        kv_ref[at, :] = out[:, hw:].astype(BF)
    if last:
        w_out[...] = w.T
        more = x[0].shape[0] - each
        for k in range(n):
            pack_ref[k * more : (k + 1) * more, :] = x[k][each:, :]
        pack_ref[n * more :, :] = vec_ref[...]


def project_qkv(meta, x, blocks, cols_n, ws, bias, local, scale, vecs=None):
    feat, wide = ws[0].shape
    hw = wide // 3
    rows = local * len(blocks)
    shapes = [
        jax.ShapeDtypeStruct((rows, LANES), BF),
        jax.ShapeDtypeStruct((rows, 2 * hw), BF),
    ]
    args = [meta, *x, *ws, bias]
    if vecs is not None:
        args.append(vecs)
        more = (x[0].shape[0] - local) * len(x) + vecs.shape[0]
        shapes.append(jax.ShapeDtypeStruct((wide, feat * len(ws)), BF))
        shapes.append(jax.ShapeDtypeStruct((more, vecs.shape[1]), BF))
    return meta_call(
        functools.partial(
            project_qkv_kernel,
            n=len(x),
            blocks=blocks,
            last=vecs is not None,
            rows_n=len(ws),
            cols_n=cols_n,
            feat=feat,
            hw=hw,
            scale=scale,
        ),
        args,
        shapes,
        "project_qkv",
        scratch=[pltpu.VMEM((feat * len(ws), wide), BF)],
    )


def project_kernel(meta, *refs, n, rows_n, sub, feat):
    mixed, packs = refs[:n], refs[n : n + rows_n]
    x_ref, hid_ref, low_ref, normal_ref, inv_ref, w_ref, vec_ref = refs[n + rows_n :]
    r = meta[1]
    for k in range(rows_n):
        at = pl.multiple_of((r ^ k) * sub, sub)
        for i in range(n):
            w_ref[i, pl.ds(at, sub), :] = packs[k][((n - i) % n) * sub : ((n - i) % n + 1) * sub, :]
    values = []
    for k in range(rows_n):
        part = packs[k][n * sub : n * sub + 32, :feat].astype(F32)
        values.append(part[0:8] + part[8:16] + part[16:24])
    pieces = []
    for owner in range(rows_n):
        value = values[0]
        for k in range(1, rows_n):
            value = jnp.where((r ^ k) == owner, values[k], value)
        pieces.append(value)
    vecs = jnp.concatenate(pieces, axis=1)
    vec_ref[...] = vecs
    total = x_ref[...].astype(F32) + vecs[0:1, :]
    for j in range(n):
        total = total + tn(mixed[j][...], w_ref[j])
    hidden, normal, inv = norm_forward(total, vecs[1:2, :], vecs[2:3, :])
    hid_ref[...] = hidden
    low_ref[...] = hidden.astype(BF)
    normal_ref[...] = normal
    inv_ref[...] = jnp.broadcast_to(inv, inv_ref.shape)


def project(meta, mixed, packs, x, sub):
    rows, width = x.shape
    feat = width // len(packs)
    return meta_call(
        functools.partial(
            project_kernel, n=len(mixed), rows_n=len(packs), sub=sub, feat=feat
        ),
        [meta, *mixed, *packs, x],
        [
            jax.ShapeDtypeStruct((rows, width), F32),
            jax.ShapeDtypeStruct((rows, width), BF),
            jax.ShapeDtypeStruct((rows, width), F32),
            jax.ShapeDtypeStruct((rows, 128), F32),
            jax.ShapeDtypeStruct((len(mixed), sub * len(packs), width), BF),
            jax.ShapeDtypeStruct((8, width), F32),
        ],
        "project_norm1",
    )


def weight_rows(meta, packs, units, down):
    size = packs[0].shape[0] // 2
    at = size if down else 0
    values = [packs[0][at : at + units, :]]
    rest = packs[1:]
    if rest[0].shape[0] > size:
        return values + [ref[at : at + units, :] for ref in rest]
    mine = (meta[4] == 0) != down
    for own, other in zip(rest[::2], rest[1::2]):
        values.append(jnp.where(mine, own[:units, :].astype(F32), other[:units, :].astype(F32)).astype(BF))
    return values


def bias_rows(meta, packs, units):
    size = packs[0].shape[0] // 2
    at = slice(units, units + 16)
    values = [packs[0][at, :].astype(F32)]
    rest = packs[1:]
    if rest[0].shape[0] > size:
        values += [ref[at, :].astype(F32) for ref in rest]
    else:
        for own, other in zip(rest[::2], rest[1::2]):
            values.append(jnp.where(meta[4] == 0, own[at, :].astype(F32), other[at, :].astype(F32)))
    return jnp.concatenate([v[0:1, :units] + v[1:2, :units] + v[2:3, :units] for v in values], axis=1)


def ffn_fwd_kernel(meta, *refs, n, units):
    h0, h1 = refs[:2]
    packs = refs[2 : 2 + n]
    keep_ref, send_ref, act_ref, slope_ref = refs[2 + n :]
    rows = h0.shape[0]
    h = jnp.concatenate([h0[...], h1[...]], axis=0)
    up = jnp.concatenate(weight_rows(meta, packs, units, False), axis=0)
    x = nt(h, up) + bias_rows(meta, packs, units)
    cdf = 0.5 * (1.0 + lax.erf(x * math.sqrt(0.5)))
    act = (x * cdf).astype(BF)
    act_ref[...] = act
    slope = cdf + x * (math.sqrt(0.5 / math.pi) * jnp.exp(-0.5 * x * x))
    slope_ref[...] = slope.astype(BF)
    out = nn(act, jnp.concatenate(weight_rows(meta, packs, units, True), axis=0))
    keep_ref[...] = out[:rows]
    send_ref[...] = out[rows:].astype(BF)


def ffn_fwd(meta, h0, h1, packs, units, wide):
    rows, width = h0.shape
    return meta_call(
        functools.partial(ffn_fwd_kernel, n=len(packs), units=units),
        [meta, h0, h1, *packs],
        [
            jax.ShapeDtypeStruct((rows, width), F32),
            jax.ShapeDtypeStruct((rows, width), BF),
            jax.ShapeDtypeStruct((2 * rows, wide), BF),
            jax.ShapeDtypeStruct((2 * rows, wide), BF),
        ],
        "ffn_fwd",
        us=1.4,
    )


def ffn_bwd_kernel(meta, *refs, n, units):
    g0, g1 = refs[:2]
    packs = refs[2 : 2 + n]
    slope_ref, keep_ref, send_ref, pre_ref = refs[2 + n :]
    rows = g0.shape[0]
    g = jnp.concatenate([g0[...], g1[...]], axis=0)
    down = jnp.concatenate(weight_rows(meta, packs, units, True), axis=0)
    pre = (nt(g, down) * slope_ref[...].astype(F32)).astype(BF)
    pre_ref[...] = pre
    out = nn(pre, jnp.concatenate(weight_rows(meta, packs, units, False), axis=0))
    keep_ref[...] = out[:rows]
    send_ref[...] = out[rows:].astype(BF)


def ffn_bwd(meta, g0, g1, packs, slope, units):
    rows, width = g0.shape
    return meta_call(
        functools.partial(ffn_bwd_kernel, n=len(packs), units=units),
        [meta, g0, g1, *packs, slope],
        [
            jax.ShapeDtypeStruct((rows, width), F32),
            jax.ShapeDtypeStruct((rows, width), BF),
            jax.ShapeDtypeStruct(slope.shape, BF),
        ],
        "ffn_bwd",
        us=1.4,
    )


def ffn_grads_kernel(meta, *refs):
    act0, act1, pre0, pre1 = refs[:4]
    h = jnp.concatenate([ref[...] for ref in refs[4:8]], axis=0)
    g = jnp.concatenate([ref[...] for ref in refs[8:12]], axis=0)
    keep_ref, send_ref, bias_ref = refs[12:]
    pre = jnp.concatenate([pre0[...], pre1[...]], axis=0)
    act = jnp.concatenate([act0[...], act1[...]], axis=0)
    g_up = tn(pre, h).astype(BF)
    g_down = tn(act, g).astype(BF)
    first = meta[4] == 0

    @pl.when(first)
    def _():
        keep_ref[...] = g_up
        send_ref[...] = g_down

    @pl.when(jnp.logical_not(first))
    def _():
        keep_ref[...] = g_down
        send_ref[...] = g_up

    bias_ref[...] = jnp.broadcast_to(col_sum(pre.astype(F32)), bias_ref.shape)


def ffn_grads(meta, acts, pres, hiddens, grads):
    width = hiddens[0].shape[1]
    wide = acts[0].shape[1]
    return meta_call(
        ffn_grads_kernel,
        [meta, *acts, *pres, *hiddens, *grads],
        [
            jax.ShapeDtypeStruct((wide, width), BF),
            jax.ShapeDtypeStruct((wide, width), BF),
            jax.ShapeDtypeStruct((8, wide), F32),
        ],
        "ffn_grads",
    )


def norm2_kernel(
    meta, hid_ref, keep_ref, near_ref, far_ref, cot_ref, vec_ref, out_ref, grad_ref, low_ref, sum_ref
):
    branch = keep_ref[...] + near_ref[...].astype(F32) + far_ref[...].astype(F32) + vec_ref[3:4, :]
    gain = vec_ref[4:5, :]
    normed, normal, inv = norm_forward(hid_ref[...] + branch, gain, vec_ref[5:6, :])
    row = lax.broadcasted_iota(jnp.int32, (out_ref.shape[0], 1), 0)
    valid = (meta[2] + row < meta[0]).astype(F32)
    out_ref[...] = (normed * valid).astype(BF)
    grad_y = cot_ref[...].astype(F32) * valid
    grad = norm_backward(grad_y, normal, inv, gain)
    grad_ref[...] = grad
    low = grad.astype(BF)
    low_ref[...] = low
    sum_ref[...] = jnp.zeros_like(sum_ref)
    sum_ref[0:1, :] = col_sum(grad_y * normal)
    sum_ref[1:2, :] = col_sum(grad_y)
    sum_ref[2:3, :] = col_sum(low.astype(F32))


def norm2(meta, hidden, keep, near, far, cot, vecs):
    rows, width = hidden.shape
    shapes = [
        jax.ShapeDtypeStruct((rows, width), BF),
        jax.ShapeDtypeStruct((rows, width), F32),
        jax.ShapeDtypeStruct((rows, width), BF),
        jax.ShapeDtypeStruct((8, width), F32),
    ]
    return meta_call(norm2_kernel, [meta, hidden, keep, near, far, cot, vecs], shapes, "norm2_both")


def norm1_back_kernel(
    keep_ref, near_ref, far_ref, add_ref, normal_ref, inv_ref, vec_ref, w_ref, out_ref, low_ref, sum_ref, *mixed
):
    grad = keep_ref[...] + near_ref[...].astype(F32) + far_ref[...].astype(F32) + add_ref[...]
    normal = normal_ref[...]
    resid = norm_backward(grad, normal, inv_ref[:, 0:1], vec_ref[1:2, :])
    out_ref[...] = resid
    low = resid.astype(BF)
    low_ref[...] = low
    for j, ref in enumerate(mixed):
        ref[...] = nt(w_ref[j], low).astype(BF)
    sum_ref[...] = jnp.zeros_like(sum_ref)
    sum_ref[0:1, :] = col_sum(grad * normal)
    sum_ref[1:2, :] = col_sum(grad)
    sum_ref[2:3, :] = col_sum(low.astype(F32))


def norm1_back(keep, near, far, add, normal, inv, vecs, w):
    rows, width = add.shape
    out = small_call(
        norm1_back_kernel,
        [
            jax.ShapeDtypeStruct((rows, width), F32),
            jax.ShapeDtypeStruct((rows, width), BF),
            jax.ShapeDtypeStruct((8, width), F32),
        ]
        + [jax.ShapeDtypeStruct((w.shape[1], rows), BF)] * w.shape[0],
        "norm1_back",
    )(keep, near, far, add, normal, inv, vecs, w)
    return out[0], out[1], out[2], out[3:]


def two_parts(x):
    hi = x.astype(BF).astype(F32)
    return jnp.concatenate([hi, x - hi], axis=0).astype(BF)


def both_parts(rows):
    n = rows.shape[0] // 2
    return rows[:n].astype(F32) + rows[n:].astype(F32)


def out_grads_kernel(meta, *refs, n, rows_n, sub):
    mixed, grad, s1, s2, bias = refs[:n], *refs[n : n + 4]
    keep, far, send, sums, total = refs[n + 4 :]
    g = grad[...]
    for j in range(n):
        total[j] = nn(mixed[j][...], g)
    count = n * sub
    for j in range(n):
        at = slice(j * sub, (j + 1) * sub)

        def rows(k):
            return total[j, pl.ds(pl.multiple_of((meta[1] ^ k) * sub, sub), sub), :]

        keep[at, :] = rows(0)
        far[at, :] = rows(2)
        send[at, :] = rows(1).astype(BF)
        send[count + j * sub : count + (j + 1) * sub, :] = rows(3).astype(BF)
    sums[...] = jnp.zeros_like(sums)
    sums[0:3, :] = s1[0:3, :]
    sums[3:6, :] = s2[0:3, :]
    units = bias.shape[1] // n
    for j in range(n):
        away = meta[3] - j
        away = jnp.where(away < 0, away + n, away)
        value = bias[0:1, :units]
        for k in range(1, n):
            value = jnp.where(away == k, bias[0:1, k * units : (k + 1) * units], value)
        zero = jnp.zeros_like(value)
        row = [jnp.where(meta[1] == owner, value, zero) for owner in range(rows_n)]
        sums[8 + j : 9 + j, :] = jnp.concatenate(row, axis=1)
    send[2 * count :, :] = two_parts(sums[...])


def out_grads(meta, mixed, grad, s1, s2, bias, sub, rows_n):
    n, heads, width = len(mixed), mixed[0].shape[0], grad.shape[1]
    shapes = [
        jax.ShapeDtypeStruct((n * sub, width), F32),
        jax.ShapeDtypeStruct((n * sub, width), F32),
        jax.ShapeDtypeStruct((2 * n * sub + 32, width), BF),
        jax.ShapeDtypeStruct((16, width), F32),
    ]
    return meta_call(
        functools.partial(out_grads_kernel, n=n, sub=sub, rows_n=rows_n),
        [meta, *mixed, grad, s1, s2, bias],
        shapes,
        "out_grads",
        scratch=[pltpu.VMEM((n, heads, width), F32)],
    )


def far_message_kernel(far, sums, got, out):
    n = far.shape[0]
    out[:n, :] = (far[...] + got[n : 2 * n, :].astype(F32)).astype(BF)
    out[n:, :] = two_parts(sums[...] + both_parts(got[2 * n :, :]))


def far_message(far, sums, got):
    n, width = far.shape
    shape = jax.ShapeDtypeStruct((n + 32, width), BF)
    return small_call(far_message_kernel, shape, "far_message", us=0.7)(far, sums, got)


def col_messages_kernel(*refs, n, sub, added):
    (one, two, keep, sums, near, far), outs = refs[:6], refs[6:]
    count = n * sub
    both = sums[...] + both_parts(near[2 * count :, :]) + both_parts(far[count:, :])
    parts = two_parts(both)
    own = keep[...] + near[:count, :].astype(F32) + far[:count, :].astype(F32)
    units = one.shape[0] // n
    size = units if added else 2 * units
    for k in range(n):
        j = (n - k) % n
        at = slice(k * units, (k + 1) * units)
        if added:
            outs[k][:units, :] = (one[at, :].astype(F32) + two[at, :].astype(F32)).astype(BF)
        else:
            outs[k][:units, :] = one[at, :]
            outs[k][units:size, :] = two[at, :]
        outs[k][size : size + sub, :] = own[j * sub : (j + 1) * sub].astype(BF)
        outs[k][size + sub :, :] = parts


def col_messages(one, two, keep, sums, near, far, sub, n, added):
    rows, width = one.shape
    size = rows // n * (1 if added else 2)
    shapes = [jax.ShapeDtypeStruct((size + sub + 32, width), BF)] * n
    return small_call(
        functools.partial(col_messages_kernel, n=n, sub=sub, added=added), shapes, "col_messages"
    )(one, two, keep, sums, near, far)


def sum_messages_kernel(*refs):
    refs, out = refs[:-1], refs[-1]
    n = out.shape[0] - 32
    total = refs[0][:n, :].astype(F32)
    sums = both_parts(refs[0][n:, :])
    for ref in refs[1:]:
        total = total + ref[:n, :].astype(F32)
        sums = sums + both_parts(ref[n:, :])
    out[:n, :] = total.astype(BF)
    out[n:, :] = two_parts(sums)


def sum_messages(messages):
    shape = jax.ShapeDtypeStruct(messages[0].shape, BF)
    return small_call(sum_messages_kernel, shape, "sum_messages", us=0.7)(*messages)


def finish_kernel(meta, own, other, *refs, rows_n, units, sub, paired):
    ups, (down, out, sums) = refs[:rows_n], refs[rows_n:]
    size = own.shape[0] - sub - 32
    a = own[:size, :].astype(F32)
    b = other[:size, :].astype(F32)
    if paired:
        first = meta[4] == 0
        up = jnp.where(first, a, b)
        down[...] = jnp.where(first, b, a)
    else:
        up = a[:units] + b[:units]
        down[...] = a[units:] + b[units:]
    feat = up.shape[1] // rows_n
    pieces = [up[:, k * feat : (k + 1) * feat] for k in range(rows_n)]
    for k in range(rows_n):
        value = pieces[0]
        for owner in range(1, rows_n):
            value = jnp.where((meta[1] ^ k) == owner, pieces[owner], value)
        ups[k][...] = value.T.astype(BF)
    at = size + sub
    out[...] = own[size:at, :].astype(F32) + other[size:at, :].astype(F32)
    sums[...] = both_parts(own[at:, :]) + both_parts(other[at:, :])


def finish(meta, own, other, rows_n, units, sub, paired):
    width = own.shape[1]
    shapes = [jax.ShapeDtypeStruct((width // rows_n, units), BF)] * rows_n
    shapes += [jax.ShapeDtypeStruct((n, width), F32) for n in (units, sub, 16)]
    return meta_call(
        functools.partial(finish_kernel, rows_n=rows_n, units=units, sub=sub, paired=paired),
        [meta, own, other],
        shapes,
        "finish_grads",
    )


def up_grads_kernel(meta, *refs, n):
    pieces, out = refs[:n], refs[n]
    units = pieces[0].shape[1]
    values = [ref[...].astype(F32) for ref in pieces]
    for owner in range(n):
        value = values[0]
        for k in range(1, n):
            value = jnp.where((meta[1] ^ k) == owner, values[k], value)
        out[:, owner * units : (owner + 1) * units] = value


def up_grads(meta, pieces):
    feat, units = pieces[0].shape
    return meta_call(
        functools.partial(up_grads_kernel, n=len(pieces)),
        [meta, *pieces],
        [jax.ShapeDtypeStruct((feat, units * len(pieces)), F32)],
        "up_grads",
    )[0]


def join_kernel(keep0, keep1, near0, near1, far, dq, w_ref, *outs, scale, hw):
    n = len(outs) // 2
    each = outs[0].shape[0]
    half = keep0.shape[0]
    for k in range(n):
        at = slice(k * each, (k + 1) * each)
        inside = slice(at.start % half, at.start % half + each)
        keep, near = ((keep0, near0), (keep1, near1))[at.start // half]
        kv = keep[inside, :].astype(F32) + near[inside, :].astype(F32) + far[at, :].astype(F32)
        d = jnp.concatenate([(dq[at, :hw] * scale).astype(BF), kv.astype(BF)], axis=1)
        outs[k][...] = d
        outs[n + k][...] = nn(d, w_ref[...]).astype(outs[n + k].dtype)


def join_grads(keep, near, far, dq, w, n, scale):
    rows = dq.shape[0]
    wide, width = w.shape
    shapes = [jax.ShapeDtypeStruct((rows // n, wide), BF)] * n
    shapes += [jax.ShapeDtypeStruct((rows // n, width), BF if k == 1 else F32) for k in range(n)]
    kernel = functools.partial(join_kernel, scale=scale, hw=wide // 3)
    out = small_call(kernel, shapes, "join_grads")(*keep, *near, far, dq, w)
    return out[:n], out[n:]


def qkv_grads_kernel(meta, *refs, n, feat):
    x, grads, keep, far, send, send_far, total = refs[:n], refs[n : 2 * n], *refs[2 * n :]
    each = grads[0].shape[0]
    rows_of_x = jnp.concatenate([ref[:each, :] for ref in x], axis=0)
    g = jnp.concatenate([ref[...] for ref in grads], axis=0)
    total[...] = tn(rows_of_x, g)

    def rows(k):
        return total[pl.ds(pl.multiple_of((meta[1] ^ k) * feat, feat), feat), :]

    bias = col_sum(g.astype(F32))
    hi = bias.astype(BF).astype(F32)
    row = lax.broadcasted_iota(jnp.int32, (16, bias.shape[1]), 0)
    tail = jnp.where(row == 0, hi, jnp.where(row == 1, bias - hi, 0.0))
    keep[:feat, :] = rows(0)
    keep[feat:, :] = tail
    far[...] = rows(2)
    send[:feat, :] = rows(1).astype(BF)
    send[feat:, :] = tail.astype(BF)
    send_far[...] = rows(3).astype(BF)


def qkv_grads(meta, x, grads, feat):
    wide = grads[0].shape[1]
    width = x[0].shape[1]
    return meta_call(
        functools.partial(qkv_grads_kernel, n=len(x), feat=feat),
        [meta, *x, *grads],
        [
            jax.ShapeDtypeStruct((feat + 16, wide), F32),
            jax.ShapeDtypeStruct((feat, wide), F32),
            jax.ShapeDtypeStruct((feat + 16, wide), BF),
            jax.ShapeDtypeStruct((feat, wide), BF),
        ],
        "qkv_grads",
        scratch=[pltpu.VMEM((width, wide), F32)],
    )


def spread_kernel(meta, *refs, n):
    pieces, outs = refs[:n], refs[n:]
    hw = pieces[0].shape[1] // 3
    values = [ref[...].astype(F32) for ref in pieces]
    for j in range(n):
        away = meta[3] - j
        away = jnp.where(away < 0, away + n, away)
        value = values[0]
        for k in range(1, n):
            value = jnp.where(away == k, values[k], value)
        for i, out in enumerate(outs):
            out[:, j * hw : (j + 1) * hw] = value[:, i * hw : (i + 1) * hw]


def spread(meta, pieces):
    sub, wide = pieces[0].shape
    width = wide // 3 * len(pieces)
    return meta_call(
        functools.partial(spread_kernel, n=len(pieces)),
        [meta, *pieces],
        [jax.ShapeDtypeStruct((sub, width), F32)] * 3,
        "spread",
    )


def pack_kernel(meta, *refs, n):
    blocks, (down, bias, out, half) = refs[:n], refs[n:]
    units, feat = blocks[0].shape
    size = out.shape[0] // 2
    values = [ref[...].astype(F32) for ref in blocks]
    for owner in range(n):
        value = values[0]
        for k in range(1, n):
            value = jnp.where((meta[1] ^ k) == owner, values[k], value)
        out[:units, owner * feat : (owner + 1) * feat] = value.astype(BF)
    out[units:size, :] = bias[...]
    out[size : size + units, :] = down[...].astype(BF)
    out[size + units :, :] = jnp.zeros((size - units, out.shape[1]), BF)

    @pl.when(meta[4] == 0)
    def _():
        half[...] = out[:size, :]

    @pl.when(meta[4] != 0)
    def _():
        half[...] = out[size:, :]


def pack_weights(meta, blocks, down, bias):
    rows, width = down.shape
    size = rows + bias.shape[0]
    return meta_call(
        functools.partial(pack_kernel, n=len(blocks)),
        [meta, *blocks, down, bias],
        [jax.ShapeDtypeStruct((2 * size, width), BF), jax.ShapeDtypeStruct((size, width), BF)],
        "pack_weights",
    )


CORE = [(0, 1), (1, 0), (2, 3), (3, 2)]
CROSS = [(0, 2), (2, 0), (1, 3), (3, 1)]


def core_swap(x):
    return lax.ppermute(x, "row", CORE)


def cross_swap(x):
    return lax.ppermute(x, "row", CROSS)


def shift_col(x, step):
    n = lax.axis_size("col")
    return lax.ppermute(x, "col", [(i, (i + step) % n) for i in range(n)])


def after(x, *others):
    return lax.optimization_barrier((x,) + others)[0]


def natural_row(blocks):
    r = lax.axis_index("row")
    low = (r & 1) == 0
    b0, b1, b2, b3 = blocks
    left = jnp.where(low, jnp.stack([b0, b1]), jnp.stack([b1, b0]))
    right = jnp.where(low, jnp.stack([b2, b3]), jnp.stack([b3, b2]))
    return jnp.where(r < 2, jnp.concatenate([left, right]), jnp.concatenate([right, left]))


def gather_row_rel(x):
    far = cross_swap(x)
    near = core_swap(x)
    return [x, near, far, core_swap(far)]


def sum_dp(x):
    n = lax.axis_size("dp")
    if n == 2:
        return x + lax.ppermute(x, "dp", [(0, 1), (1, 0)])
    return lax.psum(x, "dp")


def split3(x):
    hi = lax.reduce_precision(x, 8, 7)
    mid = lax.reduce_precision(x - hi, 8, 7)
    low = x - hi - mid
    return hi.astype(BF), mid.astype(BF), low.astype(BF)


def per_device(
    tokens,
    cotangent,
    lengths,
    query_weight,
    key_weight,
    value_weight,
    query_bias,
    value_bias,
    out_weight,
    out_bias,
    norm1_gain,
    norm1_shift,
    up_weight,
    up_bias,
    down_weight,
    down_bias,
    norm2_gain,
    norm2_shift,
):
    rows_n = lax.axis_size("row")
    cols_n = lax.axis_size("col")
    r = lax.axis_index("row")
    z = lax.axis_index("col")
    local, width = tokens.shape
    block_len = local * cols_n
    hw = width // cols_n
    heads = hw // HD
    feat = width // rows_n
    scale = 1.0 / math.sqrt(HD)
    paired = lax.axis_size("dp") == 2
    pair = lax.axis_index("dp") if paired else jnp.zeros((), jnp.int32)
    meta = jnp.stack([lengths[0], r, z * (local * rows_n) + r * local, z, pair]).astype(jnp.int32)

    sub_out = out_weight.shape[0]
    x_blocks = [jnp.concatenate([tokens, out_weight.astype(BF)])]
    x_blocks.append(shift_col(x_blocks[0], 1))

    up_t = up_weight.astype(BF).T
    units = up_t.shape[0] // rows_n
    up_t = up_t.reshape(rows_n, units, feat)
    pieces = [lax.dynamic_index_in_dim(up_t, r ^ k, 0, keepdims=False) for k in range(4)]
    up_blocks = [
        pieces[0],
        core_swap(pieces[1]),
        cross_swap(pieces[2]),
        lax.ppermute(pieces[3], "row", [(i, i ^ 3) for i in range(rows_n)]),
    ]

    qkv = jnp.stack([query_weight, key_weight, value_weight], axis=1).astype(BF)
    sub = qkv.shape[0]
    qkv = qkv.reshape(sub, 3, cols_n, hw).transpose(2, 0, 1, 3).reshape(cols_n, sub, 3 * hw)
    pieces = []
    for k in range(cols_n):
        piece = lax.dynamic_index_in_dim(qkv, (z + k) % cols_n, 0, keepdims=False)
        pieces.append(shift_col(piece, k) if k else piece)
    second, *pieces = lax.optimization_barrier((x_blocks[1], *pieces))
    x_blocks.append(shift_col(second, 1))
    w_blocks = gather_row_rel(jnp.concatenate(pieces))
    for _ in range(3, cols_n):
        x_blocks.append(shift_col(x_blocks[-1], 1))

    bias_mine = lax.dynamic_slice_in_dim(up_bias, r * units, units, 0)
    bias_rows = jnp.pad(jnp.stack(split3(bias_mine)), ((0, 13), (0, width - units)))
    def cross_dp(x):
        return lax.ppermute(x, "dp", [(0, 1), (1, 0)]) if paired else x[:1]

    pack, half = pack_weights(meta, up_blocks, down_weight, bias_rows)
    hops = [shift_col(after(half if paired else pack, x_blocks[-1]), 1)]

    qkv_bias = jnp.concatenate([query_bias, jnp.zeros_like(value_bias), value_bias])
    qkv_bias = jnp.broadcast_to(qkv_bias[None], (8, 3 * hw))
    vecs = jnp.stack([out_bias, norm1_gain, norm1_shift, down_bias, norm2_gain, norm2_shift])
    vecs = jnp.pad(jnp.stack(split3(vecs)), ((0, 1), (0, 2), (0, width - feat))).reshape(32, width)
    early, late = (0, 1), tuple(range(2, cols_n))
    q_a, kv_a = project_qkv(meta, x_blocks[:2], early, cols_n, w_blocks, qkv_bias, local, scale)
    far_a, near_a = cross_swap(kv_a), core_swap(kv_a)
    x_blocks[-1], near_a, pack = lax.optimization_barrier((x_blocks[-1], near_a, pack))
    q_b, kv_b, w_qkv, out_pack = project_qkv(
        meta, x_blocks, late, cols_n, w_blocks, qkv_bias, local, scale, vecs
    )
    far_b, near_b = cross_swap(kv_b), core_swap(kv_b)
    near_b, far_a = lax.optimization_barrier((near_b, far_a))
    sizes = (rows_n, cols_n)
    q_parts = [q_a, q_b]
    acc, stat, k_near, v_near = attn_fwd(
        meta, q_parts, [kv_a, kv_b, near_a, near_b], (0, 1), heads, local, sizes, NEAR_COST
    )
    stat, hops[0] = lax.optimization_barrier((stat, hops[0]))
    hops.append(shift_col(hops[0], 1))
    crossed = [cross_dp(hops[0])]
    stat, far_a, far_b, out_pack = lax.optimization_barrier((stat, far_a, far_b, out_pack))
    out_far, out_near = cross_swap(out_pack), core_swap(out_pack)
    state = (acc, stat)
    far = [far_a, far_b, core_swap(far_a), core_swap(far_b)]
    *mixed_part, qb_rows, k_far, v_far = attn_fwd(
        meta, q_parts, far, (2, 3), heads, local, sizes, 4, state=state
    )
    *mixed_part, second, third, out_far, qb_rows = lax.optimization_barrier(
        (*mixed_part, hops[1], crossed[0], out_far, qb_rows)
    )
    hops[1], crossed[0] = second, third
    crossed.append(cross_dp(hops[1]))
    mixed = [mixed_part[0]] + [shift_col(mixed_part[k], -k) for k in range(1, cols_n)]

    out_packs = [out_pack, out_near, out_far, core_swap(out_far)]
    *mixed, third, crossed[1] = lax.optimization_barrier((*mixed, hops[1], crossed[1]))
    hops.append(shift_col(third, 1))
    crossed.append(cross_dp(hops[2]))
    packs = [pack]
    for hop, other in zip(hops, crossed):
        packs += [hop, other] if paired else [hop]
    hidden, hidden_low, normal1, inv1, out_full, vecs = project(meta, mixed, out_packs, tokens, sub_out)

    h_own, h_far, h_near = hidden_low, cross_swap(hidden_low), core_swap(hidden_low)
    h_near, h_far, packs[-1] = lax.optimization_barrier((h_near, h_far, packs[-1]))
    h_diag = core_swap(h_far)
    keep0, send0, act0, slope0 = ffn_fwd(meta, h_own, h_near, packs, units, units * cols_n)
    keep1, send1, act1, slope1 = ffn_fwd(meta, h_far, h_diag, packs, units, units * cols_n)
    far = (keep1 + core_swap(send1).astype(F32)).astype(BF)
    got_far = cross_swap(far)
    got_near = core_swap(send0)
    output, grad_resid2, grad_branch, sums2 = norm2(
        meta, hidden, keep0, got_near, got_far, cotangent, vecs
    )

    g_own, g_far, g_near = grad_branch, cross_swap(grad_branch), core_swap(grad_branch)
    keep0, send0, pre0 = ffn_bwd(meta, g_own, g_near, packs, slope0, units)
    g_far = after(g_far, send0)
    g_diag = core_swap(g_far)
    keep1, send1, pre1 = ffn_bwd(meta, g_far, g_diag, packs, slope1, units)
    far = (keep1 + core_swap(send1).astype(F32)).astype(BF)
    got_far = cross_swap(far)
    got_near = core_swap(send0)
    g_one, g_two, g_up_bias = ffn_grads(
        meta,
        (act0, act1),
        (pre0, pre1),
        (h_own, h_near, h_far, h_diag),
        (g_own, g_near, g_far, g_diag),
    )
    if paired:
        g_two = lax.ppermute(g_two, "dp", [(0, 1), (1, 0)])
    keep0 = after(keep0, g_one)
    grad_resid1, grad_attended, sums1, grad_mixed = norm1_back(
        keep0, got_near, got_far, grad_resid2, normal1, inv1, vecs, out_full
    )
    grad_mixed = [grad_mixed[0]] + [shift_col(grad_mixed[k], k) for k in range(1, cols_n)]

    out_keep, out_far, out_send, sums = out_grads(
        meta, mixed, grad_attended, sums1, sums2, g_up_bias, sub_out, rows_n
    )
    out_got = core_swap(out_send)
    out_got = after(out_got, grad_mixed[1])
    out_message = far_message(out_far, sums, out_got)
    out_got_far = cross_swap(out_message)
    messages = col_messages(
        g_one, g_two, out_keep, sums, out_got, out_got_far, sub_out, cols_n, paired
    )

    grads = after(grad_rows(mixed_part, grad_mixed, heads), out_message)
    dq = jnp.zeros((block_len, LANES), F32)
    *part3, dq = attn_bwd(1, qb_rows, grads, k_far, v_far, dq, heads, 4)
    got3 = [core_swap(part) for part in part3]
    dq = after(dq, messages[1])
    packed = shift_col(after(messages[1], dq), 1)
    *part2, dq = attn_bwd(0, qb_rows, grads, k_far, v_far, dq, heads, 4)
    far_sum = [(a.astype(F32) + b.astype(F32)).astype(BF) for a, b in zip(part2, got3)]
    far_sum = jnp.concatenate(far_sum)
    far_got = cross_swap(far_sum)
    packed = sum_messages([messages[2], packed])
    dq = after(dq, far_sum, packed)
    packed = shift_col(after(packed, dq), 1)
    *part1, dq = attn_bwd(1, qb_rows, grads, k_near, v_near, dq, heads, 4)
    got1 = [core_swap(part) for part in part1]
    packed = sum_messages([messages[3], packed])
    dq = after(dq, packed)
    packed = shift_col(after(packed, dq), 1)
    *part0, dq = attn_bwd(0, qb_rows, grads, k_near, v_near, dq, heads, C4)

    d_blocks, back = join_grads(part0, got1, far_got, dq, w_qkv, cols_n, scale)
    ring = [shift_col(back[1], 1)]

    d_blocks = [after(d_blocks[0], packed), *d_blocks[1:]]
    own, far, send, send_far = qkv_grads(meta, x_blocks, d_blocks, feat)
    packed = sum_messages([after(messages[0], back[1]), packed])
    got, got_far = core_swap(send), core_swap(send_far)
    ring[0], got, got_far, packed = lax.optimization_barrier((ring[0], got, got_far, packed))
    for step in range(2, cols_n + 1):
        total = back[step % cols_n] + ring[-1].astype(F32)
        if step < cols_n:
            ring.append(shift_col(total.astype(BF), 1))
    grad_tokens = grad_resid1 + total
    if paired:
        other = lax.ppermute(packed, "dp", [(0, 1), (1, 0)])
    else:
        other = lax.psum(packed.astype(F32), "dp") - packed.astype(F32)
    g_bias = own[feat] + own[feat + 1]

    def with_bias(block, bias):
        hi = lax.reduce_precision(bias, 8, 7)
        rows = jnp.pad(jnp.stack([hi, bias - hi]), ((0, 14), (0, 0)))
        return jnp.concatenate([block, rows]).astype(BF)

    def bias_of(got):
        return got[-16].astype(F32) + got[-15].astype(F32)

    g_bias = g_bias + bias_of(got)
    mine = own[:feat] + got[:feat].astype(F32)
    got_x = got = cross_swap(with_bias(far + got_far.astype(F32), g_bias))
    g_bias = g_bias + bias_of(got)
    mine = mine + got[:feat].astype(F32)
    if paired:
        got = lax.ppermute(after(with_bias(mine, g_bias), ring[0]), "dp", [(0, 1), (1, 0)])
        g_bias = g_bias + bias_of(got)
        g_qkv = mine + got[:feat].astype(F32)
    else:
        g_bias, g_qkv = lax.psum((g_bias, mine), "dp")
    g_qkv = g_qkv.astype(BF).reshape(cols_n, sub, 3 * hw)
    pieces = []
    for k in range(cols_n):
        piece = lax.dynamic_index_in_dim(g_qkv, (z + k) % cols_n, 0, keepdims=False)
        pieces.append(shift_col(piece, k) if k else piece)
    g_qkv = spread(meta, pieces)
    other = after(other, ring[1], got_x)
    *g_up, g_down_weight, g_out_weight, sums = finish(
        meta, packed, other, rows_n, units, sub_out, paired
    )
    g_up[1] = core_swap(g_up[1])
    g_up[2] = cross_swap(g_up[2])
    g_up[3] = lax.ppermute(g_up[3], "row", [(i, i ^ 3) for i in range(rows_n)])
    g_up_weight = up_grads(meta, g_up)
    vec_out = lax.dynamic_slice_in_dim(sums[:6], r * feat, feat, 1)
    g_up_bias = lax.dynamic_index_in_dim(sums[8 : 8 + cols_n], z, 0, keepdims=False)

    return (
        output,
        grad_tokens,
        g_qkv[0],
        g_qkv[1],
        g_qkv[2],
        g_bias[:hw],
        g_bias[2 * hw :],
        g_out_weight,
        vec_out[2],
        vec_out[0],
        vec_out[1],
        g_up_weight,
        g_up_bias,
        g_down_weight,
        vec_out[5],
        vec_out[3],
        vec_out[4],
    )


def solution(mesh):
    token_spec = P(("dp", "col", "row"), None)
    placed = (
        token_spec,
        token_spec,
        P("dp"),
        P(("row", "col"), None),
        P(("row", "col"), None),
        P(("row", "col"), None),
        P("col"),
        P("col"),
        P(("col", "row"), None),
        P("row"),
        P("row"),
        P("row"),
        P("row", "col"),
        P("col"),
        P(("col", "row"), None),
        P("row"),
        P("row"),
        P("row"),
    )
    return jax.shard_map(
        per_device,
        mesh=mesh,
        in_specs=placed,
        out_specs=(token_spec, token_spec) + placed[3:],
        check_vma=False,
    )
```

```python
import functools
import math

import jax
import jax.numpy as jnp
from jax import lax
from jax.experimental import pallas as pl
from jax.experimental.pallas import tpu as pltpu
from jax.sharding import PartitionSpec as P

HD = 64
LANES = 256
EPS = 1e-05
BF = jnp.bfloat16
F32 = jnp.float32
VMEM_BYTES = 60 * 1024 * 1024
TURNED = HD + 16
SMALL_BYTES = 24 * 1024 * 1024
ATTN_BYTES = 36 * 1024 * 1024
NEAR_COST = 4
C4 = 6


def nn(a, b):
    return jnp.dot(a, b, preferred_element_type=F32)


def tn(a, b):
    return lax.dot_general(a, b, (((0,), (0,)), ((), ())), preferred_element_type=F32)


def nt(a, b):
    return lax.dot_general(a, b, (((1,), (1,)), ((), ())), preferred_element_type=F32)


def cost(us):
    return pl.CostEstimate(flops=int(us * 0.6e9), bytes_accessed=1000, transcendentals=0)


def head_lanes(shape, head, width):
    lane = lax.broadcasted_iota(jnp.int32, shape, 1)
    mine = (lane >= head * HD) & (lane < (head + 1) * HD)
    return mine | (lane == width) | ((lane >= width + 1 + 3 * head) & (lane < width + 4 + 3 * head))


def three_parts(x):
    hi = x.astype(BF).astype(F32)
    mid = (x - hi).astype(BF).astype(F32)
    return hi, mid, x - hi - mid


def tail_rows(parts, ones, n):
    row = lax.broadcasted_iota(jnp.int32, (n, parts[0].shape[1]), 0)
    out = jnp.where(row == 0, ones, 0.0)
    for head, value in enumerate(parts):
        for i, piece in enumerate(three_parts(value)):
            out = jnp.where(row == 1 + 3 * head + i, piece, out)
    return out


def widen_keys(kv, owner, base, meta, keys_out, values_out, turned, at, width, shift, sizes):
    n = kv.shape[0]
    rows_n, cols_n = sizes
    keys_out[at : at + n, :width] = kv[:, :width]
    values_out[at : at + n, :width] = kv[:, width:]
    shape = (n, LANES - width)
    t = lax.broadcasted_iota(jnp.int32, shape, 0) + base
    lane = lax.broadcasted_iota(jnp.int32, shape, 1)
    source = meta[3] - (t >> shift)
    source = jnp.where(source < 0, source + cols_n, source)
    position = ((source * rows_n + owner) << shift) + (t & ((1 << shift) - 1))
    mask = jnp.where(lane == 0, jnp.where(position >= meta[0], -1e30, 0.0), 1.0)
    keys_out[at : at + n, width:] = mask.astype(BF)
    values_out[at : at + n, width:] = jnp.ones(shape, BF)
    flat = values_out[at : at + n, :].T
    for head in range(width // HD):
        first = head * TURNED
        turned[first : first + HD, at : at + n] = flat[head * HD : (head + 1) * HD, :]
        turned[first + HD : first + TURNED, at : at + n] = jnp.ones((TURNED - HD, n), BF)


def attn_fwd_kernel(*refs, heads, first, pair, shift, sizes, chunk, blocks, parts):
    meta, *refs = refs
    q_refs, refs = refs[:parts], refs[parts:]
    kvs, refs = refs[: 2 * parts], refs[2 * parts :]
    if first:
        acc_out, stat_out, k_out, v_out, turned = refs
    else:
        acc_in, stat_in = refs[:2]
        outs = refs[2 : 2 + blocks]
        qb_ref, k_out, v_out, turned = refs[2 + blocks :]
    width = heads * HD
    keys = k_out.shape[0]
    at = 0
    for i, ref in enumerate(kvs):
        base = at % (keys // 2)
        owner = meta[1] ^ pair[i // parts]
        widen_keys(ref[...], owner, base, meta, k_out, v_out, turned, at, width, shift, sizes)
        at += ref.shape[0]
    q = jnp.concatenate([ref[...] for ref in q_refs], axis=0)
    rows = q.shape[0]
    slot = lax.broadcasted_iota(jnp.int32, (16, rows), 0)
    stat = jnp.zeros((16, rows), F32)
    logs = []
    for head in range(heads):
        qh = jnp.where(head_lanes(q.shape, head, width), q, jnp.zeros_like(q))
        scores = [nt(k_out[i : i + chunk, :], qh) for i in range(0, keys, chunk)]
        peak = functools.reduce(
            jnp.maximum, [jnp.max(s, axis=0, keepdims=True) for s in scores]
        )
        if not first:
            old = stat_in[head : head + 1, :]
            peak = jnp.maximum(peak, old)
        acc = None
        for i, s in enumerate(scores):
            p = jnp.exp(s - peak).astype(BF)
            at = head * TURNED
            part = nn(turned[at : at + TURNED, i * chunk : (i + 1) * chunk], p)
            acc = part if acc is None else acc + part
        total = acc[HD : HD + 1]
        mine = slice(head * HD, (head + 1) * HD)
        if first:
            acc_out[mine, :] = acc[:HD]
            stat = jnp.where(slot == head, peak, stat)
            stat = jnp.where(slot == head + 8, total, stat)
        else:
            keep = jnp.exp(old - peak)
            total = total + stat_in[head + 8 : head + 9, :] * keep
            out = ((acc[:HD] + acc_in[mine, :] * keep) * (1.0 / total)).astype(BF)
            each = rows // blocks
            for b in range(blocks):
                outs[b][mine, :] = out[:, b * each : (b + 1) * each]
            logs.append(-(peak + jnp.log(total)))
    if first:
        stat_out[...] = stat
    else:
        qb_ref[:, :width] = q[:, :width]
        qb_ref[:, width:] = tail_rows(logs, 1.0, LANES - width).T.astype(BF)


def attn_fwd(meta, q, kvs, pair, heads, local, sizes, us, state=None, chunk=512):
    rows = sum(part.shape[0] for part in q)
    half = sum(kv.shape[0] for kv in kvs) // 2
    width = kvs[0].shape[1] // 2
    first = state is None
    blocks = rows // local
    vmem = pl.BlockSpec(memory_space=pltpu.VMEM)
    args = [meta, *q, *kvs]
    if first:
        out_shape = [jax.ShapeDtypeStruct((width, rows), F32), jax.ShapeDtypeStruct((16, rows), F32)]
    else:
        args += list(state)
        out_shape = [jax.ShapeDtypeStruct((width, local), BF)] * blocks
        out_shape += [jax.ShapeDtypeStruct((rows, LANES), BF)]
    out_shape += [jax.ShapeDtypeStruct((2 * half, LANES), BF)] * 2
    return pl.pallas_call(
        functools.partial(
            attn_fwd_kernel,
            heads=heads,
            first=first,
            pair=pair,
            shift=local.bit_length() - 1,
            sizes=sizes,
            chunk=chunk,
            blocks=blocks,
            parts=len(q),
        ),
        in_specs=[pl.BlockSpec(memory_space=pltpu.SMEM)] + [vmem] * (len(args) - 1),
        out_specs=[vmem] * len(out_shape),
        out_shape=out_shape,
        scratch_shapes=[pltpu.VMEM((heads * TURNED, 2 * half), BF)],
        compiler_params=pltpu.CompilerParams(vmem_limit_bytes=ATTN_BYTES),
        cost_estimate=cost(us),
        name="attn_fwd_near" if first else "attn_fwd_far",
    )(*args)


def grad_rows_kernel(*refs, heads, blocks):
    outs, grads, wide = refs[:blocks], refs[blocks : 2 * blocks], refs[2 * blocks]
    width = heads * HD
    for b in range(blocks):
        g = grads[b][...].astype(F32)
        prod = g * outs[b][...].astype(F32)
        each = g.shape[1]
        parts = [
            -jnp.sum(prod[head * HD : (head + 1) * HD], axis=0, keepdims=True) for head in range(heads)
        ]
        tall = jnp.concatenate([g, tail_rows(parts, 0.0, LANES - width)], axis=0)
        wide[b * each : (b + 1) * each, :] = tall.T.astype(BF)


def grad_rows(outs, grads, heads):
    each = outs[0].shape[1]
    return small_call(
        functools.partial(grad_rows_kernel, heads=heads, blocks=len(outs)),
        jax.ShapeDtypeStruct((each * len(outs), LANES), BF),
        "grad_rows",
    )(*outs, *grads)


def attn_bwd_kernel(at_ref, q_ref, g_ref, k_ref, v_ref, dq_in, *refs, heads, block, pieces):
    outs, (dq_out, dk, dv) = refs[:pieces], refs[pieces:]
    width = heads * HD
    half = dk.shape[0]
    keys = pl.ds(pl.multiple_of(at_ref[0] * half, half), half)
    dk[...] = jnp.zeros_like(dk)
    dv[...] = jnp.zeros_like(dv)

    def step(i, carry):
        at = pl.ds(pl.multiple_of(i * block, block), block)
        q_all = q_ref[at, :]
        g_all = g_ref[at, :]
        k = k_ref[keys, :]
        dq = jnp.zeros((block, LANES), F32)
        for head in range(heads):
            mine = head_lanes((block, LANES), head, width)
            q = jnp.where(mine, q_all, jnp.zeros_like(q_all))
            g = jnp.where(mine, g_all, jnp.zeros_like(g_all))
            p = jnp.exp(nt(k, q))
            ds = (p * nt(v_ref[keys, :], g)).astype(BF)
            dv[...] += nn(p.astype(BF), g)
            dk[...] += nn(ds, q)
            dq = jnp.where(mine, tn(ds, k), dq)
        dq_out[at, :] = dq_in[at, :] + dq
        return carry

    lax.fori_loop(0, q_ref.shape[0] // block, step, 0)
    each = outs[0].shape[0]
    for i, out in enumerate(outs):
        at = slice(i * each, (i + 1) * each)
        out[:, :width] = dk[at, :width].astype(out.dtype)
        out[:, width:] = dv[at, :width].astype(out.dtype)


def attn_bwd(at, q, g, k, v, dq, heads, us, pieces=2, block=1024):
    rows = q.shape[0]
    half = k.shape[0] // 2
    width = heads * HD
    vmem = pl.BlockSpec(memory_space=pltpu.VMEM)
    out_shape = [jax.ShapeDtypeStruct((half // pieces, 2 * width), BF)] * pieces
    return pl.pallas_call(
        functools.partial(attn_bwd_kernel, heads=heads, block=block, pieces=pieces),
        in_specs=[pl.BlockSpec(memory_space=pltpu.SMEM)] + [vmem] * 5,
        out_specs=[vmem] * (pieces + 1),
        out_shape=out_shape + [jax.ShapeDtypeStruct((rows, LANES), F32)],
        scratch_shapes=[pltpu.VMEM((half, LANES), F32)] * 2,
        compiler_params=pltpu.CompilerParams(vmem_limit_bytes=ATTN_BYTES),
        cost_estimate=cost(us),
        name="attn_bwd",
    )(jnp.full((1,), at, jnp.int32), q, g, k, v, dq)


def small_call(kernel, out_shape, name, scratch=(), us=1.4):
    return pl.pallas_call(
        kernel,
        out_shape=out_shape,
        scratch_shapes=scratch,
        compiler_params=pltpu.CompilerParams(vmem_limit_bytes=SMALL_BYTES),
        cost_estimate=cost(us),
        name=name,
    )


def meta_call(kernel, args, out_shape, name, scratch=(), us=1.2):
    vmem = pl.BlockSpec(memory_space=pltpu.VMEM)
    return pl.pallas_call(
        kernel,
        in_specs=[pl.BlockSpec(memory_space=pltpu.SMEM)] + [vmem] * (len(args) - 1),
        out_specs=[vmem] * len(out_shape),
        out_shape=out_shape,
        scratch_shapes=scratch,
        compiler_params=pltpu.CompilerParams(vmem_limit_bytes=SMALL_BYTES),
        cost_estimate=cost(us),
        name=name,
    )(*args)


def row_mean(x):
    return jnp.mean(x, axis=1, keepdims=True)


def col_sum(x):
    return jnp.sum(x, axis=0, keepdims=True)


def norm_forward(resid, gain, shift):
    centered = resid - row_mean(resid)
    inv = lax.rsqrt(row_mean(centered * centered) + EPS)
    normal = centered * inv
    return normal * gain + shift, normal, inv


def norm_backward(grad_out, normal, inv, gain):
    scaled = grad_out * gain
    return inv * (scaled - row_mean(scaled) - normal * row_mean(scaled * normal))


def project_qkv_kernel(meta, *refs, n, blocks, last, rows_n, cols_n, feat, hw, scale):
    x, ws, bias_ref = refs[:n], refs[n : n + rows_n], refs[n + rows_n]
    if last:
        vec_ref, q_ref, kv_ref, w_out, pack_ref, w_all = refs[n + rows_n + 1 :]
    else:
        q_ref, kv_ref, w_all = refs[n + rows_n + 1 :]
    each = feat // cols_n
    for k in range(rows_n):
        for m in range(cols_n):
            source = meta[3] - m
            source = jnp.where(source < 0, source + cols_n, source)
            at = pl.multiple_of((meta[1] ^ k) * feat + source * each, each)
            w_all[pl.ds(at, each), :] = ws[k][m * each : (m + 1) * each, :]
    w = w_all[...]
    each = q_ref.shape[0] // len(blocks)
    for i, k in enumerate(blocks):
        at = slice(i * each, (i + 1) * each)
        out = nn(x[k][:each, :], w) + bias_ref[0:1, :]
        q_ref[at, :hw] = (out[:, :hw].astype(BF).astype(F32) * scale).astype(BF)
        lane = lax.broadcasted_iota(jnp.int32, (each, LANES - hw), 1)
        q_ref[at, hw:] = jnp.where(lane == 0, 1.0, 0.0).astype(BF)
        kv_ref[at, :] = out[:, hw:].astype(BF)
    if last:
        w_out[...] = w.T
        more = x[0].shape[0] - each
        for k in range(n):
            pack_ref[k * more : (k + 1) * more, :] = x[k][each:, :]
        pack_ref[n * more :, :] = vec_ref[...]


def project_qkv(meta, x, blocks, cols_n, ws, bias, local, scale, vecs=None):
    feat, wide = ws[0].shape
    hw = wide // 3
    rows = local * len(blocks)
    shapes = [
        jax.ShapeDtypeStruct((rows, LANES), BF),
        jax.ShapeDtypeStruct((rows, 2 * hw), BF),
    ]
    args = [meta, *x, *ws, bias]
    if vecs is not None:
        args.append(vecs)
        more = (x[0].shape[0] - local) * len(x) + vecs.shape[0]
        shapes.append(jax.ShapeDtypeStruct((wide, feat * len(ws)), BF))
        shapes.append(jax.ShapeDtypeStruct((more, vecs.shape[1]), BF))
    return meta_call(
        functools.partial(
            project_qkv_kernel,
            n=len(x),
            blocks=blocks,
            last=vecs is not None,
            rows_n=len(ws),
            cols_n=cols_n,
            feat=feat,
            hw=hw,
            scale=scale,
        ),
        args,
        shapes,
        "project_qkv",
        scratch=[pltpu.VMEM((feat * len(ws), wide), BF)],
    )


def project_kernel(meta, *refs, n, rows_n, sub, feat):
    mixed, packs = refs[:n], refs[n : n + rows_n]
    x_ref, hid_ref, low_ref, normal_ref, inv_ref, w_ref, vec_ref = refs[n + rows_n :]
    r = meta[1]
    for k in range(rows_n):
        at = pl.multiple_of((r ^ k) * sub, sub)
        for i in range(n):
            w_ref[i, pl.ds(at, sub), :] = packs[k][((n - i) % n) * sub : ((n - i) % n + 1) * sub, :]
    values = []
    for k in range(rows_n):
        part = packs[k][n * sub : n * sub + 32, :feat].astype(F32)
        values.append(part[0:8] + part[8:16] + part[16:24])
    pieces = []
    for owner in range(rows_n):
        value = values[0]
        for k in range(1, rows_n):
            value = jnp.where((r ^ k) == owner, values[k], value)
        pieces.append(value)
    vecs = jnp.concatenate(pieces, axis=1)
    vec_ref[...] = vecs
    total = x_ref[...].astype(F32) + vecs[0:1, :]
    for j in range(n):
        total = total + tn(mixed[j][...], w_ref[j])
    hidden, normal, inv = norm_forward(total, vecs[1:2, :], vecs[2:3, :])
    hid_ref[...] = hidden
    low_ref[...] = hidden.astype(BF)
    normal_ref[...] = normal
    inv_ref[...] = jnp.broadcast_to(inv, inv_ref.shape)


def project(meta, mixed, packs, x, sub):
    rows, width = x.shape
    feat = width // len(packs)
    return meta_call(
        functools.partial(
            project_kernel, n=len(mixed), rows_n=len(packs), sub=sub, feat=feat
        ),
        [meta, *mixed, *packs, x],
        [
            jax.ShapeDtypeStruct((rows, width), F32),
            jax.ShapeDtypeStruct((rows, width), BF),
            jax.ShapeDtypeStruct((rows, width), F32),
            jax.ShapeDtypeStruct((rows, 128), F32),
            jax.ShapeDtypeStruct((len(mixed), sub * len(packs), width), BF),
            jax.ShapeDtypeStruct((8, width), F32),
        ],
        "project_norm1",
    )


def weight_rows(meta, packs, units, down):
    size = packs[0].shape[0] // 2
    at = size if down else 0
    values = [packs[0][at : at + units, :]]
    rest = packs[1:]
    if rest[0].shape[0] > size:
        return values + [ref[at : at + units, :] for ref in rest]
    mine = (meta[4] == 0) != down
    for own, other in zip(rest[::2], rest[1::2]):
        values.append(jnp.where(mine, own[:units, :].astype(F32), other[:units, :].astype(F32)).astype(BF))
    return values


def bias_rows(meta, packs, units):
    size = packs[0].shape[0] // 2
    at = slice(units, units + 16)
    values = [packs[0][at, :].astype(F32)]
    rest = packs[1:]
    if rest[0].shape[0] > size:
        values += [ref[at, :].astype(F32) for ref in rest]
    else:
        for own, other in zip(rest[::2], rest[1::2]):
            values.append(jnp.where(meta[4] == 0, own[at, :].astype(F32), other[at, :].astype(F32)))
    return jnp.concatenate([v[0:1, :units] + v[1:2, :units] + v[2:3, :units] for v in values], axis=1)


def ffn_fwd_kernel(meta, *refs, n, units):
    h0, h1 = refs[:2]
    packs = refs[2 : 2 + n]
    keep_ref, send_ref, act_ref, slope_ref = refs[2 + n :]
    rows = h0.shape[0]
    h = jnp.concatenate([h0[...], h1[...]], axis=0)
    up = jnp.concatenate(weight_rows(meta, packs, units, False), axis=0)
    x = nt(h, up) + bias_rows(meta, packs, units)
    cdf = 0.5 * (1.0 + lax.erf(x * math.sqrt(0.5)))
    act = (x * cdf).astype(BF)
    act_ref[...] = act
    slope = cdf + x * (math.sqrt(0.5 / math.pi) * jnp.exp(-0.5 * x * x))
    slope_ref[...] = slope.astype(BF)
    out = nn(act, jnp.concatenate(weight_rows(meta, packs, units, True), axis=0))
    keep_ref[...] = out[:rows]
    send_ref[...] = out[rows:].astype(BF)


def ffn_fwd(meta, h0, h1, packs, units, wide):
    rows, width = h0.shape
    return meta_call(
        functools.partial(ffn_fwd_kernel, n=len(packs), units=units),
        [meta, h0, h1, *packs],
        [
            jax.ShapeDtypeStruct((rows, width), F32),
            jax.ShapeDtypeStruct((rows, width), BF),
            jax.ShapeDtypeStruct((2 * rows, wide), BF),
            jax.ShapeDtypeStruct((2 * rows, wide), BF),
        ],
        "ffn_fwd",
        us=1.4,
    )


def ffn_bwd_kernel(meta, *refs, n, units):
    g0, g1 = refs[:2]
    packs = refs[2 : 2 + n]
    slope_ref, keep_ref, send_ref, pre_ref = refs[2 + n :]
    rows = g0.shape[0]
    g = jnp.concatenate([g0[...], g1[...]], axis=0)
    down = jnp.concatenate(weight_rows(meta, packs, units, True), axis=0)
    pre = (nt(g, down) * slope_ref[...].astype(F32)).astype(BF)
    pre_ref[...] = pre
    out = nn(pre, jnp.concatenate(weight_rows(meta, packs, units, False), axis=0))
    keep_ref[...] = out[:rows]
    send_ref[...] = out[rows:].astype(BF)


def ffn_bwd(meta, g0, g1, packs, slope, units):
    rows, width = g0.shape
    return meta_call(
        functools.partial(ffn_bwd_kernel, n=len(packs), units=units),
        [meta, g0, g1, *packs, slope],
        [
            jax.ShapeDtypeStruct((rows, width), F32),
            jax.ShapeDtypeStruct((rows, width), BF),
            jax.ShapeDtypeStruct(slope.shape, BF),
        ],
        "ffn_bwd",
        us=1.4,
    )


def ffn_grads_kernel(meta, *refs):
    act0, act1, pre0, pre1 = refs[:4]
    h = jnp.concatenate([ref[...] for ref in refs[4:8]], axis=0)
    g = jnp.concatenate([ref[...] for ref in refs[8:12]], axis=0)
    keep_ref, send_ref, bias_ref = refs[12:]
    pre = jnp.concatenate([pre0[...], pre1[...]], axis=0)
    act = jnp.concatenate([act0[...], act1[...]], axis=0)
    g_up = tn(pre, h).astype(BF)
    g_down = tn(act, g).astype(BF)
    first = meta[4] == 0

    @pl.when(first)
    def _():
        keep_ref[...] = g_up
        send_ref[...] = g_down

    @pl.when(jnp.logical_not(first))
    def _():
        keep_ref[...] = g_down
        send_ref[...] = g_up

    bias_ref[...] = jnp.broadcast_to(col_sum(pre.astype(F32)), bias_ref.shape)


def ffn_grads(meta, acts, pres, hiddens, grads):
    width = hiddens[0].shape[1]
    wide = acts[0].shape[1]
    return meta_call(
        ffn_grads_kernel,
        [meta, *acts, *pres, *hiddens, *grads],
        [
            jax.ShapeDtypeStruct((wide, width), BF),
            jax.ShapeDtypeStruct((wide, width), BF),
            jax.ShapeDtypeStruct((8, wide), F32),
        ],
        "ffn_grads",
    )


def norm2_kernel(
    meta, hid_ref, keep_ref, near_ref, far_ref, cot_ref, vec_ref, out_ref, grad_ref, low_ref, sum_ref
):
    branch = keep_ref[...] + near_ref[...].astype(F32) + far_ref[...].astype(F32) + vec_ref[3:4, :]
    gain = vec_ref[4:5, :]
    normed, normal, inv = norm_forward(hid_ref[...] + branch, gain, vec_ref[5:6, :])
    row = lax.broadcasted_iota(jnp.int32, (out_ref.shape[0], 1), 0)
    valid = (meta[2] + row < meta[0]).astype(F32)
    out_ref[...] = (normed * valid).astype(BF)
    grad_y = cot_ref[...].astype(F32) * valid
    grad = norm_backward(grad_y, normal, inv, gain)
    grad_ref[...] = grad
    low = grad.astype(BF)
    low_ref[...] = low
    sum_ref[...] = jnp.zeros_like(sum_ref)
    sum_ref[0:1, :] = col_sum(grad_y * normal)
    sum_ref[1:2, :] = col_sum(grad_y)
    sum_ref[2:3, :] = col_sum(low.astype(F32))


def norm2(meta, hidden, keep, near, far, cot, vecs):
    rows, width = hidden.shape
    shapes = [
        jax.ShapeDtypeStruct((rows, width), BF),
        jax.ShapeDtypeStruct((rows, width), F32),
        jax.ShapeDtypeStruct((rows, width), BF),
        jax.ShapeDtypeStruct((8, width), F32),
    ]
    return meta_call(norm2_kernel, [meta, hidden, keep, near, far, cot, vecs], shapes, "norm2_both")


def norm1_back_kernel(
    keep_ref, near_ref, far_ref, add_ref, normal_ref, inv_ref, vec_ref, w_ref, out_ref, low_ref, sum_ref, *mixed
):
    grad = keep_ref[...] + near_ref[...].astype(F32) + far_ref[...].astype(F32) + add_ref[...]
    normal = normal_ref[...]
    resid = norm_backward(grad, normal, inv_ref[:, 0:1], vec_ref[1:2, :])
    out_ref[...] = resid
    low = resid.astype(BF)
    low_ref[...] = low
    for j, ref in enumerate(mixed):
        ref[...] = nt(w_ref[j], low).astype(BF)
    sum_ref[...] = jnp.zeros_like(sum_ref)
    sum_ref[0:1, :] = col_sum(grad * normal)
    sum_ref[1:2, :] = col_sum(grad)
    sum_ref[2:3, :] = col_sum(low.astype(F32))


def norm1_back(keep, near, far, add, normal, inv, vecs, w):
    rows, width = add.shape
    out = small_call(
        norm1_back_kernel,
        [
            jax.ShapeDtypeStruct((rows, width), F32),
            jax.ShapeDtypeStruct((rows, width), BF),
            jax.ShapeDtypeStruct((8, width), F32),
        ]
        + [jax.ShapeDtypeStruct((w.shape[1], rows), BF)] * w.shape[0],
        "norm1_back",
    )(keep, near, far, add, normal, inv, vecs, w)
    return out[0], out[1], out[2], out[3:]


def two_parts(x):
    hi = x.astype(BF).astype(F32)
    return jnp.concatenate([hi, x - hi], axis=0).astype(BF)


def both_parts(rows):
    n = rows.shape[0] // 2
    return rows[:n].astype(F32) + rows[n:].astype(F32)


def out_grads_kernel(meta, *refs, n, rows_n, sub):
    mixed, grad, s1, s2, bias = refs[:n], *refs[n : n + 4]
    keep, far, send, sums, total = refs[n + 4 :]
    g = grad[...]
    for j in range(n):
        total[j] = nn(mixed[j][...], g)
    count = n * sub
    for j in range(n):
        at = slice(j * sub, (j + 1) * sub)

        def rows(k):
            return total[j, pl.ds(pl.multiple_of((meta[1] ^ k) * sub, sub), sub), :]

        keep[at, :] = rows(0)
        far[at, :] = rows(2)
        send[at, :] = rows(1).astype(BF)
        send[count + j * sub : count + (j + 1) * sub, :] = rows(3).astype(BF)
    sums[...] = jnp.zeros_like(sums)
    sums[0:3, :] = s1[0:3, :]
    sums[3:6, :] = s2[0:3, :]
    units = bias.shape[1] // n
    for j in range(n):
        away = meta[3] - j
        away = jnp.where(away < 0, away + n, away)
        value = bias[0:1, :units]
        for k in range(1, n):
            value = jnp.where(away == k, bias[0:1, k * units : (k + 1) * units], value)
        zero = jnp.zeros_like(value)
        row = [jnp.where(meta[1] == owner, value, zero) for owner in range(rows_n)]
        sums[8 + j : 9 + j, :] = jnp.concatenate(row, axis=1)
    send[2 * count :, :] = two_parts(sums[...])


def out_grads(meta, mixed, grad, s1, s2, bias, sub, rows_n):
    n, heads, width = len(mixed), mixed[0].shape[0], grad.shape[1]
    shapes = [
        jax.ShapeDtypeStruct((n * sub, width), F32),
        jax.ShapeDtypeStruct((n * sub, width), F32),
        jax.ShapeDtypeStruct((2 * n * sub + 32, width), BF),
        jax.ShapeDtypeStruct((16, width), F32),
    ]
    return meta_call(
        functools.partial(out_grads_kernel, n=n, sub=sub, rows_n=rows_n),
        [meta, *mixed, grad, s1, s2, bias],
        shapes,
        "out_grads",
        scratch=[pltpu.VMEM((n, heads, width), F32)],
    )


def far_message_kernel(far, sums, got, out):
    n = far.shape[0]
    out[:n, :] = (far[...] + got[n : 2 * n, :].astype(F32)).astype(BF)
    out[n:, :] = two_parts(sums[...] + both_parts(got[2 * n :, :]))


def far_message(far, sums, got):
    n, width = far.shape
    shape = jax.ShapeDtypeStruct((n + 32, width), BF)
    return small_call(far_message_kernel, shape, "far_message", us=0.7)(far, sums, got)


def col_messages_kernel(*refs, n, sub, added):
    (one, two, keep, sums, near, far), outs = refs[:6], refs[6:]
    count = n * sub
    both = sums[...] + both_parts(near[2 * count :, :]) + both_parts(far[count:, :])
    parts = two_parts(both)
    own = keep[...] + near[:count, :].astype(F32) + far[:count, :].astype(F32)
    units = one.shape[0] // n
    size = units if added else 2 * units
    for k in range(n):
        j = (n - k) % n
        at = slice(k * units, (k + 1) * units)
        if added:
            outs[k][:units, :] = (one[at, :].astype(F32) + two[at, :].astype(F32)).astype(BF)
        else:
            outs[k][:units, :] = one[at, :]
            outs[k][units:size, :] = two[at, :]
        outs[k][size : size + sub, :] = own[j * sub : (j + 1) * sub].astype(BF)
        outs[k][size + sub :, :] = parts


def col_messages(one, two, keep, sums, near, far, sub, n, added):
    rows, width = one.shape
    size = rows // n * (1 if added else 2)
    shapes = [jax.ShapeDtypeStruct((size + sub + 32, width), BF)] * n
    return small_call(
        functools.partial(col_messages_kernel, n=n, sub=sub, added=added), shapes, "col_messages"
    )(one, two, keep, sums, near, far)


def sum_messages_kernel(*refs):
    refs, out = refs[:-1], refs[-1]
    n = out.shape[0] - 32
    total = refs[0][:n, :].astype(F32)
    sums = both_parts(refs[0][n:, :])
    for ref in refs[1:]:
        total = total + ref[:n, :].astype(F32)
        sums = sums + both_parts(ref[n:, :])
    out[:n, :] = total.astype(BF)
    out[n:, :] = two_parts(sums)


def sum_messages(messages):
    shape = jax.ShapeDtypeStruct(messages[0].shape, BF)
    return small_call(sum_messages_kernel, shape, "sum_messages", us=0.7)(*messages)


def finish_kernel(meta, own, other, *refs, rows_n, units, sub, paired):
    ups, (down, out, sums) = refs[:rows_n], refs[rows_n:]
    size = own.shape[0] - sub - 32
    a = own[:size, :].astype(F32)
    b = other[:size, :].astype(F32)
    if paired:
        first = meta[4] == 0
        up = jnp.where(first, a, b)
        down[...] = jnp.where(first, b, a)
    else:
        up = a[:units] + b[:units]
        down[...] = a[units:] + b[units:]
    feat = up.shape[1] // rows_n
    pieces = [up[:, k * feat : (k + 1) * feat] for k in range(rows_n)]
    for k in range(rows_n):
        value = pieces[0]
        for owner in range(1, rows_n):
            value = jnp.where((meta[1] ^ k) == owner, pieces[owner], value)
        ups[k][...] = value.T.astype(BF)
    at = size + sub
    out[...] = own[size:at, :].astype(F32) + other[size:at, :].astype(F32)
    sums[...] = both_parts(own[at:, :]) + both_parts(other[at:, :])


def finish(meta, own, other, rows_n, units, sub, paired):
    width = own.shape[1]
    shapes = [jax.ShapeDtypeStruct((width // rows_n, units), BF)] * rows_n
    shapes += [jax.ShapeDtypeStruct((n, width), F32) for n in (units, sub, 16)]
    return meta_call(
        functools.partial(finish_kernel, rows_n=rows_n, units=units, sub=sub, paired=paired),
        [meta, own, other],
        shapes,
        "finish_grads",
    )


def up_grads_kernel(meta, *refs, n):
    pieces, out = refs[:n], refs[n]
    units = pieces[0].shape[1]
    values = [ref[...].astype(F32) for ref in pieces]
    for owner in range(n):
        value = values[0]
        for k in range(1, n):
            value = jnp.where((meta[1] ^ k) == owner, values[k], value)
        out[:, owner * units : (owner + 1) * units] = value


def up_grads(meta, pieces):
    feat, units = pieces[0].shape
    return meta_call(
        functools.partial(up_grads_kernel, n=len(pieces)),
        [meta, *pieces],
        [jax.ShapeDtypeStruct((feat, units * len(pieces)), F32)],
        "up_grads",
    )[0]


def join_kernel(keep0, keep1, near0, near1, far, dq, w_ref, *outs, scale, hw):
    n = len(outs) // 2
    each = outs[0].shape[0]
    half = keep0.shape[0]
    for k in range(n):
        at = slice(k * each, (k + 1) * each)
        inside = slice(at.start % half, at.start % half + each)
        keep, near = ((keep0, near0), (keep1, near1))[at.start // half]
        kv = keep[inside, :].astype(F32) + near[inside, :].astype(F32) + far[at, :].astype(F32)
        d = jnp.concatenate([(dq[at, :hw] * scale).astype(BF), kv.astype(BF)], axis=1)
        outs[k][...] = d
        outs[n + k][...] = nn(d, w_ref[...]).astype(outs[n + k].dtype)


def join_grads(keep, near, far, dq, w, n, scale):
    rows = dq.shape[0]
    wide, width = w.shape
    shapes = [jax.ShapeDtypeStruct((rows // n, wide), BF)] * n
    shapes += [jax.ShapeDtypeStruct((rows // n, width), BF)] * n
    kernel = functools.partial(join_kernel, scale=scale, hw=wide // 3)
    out = small_call(kernel, shapes, "join_grads")(*keep, *near, far, dq, w)
    return out[:n], out[n:]


def qkv_grads_kernel(meta, *refs, n, feat):
    x, grads, keep, far, send, send_far, total = refs[:n], refs[n : 2 * n], *refs[2 * n :]
    each = grads[0].shape[0]
    rows_of_x = jnp.concatenate([ref[:each, :] for ref in x], axis=0)
    g = jnp.concatenate([ref[...] for ref in grads], axis=0)
    total[...] = tn(rows_of_x, g)

    def rows(k):
        return total[pl.ds(pl.multiple_of((meta[1] ^ k) * feat, feat), feat), :]

    bias = col_sum(g.astype(F32))
    hi = bias.astype(BF).astype(F32)
    row = lax.broadcasted_iota(jnp.int32, (16, bias.shape[1]), 0)
    tail = jnp.where(row == 0, hi, jnp.where(row == 1, bias - hi, 0.0))
    keep[:feat, :] = rows(0)
    keep[feat:, :] = tail
    far[...] = rows(2)
    send[:feat, :] = rows(1).astype(BF)
    send[feat:, :] = tail.astype(BF)
    send_far[...] = rows(3).astype(BF)


def qkv_grads(meta, x, grads, feat):
    wide = grads[0].shape[1]
    width = x[0].shape[1]
    return meta_call(
        functools.partial(qkv_grads_kernel, n=len(x), feat=feat),
        [meta, *x, *grads],
        [
            jax.ShapeDtypeStruct((feat + 16, wide), F32),
            jax.ShapeDtypeStruct((feat, wide), F32),
            jax.ShapeDtypeStruct((feat + 16, wide), BF),
            jax.ShapeDtypeStruct((feat, wide), BF),
        ],
        "qkv_grads",
        scratch=[pltpu.VMEM((width, wide), F32)],
    )


def spread_kernel(meta, *refs, n):
    pieces, outs = refs[:n], refs[n:]
    hw = pieces[0].shape[1] // 3
    values = [ref[...].astype(F32) for ref in pieces]
    for j in range(n):
        away = meta[3] - j
        away = jnp.where(away < 0, away + n, away)
        value = values[0]
        for k in range(1, n):
            value = jnp.where(away == k, values[k], value)
        for i, out in enumerate(outs):
            out[:, j * hw : (j + 1) * hw] = value[:, i * hw : (i + 1) * hw]


def spread(meta, pieces):
    sub, wide = pieces[0].shape
    width = wide // 3 * len(pieces)
    return meta_call(
        functools.partial(spread_kernel, n=len(pieces)),
        [meta, *pieces],
        [jax.ShapeDtypeStruct((sub, width), F32)] * 3,
        "spread",
    )


def pack_kernel(meta, *refs, n):
    blocks, (down, bias, out, half) = refs[:n], refs[n:]
    units, feat = blocks[0].shape
    size = out.shape[0] // 2
    values = [ref[...].astype(F32) for ref in blocks]
    for owner in range(n):
        value = values[0]
        for k in range(1, n):
            value = jnp.where((meta[1] ^ k) == owner, values[k], value)
        out[:units, owner * feat : (owner + 1) * feat] = value.astype(BF)
    out[units:size, :] = bias[...]
    out[size : size + units, :] = down[...].astype(BF)
    out[size + units :, :] = jnp.zeros((size - units, out.shape[1]), BF)

    @pl.when(meta[4] == 0)
    def _():
        half[...] = out[:size, :]

    @pl.when(meta[4] != 0)
    def _():
        half[...] = out[size:, :]


def pack_weights(meta, blocks, down, bias):
    rows, width = down.shape
    size = rows + bias.shape[0]
    return meta_call(
        functools.partial(pack_kernel, n=len(blocks)),
        [meta, *blocks, down, bias],
        [jax.ShapeDtypeStruct((2 * size, width), BF), jax.ShapeDtypeStruct((size, width), BF)],
        "pack_weights",
    )


CORE = [(0, 1), (1, 0), (2, 3), (3, 2)]
CROSS = [(0, 2), (2, 0), (1, 3), (3, 1)]


def core_swap(x):
    return lax.ppermute(x, "row", CORE)


def cross_swap(x):
    return lax.ppermute(x, "row", CROSS)


def shift_col(x, step):
    n = lax.axis_size("col")
    return lax.ppermute(x, "col", [(i, (i + step) % n) for i in range(n)])


def after(x, *others):
    return lax.optimization_barrier((x,) + others)[0]


def natural_row(blocks):
    r = lax.axis_index("row")
    low = (r & 1) == 0
    b0, b1, b2, b3 = blocks
    left = jnp.where(low, jnp.stack([b0, b1]), jnp.stack([b1, b0]))
    right = jnp.where(low, jnp.stack([b2, b3]), jnp.stack([b3, b2]))
    return jnp.where(r < 2, jnp.concatenate([left, right]), jnp.concatenate([right, left]))


def gather_row_rel(x):
    far = cross_swap(x)
    near = core_swap(x)
    return [x, near, far, core_swap(far)]


def sum_dp(x):
    n = lax.axis_size("dp")
    if n == 2:
        return x + lax.ppermute(x, "dp", [(0, 1), (1, 0)])
    return lax.psum(x, "dp")


def split3(x):
    hi = lax.reduce_precision(x, 8, 7)
    mid = lax.reduce_precision(x - hi, 8, 7)
    low = x - hi - mid
    return hi.astype(BF), mid.astype(BF), low.astype(BF)


def per_device(
    tokens,
    cotangent,
    lengths,
    query_weight,
    key_weight,
    value_weight,
    query_bias,
    value_bias,
    out_weight,
    out_bias,
    norm1_gain,
    norm1_shift,
    up_weight,
    up_bias,
    down_weight,
    down_bias,
    norm2_gain,
    norm2_shift,
):
    rows_n = lax.axis_size("row")
    cols_n = lax.axis_size("col")
    r = lax.axis_index("row")
    z = lax.axis_index("col")
    local, width = tokens.shape
    block_len = local * cols_n
    hw = width // cols_n
    heads = hw // HD
    feat = width // rows_n
    scale = 1.0 / math.sqrt(HD)
    paired = lax.axis_size("dp") == 2
    pair = lax.axis_index("dp") if paired else jnp.zeros((), jnp.int32)
    meta = jnp.stack([lengths[0], r, z * (local * rows_n) + r * local, z, pair]).astype(jnp.int32)

    sub_out = out_weight.shape[0]
    x_blocks = [jnp.concatenate([tokens.astype(F32), out_weight]).astype(BF)]
    x_blocks.append(shift_col(x_blocks[0], 1))

    up_t = up_weight.astype(BF).T
    units = up_t.shape[0] // rows_n
    up_t = up_t.reshape(rows_n, units, feat)
    pieces = [lax.dynamic_index_in_dim(up_t, r ^ k, 0, keepdims=False) for k in range(4)]
    up_blocks = [
        pieces[0],
        core_swap(pieces[1]),
        cross_swap(pieces[2]),
        lax.ppermute(pieces[3], "row", [(i, i ^ 3) for i in range(rows_n)]),
    ]

    qkv = jnp.stack([query_weight, key_weight, value_weight], axis=1).astype(BF)
    sub = qkv.shape[0]
    qkv = qkv.reshape(sub, 3, cols_n, hw).transpose(2, 0, 1, 3).reshape(cols_n, sub, 3 * hw)
    pieces = []
    for k in range(cols_n):
        piece = lax.dynamic_index_in_dim(qkv, (z + k) % cols_n, 0, keepdims=False)
        pieces.append(shift_col(piece, k) if k else piece)
    second, *pieces = lax.optimization_barrier((x_blocks[1], *pieces))
    x_blocks.append(shift_col(second, 1))
    w_blocks = gather_row_rel(jnp.concatenate(pieces))
    for _ in range(3, cols_n):
        x_blocks.append(shift_col(x_blocks[-1], 1))

    bias_mine = lax.dynamic_slice_in_dim(up_bias, r * units, units, 0)
    bias_rows = jnp.pad(jnp.stack(split3(bias_mine)), ((0, 13), (0, width - units)))
    def cross_dp(x):
        return lax.ppermute(x, "dp", [(0, 1), (1, 0)]) if paired else x[:1]

    pack, half = pack_weights(meta, up_blocks, down_weight, bias_rows)
    half = after(half if paired else pack, x_blocks[-1])
    hops = [shift_col(half, 1)]

    qkv_bias = jnp.concatenate([query_bias, jnp.zeros_like(value_bias), value_bias])
    qkv_bias = jnp.broadcast_to(qkv_bias[None], (8, 3 * hw))
    vecs = jnp.stack([out_bias, norm1_gain, norm1_shift, down_bias, norm2_gain, norm2_shift])
    vecs = jnp.pad(jnp.stack(split3(vecs)), ((0, 1), (0, 2), (0, width - feat))).reshape(32, width)
    early, late = (0, 1), tuple(range(2, cols_n))
    q_a, kv_a = project_qkv(meta, x_blocks[:2], early, cols_n, w_blocks, qkv_bias, local, scale)
    far_a, near_a = cross_swap(kv_a), core_swap(kv_a)
    x_blocks[-1], near_a, pack = lax.optimization_barrier((x_blocks[-1], near_a, pack))
    q_b, kv_b, w_qkv, out_pack = project_qkv(
        meta, x_blocks, late, cols_n, w_blocks, qkv_bias, local, scale, vecs
    )
    far_b, near_b = cross_swap(kv_b), core_swap(kv_b)
    near_b, far_a = lax.optimization_barrier((near_b, far_a))
    sizes = (rows_n, cols_n)
    q_parts = [q_a, q_b]
    acc, stat, k_near, v_near = attn_fwd(
        meta, q_parts, [kv_a, kv_b, near_a, near_b], (0, 1), heads, local, sizes, NEAR_COST
    )
    stat, hops[0], half = lax.optimization_barrier((stat, hops[0], half))
    hops += [shift_col(hops[0], 1), shift_col(half, -1)]
    crossed = [cross_dp(hops[0])]
    stat, far_a, far_b, out_pack = lax.optimization_barrier((stat, far_a, far_b, out_pack))
    out_far, out_near = cross_swap(out_pack), core_swap(out_pack)
    state = (acc, stat)
    far = [far_a, far_b, core_swap(far_a), core_swap(far_b)]
    *mixed_part, qb_rows, k_far, v_far = attn_fwd(
        meta, q_parts, far, (2, 3), heads, local, sizes, 4, state=state
    )
    *mixed_part, second, third, first, out_far, qb_rows = lax.optimization_barrier(
        (*mixed_part, hops[1], hops[2], crossed[0], out_far, qb_rows)
    )
    hops[1:] = [second, third]
    crossed = [first, cross_dp(second), cross_dp(third)]
    mixed = [mixed_part[0]] + [shift_col(mixed_part[k], -k) for k in range(1, cols_n)]

    out_packs = [out_pack, out_near, out_far, core_swap(out_far)]
    *mixed, crossed[1] = lax.optimization_barrier((*mixed, crossed[1]))
    packs = [pack]
    for hop, other in zip(hops, crossed):
        packs += [hop, other] if paired else [hop]
    hidden, hidden_low, normal1, inv1, out_full, vecs = project(meta, mixed, out_packs, tokens, sub_out)

    h_own, h_far, h_near = hidden_low, cross_swap(hidden_low), core_swap(hidden_low)
    h_near, h_far, packs[-1] = lax.optimization_barrier((h_near, h_far, packs[-1]))
    h_diag = core_swap(h_far)
    keep0, send0, act0, slope0 = ffn_fwd(meta, h_own, h_near, packs, units, units * cols_n)
    keep1, send1, act1, slope1 = ffn_fwd(meta, h_far, h_diag, packs, units, units * cols_n)
    far = (keep1 + core_swap(send1).astype(F32)).astype(BF)
    got_far = cross_swap(far)
    got_near = core_swap(send0)
    output, grad_resid2, grad_branch, sums2 = norm2(
        meta, hidden, keep0, got_near, got_far, cotangent, vecs
    )

    g_own, g_far, g_near = grad_branch, cross_swap(grad_branch), core_swap(grad_branch)
    keep0, send0, pre0 = ffn_bwd(meta, g_own, g_near, packs, slope0, units)
    g_far = after(g_far, send0)
    g_diag = core_swap(g_far)
    keep1, send1, pre1 = ffn_bwd(meta, g_far, g_diag, packs, slope1, units)
    far = (keep1 + core_swap(send1).astype(F32)).astype(BF)
    got_far = cross_swap(far)
    got_near = core_swap(send0)
    g_one, g_two, g_up_bias = ffn_grads(
        meta,
        (act0, act1),
        (pre0, pre1),
        (h_own, h_near, h_far, h_diag),
        (g_own, g_near, g_far, g_diag),
    )
    if paired:
        g_two = lax.ppermute(g_two, "dp", [(0, 1), (1, 0)])
    keep0 = after(keep0, g_one)
    grad_resid1, grad_attended, sums1, grad_mixed = norm1_back(
        keep0, got_near, got_far, grad_resid2, normal1, inv1, vecs, out_full
    )
    grad_mixed = [grad_mixed[0]] + [shift_col(grad_mixed[k], k) for k in range(1, cols_n)]

    out_keep, out_far, out_send, sums = out_grads(
        meta, mixed, grad_attended, sums1, sums2, g_up_bias, sub_out, rows_n
    )
    out_got = core_swap(out_send)
    out_got = after(out_got, grad_mixed[1])
    out_message = far_message(out_far, sums, out_got)
    out_got_far = cross_swap(out_message)
    messages = col_messages(
        g_one, g_two, out_keep, sums, out_got, out_got_far, sub_out, cols_n, paired
    )

    grads = after(grad_rows(mixed_part, grad_mixed, heads), out_message)
    dq = jnp.zeros((block_len, LANES), F32)
    *part3, dq = attn_bwd(1, qb_rows, grads, k_far, v_far, dq, heads, 4)
    got3 = [core_swap(part) for part in part3]
    dq = after(dq, messages[1])
    packed = shift_col(after(messages[1], dq), 1)
    *part2, dq = attn_bwd(0, qb_rows, grads, k_far, v_far, dq, heads, 4)
    far_sum = [(a.astype(F32) + b.astype(F32)).astype(BF) for a, b in zip(part2, got3)]
    far_sum = jnp.concatenate(far_sum)
    far_got = cross_swap(far_sum)
    packed = sum_messages([messages[2], packed])
    dq = after(dq, far_sum, packed)
    packed = shift_col(after(packed, dq), 1)
    *part1, dq = attn_bwd(1, qb_rows, grads, k_near, v_near, dq, heads, 4)
    got1 = [core_swap(part) for part in part1]
    packed = sum_messages([messages[3], packed])
    dq = after(dq, packed)
    packed = shift_col(after(packed, dq), 1)
    *part0, dq = attn_bwd(0, qb_rows, grads, k_near, v_near, dq, heads, C4)

    d_blocks, back = join_grads(part0, got1, far_got, dq, w_qkv, cols_n, scale)
    ring = [shift_col(back[1], 1)]

    d_blocks = [after(d_blocks[0], packed), *d_blocks[1:]]
    own, far, send, send_far = qkv_grads(meta, x_blocks, d_blocks, feat)
    packed = sum_messages([after(messages[0], back[1]), packed])
    got, got_far = core_swap(send), core_swap(send_far)
    ring[0], got, got_far, packed = lax.optimization_barrier((ring[0], got, got_far, packed))
    for step in range(2, cols_n + 1):
        total = back[step % cols_n].astype(F32) + ring[-1].astype(F32)
        if step < cols_n:
            ring.append(shift_col(total.astype(BF), 1))
    grad_tokens = grad_resid1 + total
    if paired:
        other = lax.ppermute(packed, "dp", [(0, 1), (1, 0)])
    else:
        other = lax.psum(packed.astype(F32), "dp") - packed.astype(F32)
    g_bias = own[feat] + own[feat + 1]

    def with_bias(block, bias):
        hi = lax.reduce_precision(bias, 8, 7)
        rows = jnp.pad(jnp.stack([hi, bias - hi]), ((0, 14), (0, 0)))
        return jnp.concatenate([block, rows]).astype(BF)

    def bias_of(got):
        return got[-16].astype(F32) + got[-15].astype(F32)

    g_bias = g_bias + bias_of(got)
    mine = own[:feat] + got[:feat].astype(F32)
    got_x = got = cross_swap(with_bias(far + got_far.astype(F32), g_bias))
    g_bias = g_bias + bias_of(got)
    mine = mine + got[:feat].astype(F32)
    if paired:
        got = lax.ppermute(after(with_bias(mine, g_bias), ring[0]), "dp", [(0, 1), (1, 0)])
        g_bias = g_bias + bias_of(got)
        g_qkv = mine + got[:feat].astype(F32)
    else:
        g_bias, g_qkv = lax.psum((g_bias, mine), "dp")
    g_qkv = g_qkv.astype(BF).reshape(cols_n, sub, 3 * hw)
    pieces = []
    for k in range(cols_n):
        piece = lax.dynamic_index_in_dim(g_qkv, (z + k) % cols_n, 0, keepdims=False)
        pieces.append(shift_col(piece, k) if k else piece)
    g_qkv = spread(meta, pieces)
    other = after(other, ring[1], got_x)
    *g_up, g_down_weight, g_out_weight, sums = finish(
        meta, packed, other, rows_n, units, sub_out, paired
    )
    g_up[1] = core_swap(g_up[1])
    g_up[2] = cross_swap(g_up[2])
    g_up[3] = lax.ppermute(g_up[3], "row", [(i, i ^ 3) for i in range(rows_n)])
    g_up_weight = up_grads(meta, g_up)
    vec_out = lax.dynamic_slice_in_dim(sums[:6], r * feat, feat, 1)
    g_up_bias = lax.dynamic_index_in_dim(sums[8 : 8 + cols_n], z, 0, keepdims=False)

    return (
        output,
        grad_tokens,
        g_qkv[0],
        g_qkv[1],
        g_qkv[2],
        g_bias[:hw],
        g_bias[2 * hw :],
        g_out_weight,
        vec_out[2],
        vec_out[0],
        vec_out[1],
        g_up_weight,
        g_up_bias,
        g_down_weight,
        vec_out[5],
        vec_out[3],
        vec_out[4],
    )


def solution(mesh):
    token_spec = P(("dp", "col", "row"), None)
    placed = (
        token_spec,
        token_spec,
        P("dp"),
        P(("row", "col"), None),
        P(("row", "col"), None),
        P(("row", "col"), None),
        P("col"),
        P("col"),
        P(("col", "row"), None),
        P("row"),
        P("row"),
        P("row"),
        P("row", "col"),
        P("col"),
        P(("col", "row"), None),
        P("row"),
        P("row"),
        P("row"),
    )
    return jax.shard_map(
        per_device,
        mesh=mesh,
        in_specs=placed,
        out_specs=(token_spec, token_spec) + placed[3:],
        check_vma=False,
    )
```

```python
import functools
import math

import jax
import jax.numpy as jnp
from jax import lax
from jax.experimental import pallas as pl
from jax.experimental.pallas import tpu as pltpu
from jax.sharding import PartitionSpec as P

HD = 64
LANES = 256
EPS = 1e-05
BF = jnp.bfloat16
F32 = jnp.float32
VMEM_BYTES = 60 * 1024 * 1024
TURNED = HD + 16
SMALL_BYTES = 24 * 1024 * 1024
ATTN_BYTES = 36 * 1024 * 1024
NEAR_COST = 4
C4 = 6


def nn(a, b):
    return jnp.dot(a, b, preferred_element_type=F32)


def tn(a, b):
    return lax.dot_general(a, b, (((0,), (0,)), ((), ())), preferred_element_type=F32)


def nt(a, b):
    return lax.dot_general(a, b, (((1,), (1,)), ((), ())), preferred_element_type=F32)


def cost(us):
    return pl.CostEstimate(flops=int(us * 0.6e9), bytes_accessed=1000, transcendentals=0)


def head_lanes(shape, head, width):
    lane = lax.broadcasted_iota(jnp.int32, shape, 1)
    mine = (lane >= head * HD) & (lane < (head + 1) * HD)
    return mine | (lane == width) | ((lane >= width + 1 + 3 * head) & (lane < width + 4 + 3 * head))


def three_parts(x):
    hi = x.astype(BF).astype(F32)
    mid = (x - hi).astype(BF).astype(F32)
    return hi, mid, x - hi - mid


def tail_rows(parts, ones, n):
    row = lax.broadcasted_iota(jnp.int32, (n, parts[0].shape[1]), 0)
    out = jnp.where(row == 0, ones, 0.0)
    for head, value in enumerate(parts):
        for i, piece in enumerate(three_parts(value)):
            out = jnp.where(row == 1 + 3 * head + i, piece, out)
    return out


def widen_keys(kv, owner, base, meta, keys_out, values_out, turned, at, width, shift, sizes):
    n = kv.shape[0]
    rows_n, cols_n = sizes
    keys_out[at : at + n, :width] = kv[:, :width]
    values_out[at : at + n, :width] = kv[:, width:]
    shape = (n, LANES - width)
    t = lax.broadcasted_iota(jnp.int32, shape, 0) + base
    lane = lax.broadcasted_iota(jnp.int32, shape, 1)
    source = meta[3] - (t >> shift)
    source = jnp.where(source < 0, source + cols_n, source)
    position = ((source * rows_n + owner) << shift) + (t & ((1 << shift) - 1))
    mask = jnp.where(lane == 0, jnp.where(position >= meta[0], -1e30, 0.0), 1.0)
    keys_out[at : at + n, width:] = mask.astype(BF)
    values_out[at : at + n, width:] = jnp.ones(shape, BF)
    flat = values_out[at : at + n, :].T
    for head in range(width // HD):
        first = head * TURNED
        turned[first : first + HD, at : at + n] = flat[head * HD : (head + 1) * HD, :]
        turned[first + HD : first + TURNED, at : at + n] = jnp.ones((TURNED - HD, n), BF)


def attn_fwd_kernel(*refs, heads, first, pair, shift, sizes, chunk, blocks, parts):
    meta, *refs = refs
    q_refs, refs = refs[:parts], refs[parts:]
    kvs, refs = refs[: 2 * parts], refs[2 * parts :]
    if first:
        acc_out, stat_out, k_out, v_out, turned = refs
    else:
        acc_in, stat_in = refs[:2]
        outs = refs[2 : 2 + blocks]
        qb_ref, k_out, v_out, turned = refs[2 + blocks :]
    width = heads * HD
    keys = k_out.shape[0]
    at = 0
    for i, ref in enumerate(kvs):
        base = at % (keys // 2)
        owner = meta[1] ^ pair[i // parts]
        widen_keys(ref[...], owner, base, meta, k_out, v_out, turned, at, width, shift, sizes)
        at += ref.shape[0]
    q = jnp.concatenate([ref[...] for ref in q_refs], axis=0)
    rows = q.shape[0]
    slot = lax.broadcasted_iota(jnp.int32, (16, rows), 0)
    stat = jnp.zeros((16, rows), F32)
    logs = []
    for head in range(heads):
        qh = jnp.where(head_lanes(q.shape, head, width), q, jnp.zeros_like(q))
        scores = [nt(k_out[i : i + chunk, :], qh) for i in range(0, keys, chunk)]
        peak = functools.reduce(
            jnp.maximum, [jnp.max(s, axis=0, keepdims=True) for s in scores]
        )
        if not first:
            old = stat_in[head : head + 1, :]
            peak = jnp.maximum(peak, old)
        acc = None
        for i, s in enumerate(scores):
            p = jnp.exp(s - peak).astype(BF)
            at = head * TURNED
            part = nn(turned[at : at + TURNED, i * chunk : (i + 1) * chunk], p)
            acc = part if acc is None else acc + part
        total = acc[HD : HD + 1]
        mine = slice(head * HD, (head + 1) * HD)
        if first:
            acc_out[mine, :] = acc[:HD]
            stat = jnp.where(slot == head, peak, stat)
            stat = jnp.where(slot == head + 8, total, stat)
        else:
            keep = jnp.exp(old - peak)
            total = total + stat_in[head + 8 : head + 9, :] * keep
            out = ((acc[:HD] + acc_in[mine, :] * keep) * (1.0 / total)).astype(BF)
            each = rows // blocks
            for b in range(blocks):
                outs[b][mine, :] = out[:, b * each : (b + 1) * each]
            logs.append(-(peak + jnp.log(total)))
    if first:
        stat_out[...] = stat
    else:
        qb_ref[:, :width] = q[:, :width]
        qb_ref[:, width:] = tail_rows(logs, 1.0, LANES - width).T.astype(BF)


def attn_fwd(meta, q, kvs, pair, heads, local, sizes, us, state=None, chunk=512):
    rows = sum(part.shape[0] for part in q)
    half = sum(kv.shape[0] for kv in kvs) // 2
    width = kvs[0].shape[1] // 2
    first = state is None
    blocks = rows // local
    vmem = pl.BlockSpec(memory_space=pltpu.VMEM)
    args = [meta, *q, *kvs]
    if first:
        out_shape = [jax.ShapeDtypeStruct((width, rows), F32), jax.ShapeDtypeStruct((16, rows), F32)]
    else:
        args += list(state)
        out_shape = [jax.ShapeDtypeStruct((width, local), BF)] * blocks
        out_shape += [jax.ShapeDtypeStruct((rows, LANES), BF)]
    out_shape += [jax.ShapeDtypeStruct((2 * half, LANES), BF)] * 2
    return pl.pallas_call(
        functools.partial(
            attn_fwd_kernel,
            heads=heads,
            first=first,
            pair=pair,
            shift=local.bit_length() - 1,
            sizes=sizes,
            chunk=chunk,
            blocks=blocks,
            parts=len(q),
        ),
        in_specs=[pl.BlockSpec(memory_space=pltpu.SMEM)] + [vmem] * (len(args) - 1),
        out_specs=[vmem] * len(out_shape),
        out_shape=out_shape,
        scratch_shapes=[pltpu.VMEM((heads * TURNED, 2 * half), BF)],
        compiler_params=pltpu.CompilerParams(vmem_limit_bytes=ATTN_BYTES),
        cost_estimate=cost(us),
        name="attn_fwd_near" if first else "attn_fwd_far",
    )(*args)


def grad_rows_kernel(*refs, heads, blocks):
    outs, grads, wide = refs[:blocks], refs[blocks : 2 * blocks], refs[2 * blocks]
    width = heads * HD
    for b in range(blocks):
        g = grads[b][...].astype(F32)
        prod = g * outs[b][...].astype(F32)
        each = g.shape[1]
        parts = [
            -jnp.sum(prod[head * HD : (head + 1) * HD], axis=0, keepdims=True) for head in range(heads)
        ]
        tall = jnp.concatenate([g, tail_rows(parts, 0.0, LANES - width)], axis=0)
        wide[b * each : (b + 1) * each, :] = tall.T.astype(BF)


def grad_rows(outs, grads, heads):
    each = outs[0].shape[1]
    return small_call(
        functools.partial(grad_rows_kernel, heads=heads, blocks=len(outs)),
        jax.ShapeDtypeStruct((each * len(outs), LANES), BF),
        "grad_rows",
    )(*outs, *grads)


def attn_bwd_kernel(at_ref, q_ref, g_ref, k_ref, v_ref, dq_in, *refs, heads, block, pieces):
    outs, (dq_out, dk, dv) = refs[:pieces], refs[pieces:]
    width = heads * HD
    half = dk.shape[0]
    keys = pl.ds(pl.multiple_of(at_ref[0] * half, half), half)
    dk[...] = jnp.zeros_like(dk)
    dv[...] = jnp.zeros_like(dv)

    def step(i, carry):
        at = pl.ds(pl.multiple_of(i * block, block), block)
        q_all = q_ref[at, :]
        g_all = g_ref[at, :]
        k = k_ref[keys, :]
        dq = jnp.zeros((block, LANES), F32)
        for head in range(heads):
            mine = head_lanes((block, LANES), head, width)
            q = jnp.where(mine, q_all, jnp.zeros_like(q_all))
            g = jnp.where(mine, g_all, jnp.zeros_like(g_all))
            p = jnp.exp(nt(k, q))
            ds = (p * nt(v_ref[keys, :], g)).astype(BF)
            dv[...] += nn(p.astype(BF), g)
            dk[...] += nn(ds, q)
            dq = jnp.where(mine, tn(ds, k), dq)
        dq_out[at, :] = dq_in[at, :] + dq
        return carry

    lax.fori_loop(0, q_ref.shape[0] // block, step, 0)
    each = outs[0].shape[0]
    for i, out in enumerate(outs):
        at = slice(i * each, (i + 1) * each)
        out[:, :width] = dk[at, :width].astype(out.dtype)
        out[:, width:] = dv[at, :width].astype(out.dtype)


def attn_bwd(at, q, g, k, v, dq, heads, us, pieces=2, block=1024):
    rows = q.shape[0]
    half = k.shape[0] // 2
    width = heads * HD
    vmem = pl.BlockSpec(memory_space=pltpu.VMEM)
    out_shape = [jax.ShapeDtypeStruct((half // pieces, 2 * width), BF)] * pieces
    return pl.pallas_call(
        functools.partial(attn_bwd_kernel, heads=heads, block=block, pieces=pieces),
        in_specs=[pl.BlockSpec(memory_space=pltpu.SMEM)] + [vmem] * 5,
        out_specs=[vmem] * (pieces + 1),
        out_shape=out_shape + [jax.ShapeDtypeStruct((rows, LANES), F32)],
        scratch_shapes=[pltpu.VMEM((half, LANES), F32)] * 2,
        compiler_params=pltpu.CompilerParams(vmem_limit_bytes=ATTN_BYTES),
        cost_estimate=cost(us),
        name="attn_bwd",
    )(jnp.full((1,), at, jnp.int32), q, g, k, v, dq)


def small_call(kernel, out_shape, name, scratch=(), us=1.4):
    return pl.pallas_call(
        kernel,
        out_shape=out_shape,
        scratch_shapes=scratch,
        compiler_params=pltpu.CompilerParams(vmem_limit_bytes=SMALL_BYTES),
        cost_estimate=cost(us),
        name=name,
    )


def meta_call(kernel, args, out_shape, name, scratch=(), us=1.2):
    vmem = pl.BlockSpec(memory_space=pltpu.VMEM)
    return pl.pallas_call(
        kernel,
        in_specs=[pl.BlockSpec(memory_space=pltpu.SMEM)] + [vmem] * (len(args) - 1),
        out_specs=[vmem] * len(out_shape),
        out_shape=out_shape,
        scratch_shapes=scratch,
        compiler_params=pltpu.CompilerParams(vmem_limit_bytes=SMALL_BYTES),
        cost_estimate=cost(us),
        name=name,
    )(*args)


def row_mean(x):
    return jnp.mean(x, axis=1, keepdims=True)


def col_sum(x):
    return jnp.sum(x, axis=0, keepdims=True)


def norm_forward(resid, gain, shift):
    centered = resid - row_mean(resid)
    inv = lax.rsqrt(row_mean(centered * centered) + EPS)
    normal = centered * inv
    return normal * gain + shift, normal, inv


def norm_backward(grad_out, normal, inv, gain):
    scaled = grad_out * gain
    return inv * (scaled - row_mean(scaled) - normal * row_mean(scaled * normal))


def project_qkv_kernel(meta, *refs, n, blocks, last, rows_n, cols_n, feat, hw, scale):
    x, ws, bias_ref = refs[:n], refs[n : n + rows_n], refs[n + rows_n]
    if last:
        vec_ref, q_ref, kv_ref, w_out, pack_ref, w_all = refs[n + rows_n + 1 :]
    else:
        q_ref, kv_ref, w_all = refs[n + rows_n + 1 :]
    each = feat // cols_n
    for k in range(rows_n):
        for m in range(cols_n):
            source = meta[3] - m
            source = jnp.where(source < 0, source + cols_n, source)
            at = pl.multiple_of((meta[1] ^ k) * feat + source * each, each)
            w_all[pl.ds(at, each), :] = ws[k][m * each : (m + 1) * each, :]
    w = w_all[...]
    each = q_ref.shape[0] // len(blocks)
    for i, k in enumerate(blocks):
        at = slice(i * each, (i + 1) * each)
        out = nn(x[k][:each, :], w) + bias_ref[0:1, :]
        q_ref[at, :hw] = (out[:, :hw].astype(BF).astype(F32) * scale).astype(BF)
        lane = lax.broadcasted_iota(jnp.int32, (each, LANES - hw), 1)
        q_ref[at, hw:] = jnp.where(lane == 0, 1.0, 0.0).astype(BF)
        kv_ref[at, :] = out[:, hw:].astype(BF)
    if last:
        w_out[...] = w.T
        more = x[0].shape[0] - each
        for k in range(n):
            pack_ref[k * more : (k + 1) * more, :] = x[k][each:, :]
        pack_ref[n * more :, :] = vec_ref[...]


def project_qkv(meta, x, blocks, cols_n, ws, bias, local, scale, vecs=None):
    feat, wide = ws[0].shape
    hw = wide // 3
    rows = local * len(blocks)
    shapes = [
        jax.ShapeDtypeStruct((rows, LANES), BF),
        jax.ShapeDtypeStruct((rows, 2 * hw), BF),
    ]
    args = [meta, *x, *ws, bias]
    if vecs is not None:
        args.append(vecs)
        more = (x[0].shape[0] - local) * len(x) + vecs.shape[0]
        shapes.append(jax.ShapeDtypeStruct((wide, feat * len(ws)), BF))
        shapes.append(jax.ShapeDtypeStruct((more, vecs.shape[1]), BF))
    return meta_call(
        functools.partial(
            project_qkv_kernel,
            n=len(x),
            blocks=blocks,
            last=vecs is not None,
            rows_n=len(ws),
            cols_n=cols_n,
            feat=feat,
            hw=hw,
            scale=scale,
        ),
        args,
        shapes,
        "project_qkv",
        scratch=[pltpu.VMEM((feat * len(ws), wide), BF)],
    )


def project_kernel(meta, *refs, n, rows_n, sub, feat):
    mixed, packs = refs[:n], refs[n : n + rows_n]
    x_ref, hid_ref, low_ref, normal_ref, inv_ref, w_ref, vec_ref = refs[n + rows_n :]
    r = meta[1]
    for k in range(rows_n):
        at = pl.multiple_of((r ^ k) * sub, sub)
        for i in range(n):
            w_ref[i, pl.ds(at, sub), :] = packs[k][((n - i) % n) * sub : ((n - i) % n + 1) * sub, :]
    values = []
    for k in range(rows_n):
        part = packs[k][n * sub : n * sub + 32, :feat].astype(F32)
        values.append(part[0:8] + part[8:16] + part[16:24])
    pieces = []
    for owner in range(rows_n):
        value = values[0]
        for k in range(1, rows_n):
            value = jnp.where((r ^ k) == owner, values[k], value)
        pieces.append(value)
    vecs = jnp.concatenate(pieces, axis=1)
    vec_ref[...] = vecs
    total = x_ref[...].astype(F32) + vecs[0:1, :]
    for j in range(n):
        total = total + tn(mixed[j][...], w_ref[j])
    hidden, normal, inv = norm_forward(total, vecs[1:2, :], vecs[2:3, :])
    hid_ref[...] = hidden
    low_ref[...] = hidden.astype(BF)
    normal_ref[...] = normal
    inv_ref[...] = jnp.broadcast_to(inv, inv_ref.shape)


def project(meta, mixed, packs, x, sub):
    rows, width = x.shape
    feat = width // len(packs)
    return meta_call(
        functools.partial(
            project_kernel, n=len(mixed), rows_n=len(packs), sub=sub, feat=feat
        ),
        [meta, *mixed, *packs, x],
        [
            jax.ShapeDtypeStruct((rows, width), F32),
            jax.ShapeDtypeStruct((rows, width), BF),
            jax.ShapeDtypeStruct((rows, width), F32),
            jax.ShapeDtypeStruct((rows, 128), F32),
            jax.ShapeDtypeStruct((len(mixed), sub * len(packs), width), BF),
            jax.ShapeDtypeStruct((8, width), F32),
        ],
        "project_norm1",
    )


def weight_rows(meta, packs, units, down):
    size = packs[0].shape[0] // 2
    at = size if down else 0
    values = [packs[0][at : at + units, :]]
    rest = packs[1:]
    if rest[0].shape[0] > size:
        return values + [ref[at : at + units, :] for ref in rest]
    mine = (meta[4] == 0) != down
    for own, other in zip(rest[::2], rest[1::2]):
        values.append(jnp.where(mine, own[:units, :].astype(F32), other[:units, :].astype(F32)).astype(BF))
    return values


def bias_rows(meta, packs, units):
    size = packs[0].shape[0] // 2
    at = slice(units, units + 16)
    values = [packs[0][at, :].astype(F32)]
    rest = packs[1:]
    if rest[0].shape[0] > size:
        values += [ref[at, :].astype(F32) for ref in rest]
    else:
        for own, other in zip(rest[::2], rest[1::2]):
            values.append(jnp.where(meta[4] == 0, own[at, :].astype(F32), other[at, :].astype(F32)))
    return jnp.concatenate([v[0:1, :units] + v[1:2, :units] + v[2:3, :units] for v in values], axis=1)


def ffn_fwd_kernel(meta, *refs, n, units):
    h0, h1 = refs[:2]
    packs = refs[2 : 2 + n]
    keep_ref, send_ref, act_ref, slope_ref = refs[2 + n :]
    rows = h0.shape[0]
    h = jnp.concatenate([h0[...], h1[...]], axis=0)
    up = jnp.concatenate(weight_rows(meta, packs, units, False), axis=0)
    x = nt(h, up) + bias_rows(meta, packs, units)
    cdf = 0.5 * (1.0 + lax.erf(x * math.sqrt(0.5)))
    act = (x * cdf).astype(BF)
    act_ref[...] = act
    slope = cdf + x * (math.sqrt(0.5 / math.pi) * jnp.exp(-0.5 * x * x))
    slope_ref[...] = slope.astype(BF)
    out = nn(act, jnp.concatenate(weight_rows(meta, packs, units, True), axis=0))
    keep_ref[...] = out[:rows]
    send_ref[...] = out[rows:].astype(BF)


def ffn_fwd(meta, h0, h1, packs, units, wide):
    rows, width = h0.shape
    return meta_call(
        functools.partial(ffn_fwd_kernel, n=len(packs), units=units),
        [meta, h0, h1, *packs],
        [
            jax.ShapeDtypeStruct((rows, width), F32),
            jax.ShapeDtypeStruct((rows, width), BF),
            jax.ShapeDtypeStruct((2 * rows, wide), BF),
            jax.ShapeDtypeStruct((2 * rows, wide), BF),
        ],
        "ffn_fwd",
        us=1.4,
    )


def ffn_bwd_kernel(meta, *refs, n, units):
    g0, g1 = refs[:2]
    packs = refs[2 : 2 + n]
    slope_ref, keep_ref, send_ref, pre_ref = refs[2 + n :]
    rows = g0.shape[0]
    g = jnp.concatenate([g0[...], g1[...]], axis=0)
    down = jnp.concatenate(weight_rows(meta, packs, units, True), axis=0)
    pre = (nt(g, down) * slope_ref[...].astype(F32)).astype(BF)
    pre_ref[...] = pre
    out = nn(pre, jnp.concatenate(weight_rows(meta, packs, units, False), axis=0))
    keep_ref[...] = out[:rows]
    send_ref[...] = out[rows:].astype(BF)


def ffn_bwd(meta, g0, g1, packs, slope, units):
    rows, width = g0.shape
    return meta_call(
        functools.partial(ffn_bwd_kernel, n=len(packs), units=units),
        [meta, g0, g1, *packs, slope],
        [
            jax.ShapeDtypeStruct((rows, width), F32),
            jax.ShapeDtypeStruct((rows, width), BF),
            jax.ShapeDtypeStruct(slope.shape, BF),
        ],
        "ffn_bwd",
        us=1.4,
    )


def ffn_grads_kernel(meta, *refs):
    act0, act1, pre0, pre1 = refs[:4]
    h = jnp.concatenate([ref[...] for ref in refs[4:8]], axis=0)
    g = jnp.concatenate([ref[...] for ref in refs[8:12]], axis=0)
    keep_ref, send_ref, bias_ref = refs[12:]
    pre = jnp.concatenate([pre0[...], pre1[...]], axis=0)
    act = jnp.concatenate([act0[...], act1[...]], axis=0)
    g_up = tn(pre, h).astype(BF)
    g_down = tn(act, g).astype(BF)
    first = meta[4] == 0

    @pl.when(first)
    def _():
        keep_ref[...] = g_up
        send_ref[...] = g_down

    @pl.when(jnp.logical_not(first))
    def _():
        keep_ref[...] = g_down
        send_ref[...] = g_up

    bias_ref[...] = jnp.broadcast_to(col_sum(pre.astype(F32)), bias_ref.shape)


def ffn_grads(meta, acts, pres, hiddens, grads):
    width = hiddens[0].shape[1]
    wide = acts[0].shape[1]
    return meta_call(
        ffn_grads_kernel,
        [meta, *acts, *pres, *hiddens, *grads],
        [
            jax.ShapeDtypeStruct((wide, width), BF),
            jax.ShapeDtypeStruct((wide, width), BF),
            jax.ShapeDtypeStruct((8, wide), F32),
        ],
        "ffn_grads",
    )


def norm2_kernel(
    meta, hid_ref, keep_ref, near_ref, far_ref, cot_ref, vec_ref, out_ref, grad_ref, low_ref, sum_ref
):
    branch = keep_ref[...] + near_ref[...].astype(F32) + far_ref[...].astype(F32) + vec_ref[3:4, :]
    gain = vec_ref[4:5, :]
    normed, normal, inv = norm_forward(hid_ref[...] + branch, gain, vec_ref[5:6, :])
    row = lax.broadcasted_iota(jnp.int32, (out_ref.shape[0], 1), 0)
    valid = (meta[2] + row < meta[0]).astype(F32)
    out_ref[...] = (normed * valid).astype(BF)
    grad_y = cot_ref[...].astype(F32) * valid
    grad = norm_backward(grad_y, normal, inv, gain)
    grad_ref[...] = grad
    low = grad.astype(BF)
    low_ref[...] = low
    sum_ref[...] = jnp.zeros_like(sum_ref)
    sum_ref[0:1, :] = col_sum(grad_y * normal)
    sum_ref[1:2, :] = col_sum(grad_y)
    sum_ref[2:3, :] = col_sum(low.astype(F32))


def norm2(meta, hidden, keep, near, far, cot, vecs):
    rows, width = hidden.shape
    shapes = [
        jax.ShapeDtypeStruct((rows, width), BF),
        jax.ShapeDtypeStruct((rows, width), F32),
        jax.ShapeDtypeStruct((rows, width), BF),
        jax.ShapeDtypeStruct((8, width), F32),
    ]
    return meta_call(norm2_kernel, [meta, hidden, keep, near, far, cot, vecs], shapes, "norm2_both")


def norm1_back_kernel(
    keep_ref, near_ref, far_ref, add_ref, normal_ref, inv_ref, vec_ref, w_ref, out_ref, low_ref, sum_ref, *mixed
):
    grad = keep_ref[...] + near_ref[...].astype(F32) + far_ref[...].astype(F32) + add_ref[...]
    normal = normal_ref[...]
    resid = norm_backward(grad, normal, inv_ref[:, 0:1], vec_ref[1:2, :])
    out_ref[...] = resid
    low = resid.astype(BF)
    low_ref[...] = low
    for j, ref in enumerate(mixed):
        ref[...] = nt(w_ref[j], low).astype(BF)
    sum_ref[...] = jnp.zeros_like(sum_ref)
    sum_ref[0:1, :] = col_sum(grad * normal)
    sum_ref[1:2, :] = col_sum(grad)
    sum_ref[2:3, :] = col_sum(low.astype(F32))


def norm1_back(keep, near, far, add, normal, inv, vecs, w):
    rows, width = add.shape
    out = small_call(
        norm1_back_kernel,
        [
            jax.ShapeDtypeStruct((rows, width), F32),
            jax.ShapeDtypeStruct((rows, width), BF),
            jax.ShapeDtypeStruct((8, width), F32),
        ]
        + [jax.ShapeDtypeStruct((w.shape[1], rows), BF)] * w.shape[0],
        "norm1_back",
    )(keep, near, far, add, normal, inv, vecs, w)
    return out[0], out[1], out[2], out[3:]


def two_parts(x):
    hi = x.astype(BF).astype(F32)
    return jnp.concatenate([hi, x - hi], axis=0).astype(BF)


def both_parts(rows):
    n = rows.shape[0] // 2
    return rows[:n].astype(F32) + rows[n:].astype(F32)


def out_grads_kernel(meta, *refs, n, rows_n, sub):
    mixed, grad, s1, s2, bias = refs[:n], *refs[n : n + 4]
    keep, far, send, sums, total = refs[n + 4 :]
    g = grad[...]
    for j in range(n):
        total[j] = nn(mixed[j][...], g)
    count = n * sub
    for j in range(n):
        at = slice(j * sub, (j + 1) * sub)

        def rows(k):
            return total[j, pl.ds(pl.multiple_of((meta[1] ^ k) * sub, sub), sub), :]

        keep[at, :] = rows(0)
        far[at, :] = rows(2)
        send[at, :] = rows(1).astype(BF)
        send[count + j * sub : count + (j + 1) * sub, :] = rows(3).astype(BF)
    sums[...] = jnp.zeros_like(sums)
    sums[0:3, :] = s1[0:3, :]
    sums[3:6, :] = s2[0:3, :]
    units = bias.shape[1] // n
    for j in range(n):
        away = meta[3] - j
        away = jnp.where(away < 0, away + n, away)
        value = bias[0:1, :units]
        for k in range(1, n):
            value = jnp.where(away == k, bias[0:1, k * units : (k + 1) * units], value)
        zero = jnp.zeros_like(value)
        row = [jnp.where(meta[1] == owner, value, zero) for owner in range(rows_n)]
        sums[8 + j : 9 + j, :] = jnp.concatenate(row, axis=1)
    send[2 * count :, :] = two_parts(sums[...])


def out_grads(meta, mixed, grad, s1, s2, bias, sub, rows_n):
    n, heads, width = len(mixed), mixed[0].shape[0], grad.shape[1]
    shapes = [
        jax.ShapeDtypeStruct((n * sub, width), F32),
        jax.ShapeDtypeStruct((n * sub, width), F32),
        jax.ShapeDtypeStruct((2 * n * sub + 32, width), BF),
        jax.ShapeDtypeStruct((16, width), F32),
    ]
    return meta_call(
        functools.partial(out_grads_kernel, n=n, sub=sub, rows_n=rows_n),
        [meta, *mixed, grad, s1, s2, bias],
        shapes,
        "out_grads",
        scratch=[pltpu.VMEM((n, heads, width), F32)],
    )


def far_message_kernel(far, sums, got, out):
    n = far.shape[0]
    out[:n, :] = (far[...] + got[n : 2 * n, :].astype(F32)).astype(BF)
    out[n:, :] = two_parts(sums[...] + both_parts(got[2 * n :, :]))


def far_message(far, sums, got):
    n, width = far.shape
    shape = jax.ShapeDtypeStruct((n + 32, width), BF)
    return small_call(far_message_kernel, shape, "far_message", us=0.7)(far, sums, got)


def col_messages_kernel(*refs, n, sub, added):
    (one, two, keep, sums, near, far), outs = refs[:6], refs[6:]
    count = n * sub
    both = sums[...] + both_parts(near[2 * count :, :]) + both_parts(far[count:, :])
    parts = two_parts(both)
    own = keep[...] + near[:count, :].astype(F32) + far[:count, :].astype(F32)
    units = one.shape[0] // n
    size = units if added else 2 * units
    for k in range(n):
        j = (n - k) % n
        at = slice(k * units, (k + 1) * units)
        if added:
            outs[k][:units, :] = (one[at, :].astype(F32) + two[at, :].astype(F32)).astype(BF)
        else:
            outs[k][:units, :] = one[at, :]
            outs[k][units:size, :] = two[at, :]
        outs[k][size : size + sub, :] = own[j * sub : (j + 1) * sub].astype(BF)
        outs[k][size + sub :, :] = parts


def col_messages(one, two, keep, sums, near, far, sub, n, added):
    rows, width = one.shape
    size = rows // n * (1 if added else 2)
    shapes = [jax.ShapeDtypeStruct((size + sub + 32, width), BF)] * n
    return small_call(
        functools.partial(col_messages_kernel, n=n, sub=sub, added=added), shapes, "col_messages"
    )(one, two, keep, sums, near, far)


def sum_messages_kernel(*refs):
    refs, out = refs[:-1], refs[-1]
    n = out.shape[0] - 32
    total = refs[0][:n, :].astype(F32)
    sums = both_parts(refs[0][n:, :])
    for ref in refs[1:]:
        total = total + ref[:n, :].astype(F32)
        sums = sums + both_parts(ref[n:, :])
    out[:n, :] = total.astype(BF)
    out[n:, :] = two_parts(sums)


def sum_messages(messages):
    shape = jax.ShapeDtypeStruct(messages[0].shape, BF)
    return small_call(sum_messages_kernel, shape, "sum_messages", us=0.7)(*messages)


def finish_kernel(meta, own, other, *refs, rows_n, units, sub, paired):
    ups, (down, out, sums) = refs[:rows_n], refs[rows_n:]
    size = own.shape[0] - sub - 32
    a = own[:size, :].astype(F32)
    b = other[:size, :].astype(F32)
    if paired:
        first = meta[4] == 0
        up = jnp.where(first, a, b)
        down[...] = jnp.where(first, b, a)
    else:
        up = a[:units] + b[:units]
        down[...] = a[units:] + b[units:]
    feat = up.shape[1] // rows_n
    pieces = [up[:, k * feat : (k + 1) * feat] for k in range(rows_n)]
    for k in range(rows_n):
        value = pieces[0]
        for owner in range(1, rows_n):
            value = jnp.where((meta[1] ^ k) == owner, pieces[owner], value)
        ups[k][...] = value.T.astype(BF)
    at = size + sub
    out[...] = own[size:at, :].astype(F32) + other[size:at, :].astype(F32)
    sums[...] = both_parts(own[at:, :]) + both_parts(other[at:, :])


def finish(meta, own, other, rows_n, units, sub, paired):
    width = own.shape[1]
    shapes = [jax.ShapeDtypeStruct((width // rows_n, units), BF)] * rows_n
    shapes += [jax.ShapeDtypeStruct((n, width), F32) for n in (units, sub, 16)]
    return meta_call(
        functools.partial(finish_kernel, rows_n=rows_n, units=units, sub=sub, paired=paired),
        [meta, own, other],
        shapes,
        "finish_grads",
    )


def up_grads_kernel(meta, *refs, n):
    pieces, out = refs[:n], refs[n]
    units = pieces[0].shape[1]
    values = [ref[...].astype(F32) for ref in pieces]
    for owner in range(n):
        value = values[0]
        for k in range(1, n):
            value = jnp.where((meta[1] ^ k) == owner, values[k], value)
        out[:, owner * units : (owner + 1) * units] = value


def up_grads(meta, pieces):
    feat, units = pieces[0].shape
    return meta_call(
        functools.partial(up_grads_kernel, n=len(pieces)),
        [meta, *pieces],
        [jax.ShapeDtypeStruct((feat, units * len(pieces)), F32)],
        "up_grads",
    )[0]


def join_kernel(keep0, keep1, near0, near1, far, dq, w_ref, *outs, scale, hw):
    n = len(outs) // 2
    each = outs[0].shape[0]
    half = keep0.shape[0]
    for k in range(n):
        at = slice(k * each, (k + 1) * each)
        inside = slice(at.start % half, at.start % half + each)
        keep, near = ((keep0, near0), (keep1, near1))[at.start // half]
        kv = keep[inside, :].astype(F32) + near[inside, :].astype(F32) + far[at, :].astype(F32)
        d = jnp.concatenate([(dq[at, :hw] * scale).astype(BF), kv.astype(BF)], axis=1)
        outs[k][...] = d
        outs[n + k][...] = nn(d, w_ref[...]).astype(outs[n + k].dtype)


def join_grads(keep, near, far, dq, w, n, scale):
    rows = dq.shape[0]
    wide, width = w.shape
    shapes = [jax.ShapeDtypeStruct((rows // n, wide), BF)] * n
    shapes += [jax.ShapeDtypeStruct((rows // n, width), BF)] * n
    kernel = functools.partial(join_kernel, scale=scale, hw=wide // 3)
    out = small_call(kernel, shapes, "join_grads")(*keep, *near, far, dq, w)
    return out[:n], out[n:]


def qkv_grads_kernel(meta, *refs, n, feat):
    x, grads, keep, far, send, send_far, total = refs[:n], refs[n : 2 * n], *refs[2 * n :]
    each = grads[0].shape[0]
    rows_of_x = jnp.concatenate([ref[:each, :] for ref in x], axis=0)
    g = jnp.concatenate([ref[...] for ref in grads], axis=0)
    total[...] = tn(rows_of_x, g)

    def rows(k):
        return total[pl.ds(pl.multiple_of((meta[1] ^ k) * feat, feat), feat), :]

    bias = col_sum(g.astype(F32))
    hi = bias.astype(BF).astype(F32)
    row = lax.broadcasted_iota(jnp.int32, (16, bias.shape[1]), 0)
    tail = jnp.where(row == 0, hi, jnp.where(row == 1, bias - hi, 0.0))
    keep[:feat, :] = rows(0)
    keep[feat:, :] = tail
    far[...] = rows(2)
    send[:feat, :] = rows(1).astype(BF)
    send[feat:, :] = tail.astype(BF)
    send_far[...] = rows(3).astype(BF)


def qkv_grads(meta, x, grads, feat):
    wide = grads[0].shape[1]
    width = x[0].shape[1]
    return meta_call(
        functools.partial(qkv_grads_kernel, n=len(x), feat=feat),
        [meta, *x, *grads],
        [
            jax.ShapeDtypeStruct((feat + 16, wide), F32),
            jax.ShapeDtypeStruct((feat, wide), F32),
            jax.ShapeDtypeStruct((feat + 16, wide), BF),
            jax.ShapeDtypeStruct((feat, wide), BF),
        ],
        "qkv_grads",
        scratch=[pltpu.VMEM((width, wide), F32)],
    )


def spread_kernel(meta, *refs, n):
    pieces, outs = refs[:n], refs[n:]
    hw = pieces[0].shape[1] // 3
    values = [ref[...].astype(F32) for ref in pieces]
    for j in range(n):
        away = meta[3] - j
        away = jnp.where(away < 0, away + n, away)
        value = values[0]
        for k in range(1, n):
            value = jnp.where(away == k, values[k], value)
        for i, out in enumerate(outs):
            out[:, j * hw : (j + 1) * hw] = value[:, i * hw : (i + 1) * hw]


def spread(meta, pieces):
    sub, wide = pieces[0].shape
    width = wide // 3 * len(pieces)
    return meta_call(
        functools.partial(spread_kernel, n=len(pieces)),
        [meta, *pieces],
        [jax.ShapeDtypeStruct((sub, width), F32)] * 3,
        "spread",
    )


def pack_kernel(meta, *refs, n):
    blocks, (down, bias, out, half) = refs[:n], refs[n:]
    units, feat = blocks[0].shape
    size = out.shape[0] // 2
    values = [ref[...].astype(F32) for ref in blocks]
    for owner in range(n):
        value = values[0]
        for k in range(1, n):
            value = jnp.where((meta[1] ^ k) == owner, values[k], value)
        out[:units, owner * feat : (owner + 1) * feat] = value.astype(BF)
    out[units:size, :] = bias[...]
    out[size : size + units, :] = down[...].astype(BF)
    out[size + units :, :] = jnp.zeros((size - units, out.shape[1]), BF)

    @pl.when(meta[4] == 0)
    def _():
        half[...] = out[:size, :]

    @pl.when(meta[4] != 0)
    def _():
        half[...] = out[size:, :]


def pack_weights(meta, blocks, down, bias):
    rows, width = down.shape
    size = rows + bias.shape[0]
    return meta_call(
        functools.partial(pack_kernel, n=len(blocks)),
        [meta, *blocks, down, bias],
        [jax.ShapeDtypeStruct((2 * size, width), BF), jax.ShapeDtypeStruct((size, width), BF)],
        "pack_weights",
    )


CORE = [(0, 1), (1, 0), (2, 3), (3, 2)]
CROSS = [(0, 2), (2, 0), (1, 3), (3, 1)]


def core_swap(x):
    return lax.ppermute(x, "row", CORE)


def cross_swap(x):
    return lax.ppermute(x, "row", CROSS)


def shift_col(x, step):
    n = lax.axis_size("col")
    return lax.ppermute(x, "col", [(i, (i + step) % n) for i in range(n)])


def after(x, *others):
    return lax.optimization_barrier((x,) + others)[0]


def natural_row(blocks):
    r = lax.axis_index("row")
    low = (r & 1) == 0
    b0, b1, b2, b3 = blocks
    left = jnp.where(low, jnp.stack([b0, b1]), jnp.stack([b1, b0]))
    right = jnp.where(low, jnp.stack([b2, b3]), jnp.stack([b3, b2]))
    return jnp.where(r < 2, jnp.concatenate([left, right]), jnp.concatenate([right, left]))


def gather_row_rel(x):
    far = cross_swap(x)
    near = core_swap(x)
    return [x, near, far, core_swap(far)]


def sum_dp(x):
    n = lax.axis_size("dp")
    if n == 2:
        return x + lax.ppermute(x, "dp", [(0, 1), (1, 0)])
    return lax.psum(x, "dp")


def split3(x):
    hi = lax.reduce_precision(x, 8, 7)
    mid = lax.reduce_precision(x - hi, 8, 7)
    low = x - hi - mid
    return hi.astype(BF), mid.astype(BF), low.astype(BF)


def per_device(
    tokens,
    cotangent,
    lengths,
    query_weight,
    key_weight,
    value_weight,
    query_bias,
    value_bias,
    out_weight,
    out_bias,
    norm1_gain,
    norm1_shift,
    up_weight,
    up_bias,
    down_weight,
    down_bias,
    norm2_gain,
    norm2_shift,
):
    rows_n = lax.axis_size("row")
    cols_n = lax.axis_size("col")
    r = lax.axis_index("row")
    z = lax.axis_index("col")
    local, width = tokens.shape
    block_len = local * cols_n
    hw = width // cols_n
    heads = hw // HD
    feat = width // rows_n
    scale = 1.0 / math.sqrt(HD)
    paired = lax.axis_size("dp") == 2
    pair = lax.axis_index("dp") if paired else jnp.zeros((), jnp.int32)
    meta = jnp.stack([lengths[0], r, z * (local * rows_n) + r * local, z, pair]).astype(jnp.int32)

    sub_out = out_weight.shape[0]
    x_blocks = [jnp.concatenate([tokens, out_weight.astype(BF)])]
    x_blocks.append(shift_col(x_blocks[0], 1))

    up_t = up_weight.astype(BF).T
    units = up_t.shape[0] // rows_n
    up_t = up_t.reshape(rows_n, units, feat)
    pieces = [lax.dynamic_index_in_dim(up_t, r ^ k, 0, keepdims=False) for k in range(4)]
    up_blocks = [
        pieces[0],
        core_swap(pieces[1]),
        cross_swap(pieces[2]),
        lax.ppermute(pieces[3], "row", [(i, i ^ 3) for i in range(rows_n)]),
    ]

    qkv = jnp.stack([query_weight, key_weight, value_weight], axis=1).astype(BF)
    sub = qkv.shape[0]
    qkv = qkv.reshape(sub, 3, cols_n, hw).transpose(2, 0, 1, 3).reshape(cols_n, sub, 3 * hw)
    pieces = []
    for k in range(cols_n):
        piece = lax.dynamic_index_in_dim(qkv, (z + k) % cols_n, 0, keepdims=False)
        pieces.append(shift_col(piece, k) if k else piece)
    second, *pieces = lax.optimization_barrier((x_blocks[1], *pieces))
    x_blocks.append(shift_col(second, 1))
    w_blocks = gather_row_rel(jnp.concatenate(pieces))
    for _ in range(3, cols_n):
        x_blocks.append(shift_col(x_blocks[-1], 1))

    bias_mine = lax.dynamic_slice_in_dim(up_bias, r * units, units, 0)
    bias_rows = jnp.pad(jnp.stack(split3(bias_mine)), ((0, 13), (0, width - units)))
    def cross_dp(x):
        return lax.ppermute(x, "dp", [(0, 1), (1, 0)]) if paired else x[:1]

    pack, half = pack_weights(meta, up_blocks, down_weight, bias_rows)
    hops = [shift_col(after(half if paired else pack, x_blocks[-1]), 1)]

    qkv_bias = jnp.concatenate([query_bias, jnp.zeros_like(value_bias), value_bias])
    qkv_bias = jnp.broadcast_to(qkv_bias[None], (8, 3 * hw))
    vecs = jnp.stack([out_bias, norm1_gain, norm1_shift, down_bias, norm2_gain, norm2_shift])
    vecs = jnp.pad(jnp.stack(split3(vecs)), ((0, 1), (0, 2), (0, width - feat))).reshape(32, width)
    early, late = (0, 1), tuple(range(2, cols_n))
    q_a, kv_a = project_qkv(meta, x_blocks[:2], early, cols_n, w_blocks, qkv_bias, local, scale)
    far_a, near_a = cross_swap(kv_a), core_swap(kv_a)
    x_blocks[-1], near_a, pack = lax.optimization_barrier((x_blocks[-1], near_a, pack))
    q_b, kv_b, w_qkv, out_pack = project_qkv(
        meta, x_blocks, late, cols_n, w_blocks, qkv_bias, local, scale, vecs
    )
    far_b, near_b = cross_swap(kv_b), core_swap(kv_b)
    near_b, far_a = lax.optimization_barrier((near_b, far_a))
    sizes = (rows_n, cols_n)
    q_parts = [q_a, q_b]
    acc, stat, k_near, v_near = attn_fwd(
        meta, q_parts, [kv_a, kv_b, near_a, near_b], (0, 1), heads, local, sizes, NEAR_COST
    )
    stat, hops[0] = lax.optimization_barrier((stat, hops[0]))
    hops.append(shift_col(hops[0], 1))
    crossed = [cross_dp(hops[0])]
    stat, far_a, far_b, out_pack = lax.optimization_barrier((stat, far_a, far_b, out_pack))
    out_far, out_near = cross_swap(out_pack), core_swap(out_pack)
    state = (acc, stat)
    far = [far_a, far_b, core_swap(far_a), core_swap(far_b)]
    *mixed_part, qb_rows, k_far, v_far = attn_fwd(
        meta, q_parts, far, (2, 3), heads, local, sizes, 4, state=state
    )
    *mixed_part, second, third, out_far, qb_rows = lax.optimization_barrier(
        (*mixed_part, hops[1], crossed[0], out_far, qb_rows)
    )
    hops[1], crossed[0] = second, third
    crossed.append(cross_dp(hops[1]))
    mixed = [mixed_part[0]] + [shift_col(mixed_part[k], -k) for k in range(1, cols_n)]

    out_packs = [out_pack, out_near, out_far, core_swap(out_far)]
    *mixed, third, crossed[1] = lax.optimization_barrier((*mixed, hops[1], crossed[1]))
    hops.append(shift_col(third, 1))
    crossed.append(cross_dp(hops[2]))
    packs = [pack]
    for hop, other in zip(hops, crossed):
        packs += [hop, other] if paired else [hop]
    hidden, hidden_low, normal1, inv1, out_full, vecs = project(meta, mixed, out_packs, tokens, sub_out)

    h_own, h_far, h_near = hidden_low, cross_swap(hidden_low), core_swap(hidden_low)
    h_near, h_far, packs[-1] = lax.optimization_barrier((h_near, h_far, packs[-1]))
    h_diag = core_swap(h_far)
    keep0, send0, act0, slope0 = ffn_fwd(meta, h_own, h_near, packs, units, units * cols_n)
    keep1, send1, act1, slope1 = ffn_fwd(meta, h_far, h_diag, packs, units, units * cols_n)
    far = (keep1 + core_swap(send1).astype(F32)).astype(BF)
    got_far = cross_swap(far)
    got_near = core_swap(send0)
    output, grad_resid2, grad_branch, sums2 = norm2(
        meta, hidden, keep0, got_near, got_far, cotangent, vecs
    )

    g_own, g_far, g_near = grad_branch, cross_swap(grad_branch), core_swap(grad_branch)
    keep0, send0, pre0 = ffn_bwd(meta, g_own, g_near, packs, slope0, units)
    g_far = after(g_far, send0)
    g_diag = core_swap(g_far)
    keep1, send1, pre1 = ffn_bwd(meta, g_far, g_diag, packs, slope1, units)
    far = (keep1 + core_swap(send1).astype(F32)).astype(BF)
    got_far = cross_swap(far)
    got_near = core_swap(send0)
    g_one, g_two, g_up_bias = ffn_grads(
        meta,
        (act0, act1),
        (pre0, pre1),
        (h_own, h_near, h_far, h_diag),
        (g_own, g_near, g_far, g_diag),
    )
    if paired:
        g_two = lax.ppermute(g_two, "dp", [(0, 1), (1, 0)])
    keep0 = after(keep0, g_one)
    grad_resid1, grad_attended, sums1, grad_mixed = norm1_back(
        keep0, got_near, got_far, grad_resid2, normal1, inv1, vecs, out_full
    )
    grad_mixed = [grad_mixed[0]] + [shift_col(grad_mixed[k], k) for k in range(1, cols_n)]

    out_keep, out_far, out_send, sums = out_grads(
        meta, mixed, grad_attended, sums1, sums2, g_up_bias, sub_out, rows_n
    )
    out_got = core_swap(out_send)
    out_got = after(out_got, grad_mixed[1])
    out_message = far_message(out_far, sums, out_got)
    out_got_far = cross_swap(out_message)
    messages = col_messages(
        g_one, g_two, out_keep, sums, out_got, out_got_far, sub_out, cols_n, paired
    )

    grads = after(grad_rows(mixed_part, grad_mixed, heads), out_message)
    dq = jnp.zeros((block_len, LANES), F32)
    *part3, dq = attn_bwd(1, qb_rows, grads, k_far, v_far, dq, heads, 4)
    got3 = [core_swap(part) for part in part3]
    dq = after(dq, messages[1])
    packed = shift_col(after(messages[1], dq), 1)
    *part2, dq = attn_bwd(0, qb_rows, grads, k_far, v_far, dq, heads, 4)
    far_sum = [(a.astype(F32) + b.astype(F32)).astype(BF) for a, b in zip(part2, got3)]
    far_sum = jnp.concatenate(far_sum)
    far_got = cross_swap(far_sum)
    packed = sum_messages([messages[2], packed])
    dq = after(dq, far_sum, packed)
    packed = shift_col(after(packed, dq), 1)
    *part1, dq = attn_bwd(1, qb_rows, grads, k_near, v_near, dq, heads, 4)
    got1 = [core_swap(part) for part in part1]
    packed = sum_messages([messages[3], packed])
    dq = after(dq, packed)
    packed = shift_col(after(packed, dq), 1)
    *part0, dq = attn_bwd(0, qb_rows, grads, k_near, v_near, dq, heads, C4)

    d_blocks, back = join_grads(part0, got1, far_got, dq, w_qkv, cols_n, scale)
    ring = [shift_col(back[1], 1)]

    d_blocks = [after(d_blocks[0], packed), *d_blocks[1:]]
    own, far, send, send_far = qkv_grads(meta, x_blocks, d_blocks, feat)
    packed = sum_messages([after(messages[0], back[1]), packed])
    got, got_far = core_swap(send), core_swap(send_far)
    ring[0], got, got_far, packed = lax.optimization_barrier((ring[0], got, got_far, packed))
    for step in range(2, cols_n + 1):
        total = back[step % cols_n].astype(F32) + ring[-1].astype(F32)
        if step < cols_n:
            ring.append(shift_col(total.astype(BF), 1))
    grad_tokens = grad_resid1 + total
    if paired:
        other = lax.ppermute(packed, "dp", [(0, 1), (1, 0)])
    else:
        other = lax.psum(packed.astype(F32), "dp") - packed.astype(F32)
    g_bias = own[feat] + own[feat + 1]

    def with_bias(block, bias):
        hi = lax.reduce_precision(bias, 8, 7)
        rows = jnp.pad(jnp.stack([hi, bias - hi]), ((0, 14), (0, 0)))
        return jnp.concatenate([block, rows]).astype(BF)

    def bias_of(got):
        return got[-16].astype(F32) + got[-15].astype(F32)

    g_bias = g_bias + bias_of(got)
    mine = own[:feat] + got[:feat].astype(F32)
    got_x = got = cross_swap(with_bias(far + got_far.astype(F32), g_bias))
    g_bias = g_bias + bias_of(got)
    mine = mine + got[:feat].astype(F32)
    if paired:
        got = lax.ppermute(after(with_bias(mine, g_bias), ring[0]), "dp", [(0, 1), (1, 0)])
        g_bias = g_bias + bias_of(got)
        g_qkv = mine + got[:feat].astype(F32)
    else:
        g_bias, g_qkv = lax.psum((g_bias, mine), "dp")
    g_qkv = g_qkv.astype(BF).reshape(cols_n, sub, 3 * hw)
    pieces = []
    for k in range(cols_n):
        piece = lax.dynamic_index_in_dim(g_qkv, (z + k) % cols_n, 0, keepdims=False)
        pieces.append(shift_col(piece, k) if k else piece)
    g_qkv = spread(meta, pieces)
    other = after(other, ring[1], got_x)
    *g_up, g_down_weight, g_out_weight, sums = finish(
        meta, packed, other, rows_n, units, sub_out, paired
    )
    g_up[1] = core_swap(g_up[1])
    g_up[2] = cross_swap(g_up[2])
    g_up[3] = lax.ppermute(g_up[3], "row", [(i, i ^ 3) for i in range(rows_n)])
    g_up_weight = up_grads(meta, g_up)
    vec_out = lax.dynamic_slice_in_dim(sums[:6], r * feat, feat, 1)
    g_up_bias = lax.dynamic_index_in_dim(sums[8 : 8 + cols_n], z, 0, keepdims=False)

    return (
        output,
        grad_tokens,
        g_qkv[0],
        g_qkv[1],
        g_qkv[2],
        g_bias[:hw],
        g_bias[2 * hw :],
        g_out_weight,
        vec_out[2],
        vec_out[0],
        vec_out[1],
        g_up_weight,
        g_up_bias,
        g_down_weight,
        vec_out[5],
        vec_out[3],
        vec_out[4],
    )


def solution(mesh):
    token_spec = P(("dp", "col", "row"), None)
    placed = (
        token_spec,
        token_spec,
        P("dp"),
        P(("row", "col"), None),
        P(("row", "col"), None),
        P(("row", "col"), None),
        P("col"),
        P("col"),
        P(("col", "row"), None),
        P("row"),
        P("row"),
        P("row"),
        P("row", "col"),
        P("col"),
        P(("col", "row"), None),
        P("row"),
        P("row"),
        P("row"),
    )
    return jax.shard_map(
        per_device,
        mesh=mesh,
        in_specs=placed,
        out_specs=(token_spec, token_spec) + placed[3:],
        check_vma=False,
    )
```

```python
import functools
import math

import jax
import jax.numpy as jnp
from jax import lax
from jax.experimental import pallas as pl
from jax.experimental.pallas import tpu as pltpu
from jax.sharding import PartitionSpec as P

HD = 64
LANES = 256
EPS = 1e-05
BF = jnp.bfloat16
F32 = jnp.float32
VMEM_BYTES = 60 * 1024 * 1024
TURNED = HD + 16
SMALL_BYTES = 24 * 1024 * 1024
ATTN_BYTES = 36 * 1024 * 1024
NEAR_COST = 4
C4 = 6


def nn(a, b):
    return jnp.dot(a, b, preferred_element_type=F32)


def tn(a, b):
    return lax.dot_general(a, b, (((0,), (0,)), ((), ())), preferred_element_type=F32)


def nt(a, b):
    return lax.dot_general(a, b, (((1,), (1,)), ((), ())), preferred_element_type=F32)


def cost(us):
    return pl.CostEstimate(flops=int(us * 0.6e9), bytes_accessed=1000, transcendentals=0)


def head_lanes(shape, head, width):
    lane = lax.broadcasted_iota(jnp.int32, shape, 1)
    mine = (lane >= head * HD) & (lane < (head + 1) * HD)
    return mine | (lane == width) | ((lane >= width + 1 + 3 * head) & (lane < width + 4 + 3 * head))


def three_parts(x):
    hi = x.astype(BF).astype(F32)
    mid = (x - hi).astype(BF).astype(F32)
    return hi, mid, x - hi - mid


def tail_rows(parts, ones, n):
    row = lax.broadcasted_iota(jnp.int32, (n, parts[0].shape[1]), 0)
    out = jnp.where(row == 0, ones, 0.0)
    for head, value in enumerate(parts):
        for i, piece in enumerate(three_parts(value)):
            out = jnp.where(row == 1 + 3 * head + i, piece, out)
    return out


def widen_keys(kv, owner, base, meta, keys_out, values_out, turned, at, width, shift, sizes):
    n = kv.shape[0]
    rows_n, cols_n = sizes
    keys_out[at : at + n, :width] = kv[:, :width]
    values_out[at : at + n, :width] = kv[:, width:]
    shape = (n, LANES - width)
    t = lax.broadcasted_iota(jnp.int32, shape, 0) + base
    lane = lax.broadcasted_iota(jnp.int32, shape, 1)
    source = meta[3] - (t >> shift)
    source = jnp.where(source < 0, source + cols_n, source)
    position = ((source * rows_n + owner) << shift) + (t & ((1 << shift) - 1))
    mask = jnp.where(lane == 0, jnp.where(position >= meta[0], -1e30, 0.0), 1.0)
    keys_out[at : at + n, width:] = mask.astype(BF)
    values_out[at : at + n, width:] = jnp.ones(shape, BF)
    flat = values_out[at : at + n, :].T
    for head in range(width // HD):
        first = head * TURNED
        turned[first : first + HD, at : at + n] = flat[head * HD : (head + 1) * HD, :]
        turned[first + HD : first + TURNED, at : at + n] = jnp.ones((TURNED - HD, n), BF)


def attn_fwd_kernel(*refs, heads, first, pair, shift, sizes, chunk, blocks, parts):
    meta, *refs = refs
    q_refs, refs = refs[:parts], refs[parts:]
    kvs, refs = refs[: 2 * parts], refs[2 * parts :]
    if first:
        acc_out, stat_out, k_out, v_out, turned = refs
    else:
        acc_in, stat_in = refs[:2]
        outs = refs[2 : 2 + blocks]
        qb_ref, k_out, v_out, turned = refs[2 + blocks :]
    width = heads * HD
    keys = k_out.shape[0]
    at = 0
    for i, ref in enumerate(kvs):
        base = at % (keys // 2)
        owner = meta[1] ^ pair[i // parts]
        widen_keys(ref[...], owner, base, meta, k_out, v_out, turned, at, width, shift, sizes)
        at += ref.shape[0]
    q = jnp.concatenate([ref[...] for ref in q_refs], axis=0)
    rows = q.shape[0]
    slot = lax.broadcasted_iota(jnp.int32, (16, rows), 0)
    stat = jnp.zeros((16, rows), F32)
    logs = []
    for head in range(heads):
        qh = jnp.where(head_lanes(q.shape, head, width), q, jnp.zeros_like(q))
        scores = [nt(k_out[i : i + chunk, :], qh) for i in range(0, keys, chunk)]
        peak = functools.reduce(
            jnp.maximum, [jnp.max(s, axis=0, keepdims=True) for s in scores]
        )
        if not first:
            old = stat_in[head : head + 1, :]
            peak = jnp.maximum(peak, old)
        acc = None
        for i, s in enumerate(scores):
            p = jnp.exp(s - peak).astype(BF)
            at = head * TURNED
            part = nn(turned[at : at + TURNED, i * chunk : (i + 1) * chunk], p)
            acc = part if acc is None else acc + part
        total = acc[HD : HD + 1]
        mine = slice(head * HD, (head + 1) * HD)
        if first:
            acc_out[mine, :] = acc[:HD]
            stat = jnp.where(slot == head, peak, stat)
            stat = jnp.where(slot == head + 8, total, stat)
        else:
            keep = jnp.exp(old - peak)
            total = total + stat_in[head + 8 : head + 9, :] * keep
            out = ((acc[:HD] + acc_in[mine, :] * keep) * (1.0 / total)).astype(BF)
            each = rows // blocks
            for b in range(blocks):
                outs[b][mine, :] = out[:, b * each : (b + 1) * each]
            logs.append(-(peak + jnp.log(total)))
    if first:
        stat_out[...] = stat
    else:
        qb_ref[:, :width] = q[:, :width]
        qb_ref[:, width:] = tail_rows(logs, 1.0, LANES - width).T.astype(BF)


def attn_fwd(meta, q, kvs, pair, heads, local, sizes, us, state=None, chunk=512):
    rows = sum(part.shape[0] for part in q)
    half = sum(kv.shape[0] for kv in kvs) // 2
    width = kvs[0].shape[1] // 2
    first = state is None
    blocks = rows // local
    vmem = pl.BlockSpec(memory_space=pltpu.VMEM)
    args = [meta, *q, *kvs]
    if first:
        out_shape = [jax.ShapeDtypeStruct((width, rows), F32), jax.ShapeDtypeStruct((16, rows), F32)]
    else:
        args += list(state)
        out_shape = [jax.ShapeDtypeStruct((width, local), BF)] * blocks
        out_shape += [jax.ShapeDtypeStruct((rows, LANES), BF)]
    out_shape += [jax.ShapeDtypeStruct((2 * half, LANES), BF)] * 2
    return pl.pallas_call(
        functools.partial(
            attn_fwd_kernel,
            heads=heads,
            first=first,
            pair=pair,
            shift=local.bit_length() - 1,
            sizes=sizes,
            chunk=chunk,
            blocks=blocks,
            parts=len(q),
        ),
        in_specs=[pl.BlockSpec(memory_space=pltpu.SMEM)] + [vmem] * (len(args) - 1),
        out_specs=[vmem] * len(out_shape),
        out_shape=out_shape,
        scratch_shapes=[pltpu.VMEM((heads * TURNED, 2 * half), BF)],
        compiler_params=pltpu.CompilerParams(vmem_limit_bytes=ATTN_BYTES),
        cost_estimate=cost(us),
        name="attn_fwd_near" if first else "attn_fwd_far",
    )(*args)


def grad_rows_kernel(*refs, heads, blocks):
    outs, grads, wide = refs[:blocks], refs[blocks : 2 * blocks], refs[2 * blocks]
    width = heads * HD
    for b in range(blocks):
        g = grads[b][...].astype(F32)
        prod = g * outs[b][...].astype(F32)
        each = g.shape[1]
        parts = [
            -jnp.sum(prod[head * HD : (head + 1) * HD], axis=0, keepdims=True) for head in range(heads)
        ]
        tall = jnp.concatenate([g, tail_rows(parts, 0.0, LANES - width)], axis=0)
        wide[b * each : (b + 1) * each, :] = tall.T.astype(BF)


def grad_rows(outs, grads, heads):
    each = outs[0].shape[1]
    return small_call(
        functools.partial(grad_rows_kernel, heads=heads, blocks=len(outs)),
        jax.ShapeDtypeStruct((each * len(outs), LANES), BF),
        "grad_rows",
    )(*outs, *grads)


def attn_bwd_kernel(at_ref, q_ref, g_ref, k_ref, v_ref, dq_in, *refs, heads, block, pieces):
    outs, (dq_out, dk, dv) = refs[:pieces], refs[pieces:]
    width = heads * HD
    half = dk.shape[0]
    keys = pl.ds(pl.multiple_of(at_ref[0] * half, half), half)
    dk[...] = jnp.zeros_like(dk)
    dv[...] = jnp.zeros_like(dv)

    def step(i, carry):
        at = pl.ds(pl.multiple_of(i * block, block), block)
        q_all = q_ref[at, :]
        g_all = g_ref[at, :]
        k = k_ref[keys, :]
        dq = jnp.zeros((block, LANES), F32)
        for head in range(heads):
            mine = head_lanes((block, LANES), head, width)
            q = jnp.where(mine, q_all, jnp.zeros_like(q_all))
            g = jnp.where(mine, g_all, jnp.zeros_like(g_all))
            p = jnp.exp(nt(k, q))
            ds = (p * nt(v_ref[keys, :], g)).astype(BF)
            dv[...] += nn(p.astype(BF), g)
            dk[...] += nn(ds, q)
            dq = jnp.where(mine, tn(ds, k), dq)
        dq_out[at, :] = dq_in[at, :] + dq
        return carry

    lax.fori_loop(0, q_ref.shape[0] // block, step, 0)
    each = outs[0].shape[0]
    for i, out in enumerate(outs):
        at = slice(i * each, (i + 1) * each)
        out[:, :width] = dk[at, :width].astype(out.dtype)
        out[:, width:] = dv[at, :width].astype(out.dtype)


def attn_bwd(at, q, g, k, v, dq, heads, us, pieces=2, block=1024):
    rows = q.shape[0]
    half = k.shape[0] // 2
    width = heads * HD
    vmem = pl.BlockSpec(memory_space=pltpu.VMEM)
    out_shape = [jax.ShapeDtypeStruct((half // pieces, 2 * width), BF)] * pieces
    return pl.pallas_call(
        functools.partial(attn_bwd_kernel, heads=heads, block=block, pieces=pieces),
        in_specs=[pl.BlockSpec(memory_space=pltpu.SMEM)] + [vmem] * 5,
        out_specs=[vmem] * (pieces + 1),
        out_shape=out_shape + [jax.ShapeDtypeStruct((rows, LANES), F32)],
        scratch_shapes=[pltpu.VMEM((half, LANES), F32)] * 2,
        compiler_params=pltpu.CompilerParams(vmem_limit_bytes=ATTN_BYTES),
        cost_estimate=cost(us),
        name="attn_bwd",
    )(jnp.full((1,), at, jnp.int32), q, g, k, v, dq)


def small_call(kernel, out_shape, name, scratch=(), us=1.4):
    return pl.pallas_call(
        kernel,
        out_shape=out_shape,
        scratch_shapes=scratch,
        compiler_params=pltpu.CompilerParams(vmem_limit_bytes=SMALL_BYTES),
        cost_estimate=cost(us),
        name=name,
    )


def meta_call(kernel, args, out_shape, name, scratch=(), us=1.2):
    vmem = pl.BlockSpec(memory_space=pltpu.VMEM)
    return pl.pallas_call(
        kernel,
        in_specs=[pl.BlockSpec(memory_space=pltpu.SMEM)] + [vmem] * (len(args) - 1),
        out_specs=[vmem] * len(out_shape),
        out_shape=out_shape,
        scratch_shapes=scratch,
        compiler_params=pltpu.CompilerParams(vmem_limit_bytes=SMALL_BYTES),
        cost_estimate=cost(us),
        name=name,
    )(*args)


def row_mean(x):
    return jnp.mean(x, axis=1, keepdims=True)


def col_sum(x):
    return jnp.sum(x, axis=0, keepdims=True)


def norm_forward(resid, gain, shift):
    centered = resid - row_mean(resid)
    inv = lax.rsqrt(row_mean(centered * centered) + EPS)
    normal = centered * inv
    return normal * gain + shift, normal, inv


def norm_backward(grad_out, normal, inv, gain):
    scaled = grad_out * gain
    return inv * (scaled - row_mean(scaled) - normal * row_mean(scaled * normal))


def project_qkv_kernel(meta, *refs, n, blocks, last, rows_n, cols_n, feat, hw, scale):
    x, ws, bias_ref = refs[:n], refs[n : n + rows_n], refs[n + rows_n]
    if last:
        vec_ref, q_ref, kv_ref, w_out, pack_ref, w_all = refs[n + rows_n + 1 :]
    else:
        q_ref, kv_ref, w_all = refs[n + rows_n + 1 :]
    each = feat // cols_n
    for k in range(rows_n):
        for m in range(cols_n):
            source = meta[3] - m
            source = jnp.where(source < 0, source + cols_n, source)
            at = pl.multiple_of((meta[1] ^ k) * feat + source * each, each)
            w_all[pl.ds(at, each), :] = ws[k][m * each : (m + 1) * each, :]
    w = w_all[...]
    each = q_ref.shape[0] // len(blocks)
    for i, k in enumerate(blocks):
        at = slice(i * each, (i + 1) * each)
        out = nn(x[k][:each, :], w) + bias_ref[0:1, :]
        q_ref[at, :hw] = (out[:, :hw].astype(BF).astype(F32) * scale).astype(BF)
        lane = lax.broadcasted_iota(jnp.int32, (each, LANES - hw), 1)
        q_ref[at, hw:] = jnp.where(lane == 0, 1.0, 0.0).astype(BF)
        kv_ref[at, :] = out[:, hw:].astype(BF)
    if last:
        w_out[...] = w.T
        more = x[0].shape[0] - each
        for k in range(n):
            pack_ref[k * more : (k + 1) * more, :] = x[k][each:, :]
        pack_ref[n * more :, :] = vec_ref[...]


def project_qkv(meta, x, blocks, cols_n, ws, bias, local, scale, vecs=None):
    feat, wide = ws[0].shape
    hw = wide // 3
    rows = local * len(blocks)
    shapes = [
        jax.ShapeDtypeStruct((rows, LANES), BF),
        jax.ShapeDtypeStruct((rows, 2 * hw), BF),
    ]
    args = [meta, *x, *ws, bias]
    if vecs is not None:
        args.append(vecs)
        more = (x[0].shape[0] - local) * len(x) + vecs.shape[0]
        shapes.append(jax.ShapeDtypeStruct((wide, feat * len(ws)), BF))
        shapes.append(jax.ShapeDtypeStruct((more, vecs.shape[1]), BF))
    return meta_call(
        functools.partial(
            project_qkv_kernel,
            n=len(x),
            blocks=blocks,
            last=vecs is not None,
            rows_n=len(ws),
            cols_n=cols_n,
            feat=feat,
            hw=hw,
            scale=scale,
        ),
        args,
        shapes,
        "project_qkv",
        scratch=[pltpu.VMEM((feat * len(ws), wide), BF)],
    )


def project_kernel(meta, *refs, n, rows_n, sub, feat):
    mixed, packs = refs[:n], refs[n : n + rows_n]
    x_ref, hid_ref, low_ref, normal_ref, inv_ref, w_ref, vec_ref = refs[n + rows_n :]
    r = meta[1]
    for k in range(rows_n):
        at = pl.multiple_of((r ^ k) * sub, sub)
        for i in range(n):
            w_ref[i, pl.ds(at, sub), :] = packs[k][((n - i) % n) * sub : ((n - i) % n + 1) * sub, :]
    values = []
    for k in range(rows_n):
        part = packs[k][n * sub : n * sub + 32, :feat].astype(F32)
        values.append(part[0:8] + part[8:16] + part[16:24])
    pieces = []
    for owner in range(rows_n):
        value = values[0]
        for k in range(1, rows_n):
            value = jnp.where((r ^ k) == owner, values[k], value)
        pieces.append(value)
    vecs = jnp.concatenate(pieces, axis=1)
    vec_ref[...] = vecs
    total = x_ref[...].astype(F32) + vecs[0:1, :]
    for j in range(n):
        total = total + tn(mixed[j][...], w_ref[j])
    hidden, normal, inv = norm_forward(total, vecs[1:2, :], vecs[2:3, :])
    hid_ref[...] = hidden
    low_ref[...] = hidden.astype(BF)
    normal_ref[...] = normal
    inv_ref[...] = jnp.broadcast_to(inv, inv_ref.shape)


def project(meta, mixed, packs, x, sub):
    rows, width = x.shape
    feat = width // len(packs)
    return meta_call(
        functools.partial(
            project_kernel, n=len(mixed), rows_n=len(packs), sub=sub, feat=feat
        ),
        [meta, *mixed, *packs, x],
        [
            jax.ShapeDtypeStruct((rows, width), F32),
            jax.ShapeDtypeStruct((rows, width), BF),
            jax.ShapeDtypeStruct((rows, width), F32),
            jax.ShapeDtypeStruct((rows, 128), F32),
            jax.ShapeDtypeStruct((len(mixed), sub * len(packs), width), BF),
            jax.ShapeDtypeStruct((8, width), F32),
        ],
        "project_norm1",
    )


def weight_rows(meta, packs, units, down):
    size = packs[0].shape[0] // 2
    at = size if down else 0
    values = [packs[0][at : at + units, :]]
    rest = packs[1:]
    if rest[0].shape[0] > size:
        return values + [ref[at : at + units, :] for ref in rest]
    mine = (meta[4] == 0) != down
    for own, other in zip(rest[::2], rest[1::2]):
        values.append(jnp.where(mine, own[:units, :].astype(F32), other[:units, :].astype(F32)).astype(BF))
    return values


def bias_rows(meta, packs, units):
    size = packs[0].shape[0] // 2
    at = slice(units, units + 16)
    values = [packs[0][at, :].astype(F32)]
    rest = packs[1:]
    if rest[0].shape[0] > size:
        values += [ref[at, :].astype(F32) for ref in rest]
    else:
        for own, other in zip(rest[::2], rest[1::2]):
            values.append(jnp.where(meta[4] == 0, own[at, :].astype(F32), other[at, :].astype(F32)))
    return jnp.concatenate([v[0:1, :units] + v[1:2, :units] + v[2:3, :units] for v in values], axis=1)


def ffn_fwd_kernel(meta, *refs, n, units):
    h0, h1 = refs[:2]
    packs = refs[2 : 2 + n]
    keep_ref, send_ref, act_ref, slope_ref = refs[2 + n :]
    rows = h0.shape[0]
    h = jnp.concatenate([h0[...], h1[...]], axis=0)
    up = jnp.concatenate(weight_rows(meta, packs, units, False), axis=0)
    x = nt(h, up) + bias_rows(meta, packs, units)
    cdf = 0.5 * (1.0 + lax.erf(x * math.sqrt(0.5)))
    act = (x * cdf).astype(BF)
    act_ref[...] = act
    slope = cdf + x * (math.sqrt(0.5 / math.pi) * jnp.exp(-0.5 * x * x))
    slope_ref[...] = slope.astype(BF)
    out = nn(act, jnp.concatenate(weight_rows(meta, packs, units, True), axis=0))
    keep_ref[...] = out[:rows].astype(BF)
    send_ref[...] = out[rows:].astype(BF)


def ffn_fwd(meta, h0, h1, packs, units, wide):
    rows, width = h0.shape
    return meta_call(
        functools.partial(ffn_fwd_kernel, n=len(packs), units=units),
        [meta, h0, h1, *packs],
        [
            jax.ShapeDtypeStruct((rows, width), BF),
            jax.ShapeDtypeStruct((rows, width), BF),
            jax.ShapeDtypeStruct((2 * rows, wide), BF),
            jax.ShapeDtypeStruct((2 * rows, wide), BF),
        ],
        "ffn_fwd",
        us=1.4,
    )


def ffn_bwd_kernel(meta, *refs, n, units):
    g0, g1 = refs[:2]
    packs = refs[2 : 2 + n]
    slope_ref, keep_ref, send_ref, pre_ref = refs[2 + n :]
    rows = g0.shape[0]
    g = jnp.concatenate([g0[...], g1[...]], axis=0)
    down = jnp.concatenate(weight_rows(meta, packs, units, True), axis=0)
    pre = (nt(g, down) * slope_ref[...].astype(F32)).astype(BF)
    pre_ref[...] = pre
    out = nn(pre, jnp.concatenate(weight_rows(meta, packs, units, False), axis=0))
    keep_ref[...] = out[:rows].astype(BF)
    send_ref[...] = out[rows:].astype(BF)


def ffn_bwd(meta, g0, g1, packs, slope, units):
    rows, width = g0.shape
    return meta_call(
        functools.partial(ffn_bwd_kernel, n=len(packs), units=units),
        [meta, g0, g1, *packs, slope],
        [
            jax.ShapeDtypeStruct((rows, width), BF),
            jax.ShapeDtypeStruct((rows, width), BF),
            jax.ShapeDtypeStruct(slope.shape, BF),
        ],
        "ffn_bwd",
        us=1.4,
    )


def ffn_grads_kernel(meta, *refs):
    act0, act1, pre0, pre1 = refs[:4]
    h = jnp.concatenate([ref[...] for ref in refs[4:8]], axis=0)
    g = jnp.concatenate([ref[...] for ref in refs[8:12]], axis=0)
    keep_ref, send_ref, bias_ref = refs[12:]
    pre = jnp.concatenate([pre0[...], pre1[...]], axis=0)
    act = jnp.concatenate([act0[...], act1[...]], axis=0)
    g_up = tn(pre, h).astype(BF)
    g_down = tn(act, g).astype(BF)
    first = meta[4] == 0

    @pl.when(first)
    def _():
        keep_ref[...] = g_up
        send_ref[...] = g_down

    @pl.when(jnp.logical_not(first))
    def _():
        keep_ref[...] = g_down
        send_ref[...] = g_up

    bias_ref[...] = jnp.broadcast_to(col_sum(pre.astype(F32)), bias_ref.shape)


def ffn_grads(meta, acts, pres, hiddens, grads):
    width = hiddens[0].shape[1]
    wide = acts[0].shape[1]
    return meta_call(
        ffn_grads_kernel,
        [meta, *acts, *pres, *hiddens, *grads],
        [
            jax.ShapeDtypeStruct((wide, width), BF),
            jax.ShapeDtypeStruct((wide, width), BF),
            jax.ShapeDtypeStruct((8, wide), F32),
        ],
        "ffn_grads",
    )


def norm2_kernel(
    meta, hid_ref, keep_ref, near_ref, far_ref, cot_ref, vec_ref, out_ref, grad_ref, low_ref, sum_ref
):
    branch = keep_ref[...].astype(F32) + near_ref[...].astype(F32) + far_ref[...].astype(F32) + vec_ref[3:4, :]
    gain = vec_ref[4:5, :]
    normed, normal, inv = norm_forward(hid_ref[...] + branch, gain, vec_ref[5:6, :])
    row = lax.broadcasted_iota(jnp.int32, (out_ref.shape[0], 1), 0)
    valid = (meta[2] + row < meta[0]).astype(F32)
    out_ref[...] = (normed * valid).astype(BF)
    grad_y = cot_ref[...].astype(F32) * valid
    grad = norm_backward(grad_y, normal, inv, gain)
    grad_ref[...] = grad
    low = grad.astype(BF)
    low_ref[...] = low
    sum_ref[...] = jnp.zeros_like(sum_ref)
    sum_ref[0:1, :] = col_sum(grad_y * normal)
    sum_ref[1:2, :] = col_sum(grad_y)
    sum_ref[2:3, :] = col_sum(low.astype(F32))


def norm2(meta, hidden, keep, near, far, cot, vecs):
    rows, width = hidden.shape
    shapes = [
        jax.ShapeDtypeStruct((rows, width), BF),
        jax.ShapeDtypeStruct((rows, width), F32),
        jax.ShapeDtypeStruct((rows, width), BF),
        jax.ShapeDtypeStruct((8, width), F32),
    ]
    return meta_call(norm2_kernel, [meta, hidden, keep, near, far, cot, vecs], shapes, "norm2_both")


def norm1_back_kernel(
    keep_ref, near_ref, far_ref, add_ref, normal_ref, inv_ref, vec_ref, w_ref, out_ref, low_ref, sum_ref, *mixed
):
    grad = keep_ref[...].astype(F32) + near_ref[...].astype(F32) + far_ref[...].astype(F32) + add_ref[...]
    normal = normal_ref[...]
    resid = norm_backward(grad, normal, inv_ref[:, 0:1], vec_ref[1:2, :])
    out_ref[...] = resid
    low = resid.astype(BF)
    low_ref[...] = low
    for j, ref in enumerate(mixed):
        ref[...] = nt(w_ref[j], low).astype(BF)
    sum_ref[...] = jnp.zeros_like(sum_ref)
    sum_ref[0:1, :] = col_sum(grad * normal)
    sum_ref[1:2, :] = col_sum(grad)
    sum_ref[2:3, :] = col_sum(low.astype(F32))


def norm1_back(keep, near, far, add, normal, inv, vecs, w):
    rows, width = add.shape
    out = small_call(
        norm1_back_kernel,
        [
            jax.ShapeDtypeStruct((rows, width), F32),
            jax.ShapeDtypeStruct((rows, width), BF),
            jax.ShapeDtypeStruct((8, width), F32),
        ]
        + [jax.ShapeDtypeStruct((w.shape[1], rows), BF)] * w.shape[0],
        "norm1_back",
    )(keep, near, far, add, normal, inv, vecs, w)
    return out[0], out[1], out[2], out[3:]


def two_parts(x):
    hi = x.astype(BF).astype(F32)
    return jnp.concatenate([hi, x - hi], axis=0).astype(BF)


def both_parts(rows):
    n = rows.shape[0] // 2
    return rows[:n].astype(F32) + rows[n:].astype(F32)


def out_grads_kernel(meta, *refs, n, rows_n, sub):
    mixed, grad, s1, s2, bias = refs[:n], *refs[n : n + 4]
    keep, far, send, sums, total = refs[n + 4 :]
    g = grad[...]
    for j in range(n):
        total[j] = nn(mixed[j][...], g)
    count = n * sub
    for j in range(n):
        at = slice(j * sub, (j + 1) * sub)

        def rows(k):
            return total[j, pl.ds(pl.multiple_of((meta[1] ^ k) * sub, sub), sub), :]

        keep[at, :] = rows(0)
        far[at, :] = rows(2)
        send[at, :] = rows(1).astype(BF)
        send[count + j * sub : count + (j + 1) * sub, :] = rows(3).astype(BF)
    sums[...] = jnp.zeros_like(sums)
    sums[0:3, :] = s1[0:3, :]
    sums[3:6, :] = s2[0:3, :]
    units = bias.shape[1] // n
    for j in range(n):
        away = meta[3] - j
        away = jnp.where(away < 0, away + n, away)
        value = bias[0:1, :units]
        for k in range(1, n):
            value = jnp.where(away == k, bias[0:1, k * units : (k + 1) * units], value)
        zero = jnp.zeros_like(value)
        row = [jnp.where(meta[1] == owner, value, zero) for owner in range(rows_n)]
        sums[8 + j : 9 + j, :] = jnp.concatenate(row, axis=1)
    send[2 * count :, :] = two_parts(sums[...])


def out_grads(meta, mixed, grad, s1, s2, bias, sub, rows_n):
    n, heads, width = len(mixed), mixed[0].shape[0], grad.shape[1]
    shapes = [
        jax.ShapeDtypeStruct((n * sub, width), F32),
        jax.ShapeDtypeStruct((n * sub, width), F32),
        jax.ShapeDtypeStruct((2 * n * sub + 32, width), BF),
        jax.ShapeDtypeStruct((16, width), F32),
    ]
    return meta_call(
        functools.partial(out_grads_kernel, n=n, sub=sub, rows_n=rows_n),
        [meta, *mixed, grad, s1, s2, bias],
        shapes,
        "out_grads",
        scratch=[pltpu.VMEM((n, heads, width), F32)],
    )


def far_message_kernel(far, sums, got, out):
    n = far.shape[0]
    out[:n, :] = (far[...] + got[n : 2 * n, :].astype(F32)).astype(BF)
    out[n:, :] = two_parts(sums[...] + both_parts(got[2 * n :, :]))


def far_message(far, sums, got):
    n, width = far.shape
    shape = jax.ShapeDtypeStruct((n + 32, width), BF)
    return small_call(far_message_kernel, shape, "far_message", us=0.7)(far, sums, got)


def col_messages_kernel(*refs, n, sub, added):
    (one, two, keep, sums, near, far), outs = refs[:6], refs[6:]
    count = n * sub
    both = sums[...] + both_parts(near[2 * count :, :]) + both_parts(far[count:, :])
    parts = two_parts(both)
    own = keep[...] + near[:count, :].astype(F32) + far[:count, :].astype(F32)
    units = one.shape[0] // n
    size = units if added else 2 * units
    for k in range(n):
        j = (n - k) % n
        at = slice(k * units, (k + 1) * units)
        if added:
            outs[k][:units, :] = (one[at, :].astype(F32) + two[at, :].astype(F32)).astype(BF)
        else:
            outs[k][:units, :] = one[at, :]
            outs[k][units:size, :] = two[at, :]
        outs[k][size : size + sub, :] = own[j * sub : (j + 1) * sub].astype(BF)
        outs[k][size + sub :, :] = parts


def col_messages(one, two, keep, sums, near, far, sub, n, added):
    rows, width = one.shape
    size = rows // n * (1 if added else 2)
    shapes = [jax.ShapeDtypeStruct((size + sub + 32, width), BF)] * n
    return small_call(
        functools.partial(col_messages_kernel, n=n, sub=sub, added=added), shapes, "col_messages"
    )(one, two, keep, sums, near, far)


def sum_messages_kernel(*refs):
    refs, out = refs[:-1], refs[-1]
    n = out.shape[0] - 32
    total = refs[0][:n, :].astype(F32)
    sums = both_parts(refs[0][n:, :])
    for ref in refs[1:]:
        total = total + ref[:n, :].astype(F32)
        sums = sums + both_parts(ref[n:, :])
    out[:n, :] = total.astype(BF)
    out[n:, :] = two_parts(sums)


def sum_messages(messages):
    shape = jax.ShapeDtypeStruct(messages[0].shape, BF)
    return small_call(sum_messages_kernel, shape, "sum_messages", us=0.7)(*messages)


def finish_kernel(meta, own, other, *refs, rows_n, units, sub, paired):
    ups, (down, out, sums) = refs[:rows_n], refs[rows_n:]
    size = own.shape[0] - sub - 32
    a = own[:size, :].astype(F32)
    b = other[:size, :].astype(F32)
    if paired:
        first = meta[4] == 0
        up = jnp.where(first, a, b)
        down[...] = jnp.where(first, b, a)
    else:
        up = a[:units] + b[:units]
        down[...] = a[units:] + b[units:]
    feat = up.shape[1] // rows_n
    pieces = [up[:, k * feat : (k + 1) * feat] for k in range(rows_n)]
    for k in range(rows_n):
        value = pieces[0]
        for owner in range(1, rows_n):
            value = jnp.where((meta[1] ^ k) == owner, pieces[owner], value)
        ups[k][...] = value.T.astype(BF)
    at = size + sub
    out[...] = own[size:at, :].astype(F32) + other[size:at, :].astype(F32)
    sums[...] = both_parts(own[at:, :]) + both_parts(other[at:, :])


def finish(meta, own, other, rows_n, units, sub, paired):
    width = own.shape[1]
    shapes = [jax.ShapeDtypeStruct((width // rows_n, units), BF)] * rows_n
    shapes += [jax.ShapeDtypeStruct((n, width), F32) for n in (units, sub, 16)]
    return meta_call(
        functools.partial(finish_kernel, rows_n=rows_n, units=units, sub=sub, paired=paired),
        [meta, own, other],
        shapes,
        "finish_grads",
    )


def up_grads_kernel(meta, *refs, n):
    pieces, out = refs[:n], refs[n]
    units = pieces[0].shape[1]
    values = [ref[...].astype(F32) for ref in pieces]
    for owner in range(n):
        value = values[0]
        for k in range(1, n):
            value = jnp.where((meta[1] ^ k) == owner, values[k], value)
        out[:, owner * units : (owner + 1) * units] = value


def up_grads(meta, pieces):
    feat, units = pieces[0].shape
    return meta_call(
        functools.partial(up_grads_kernel, n=len(pieces)),
        [meta, *pieces],
        [jax.ShapeDtypeStruct((feat, units * len(pieces)), F32)],
        "up_grads",
    )[0]


def join_kernel(keep0, keep1, near0, near1, far, dq, w_ref, *outs, scale, hw):
    n = len(outs) // 2
    each = outs[0].shape[0]
    half = keep0.shape[0]
    for k in range(n):
        at = slice(k * each, (k + 1) * each)
        inside = slice(at.start % half, at.start % half + each)
        keep, near = ((keep0, near0), (keep1, near1))[at.start // half]
        kv = keep[inside, :].astype(F32) + near[inside, :].astype(F32) + far[at, :].astype(F32)
        d = jnp.concatenate([(dq[at, :hw] * scale).astype(BF), kv.astype(BF)], axis=1)
        outs[k][...] = d
        outs[n + k][...] = nn(d, w_ref[...]).astype(outs[n + k].dtype)


def join_grads(keep, near, far, dq, w, n, scale):
    rows = dq.shape[0]
    wide, width = w.shape
    shapes = [jax.ShapeDtypeStruct((rows // n, wide), BF)] * n
    shapes += [jax.ShapeDtypeStruct((rows // n, width), BF)] * n
    kernel = functools.partial(join_kernel, scale=scale, hw=wide // 3)
    out = small_call(kernel, shapes, "join_grads")(*keep, *near, far, dq, w)
    return out[:n], out[n:]


def qkv_grads_kernel(meta, *refs, n, feat):
    x, grads, keep, far, send, send_far, total = refs[:n], refs[n : 2 * n], *refs[2 * n :]
    each = grads[0].shape[0]
    rows_of_x = jnp.concatenate([ref[:each, :] for ref in x], axis=0)
    g = jnp.concatenate([ref[...] for ref in grads], axis=0)
    total[...] = tn(rows_of_x, g)

    def rows(k):
        return total[pl.ds(pl.multiple_of((meta[1] ^ k) * feat, feat), feat), :]

    bias = col_sum(g.astype(F32))
    hi = bias.astype(BF).astype(F32)
    row = lax.broadcasted_iota(jnp.int32, (16, bias.shape[1]), 0)
    tail = jnp.where(row == 0, hi, jnp.where(row == 1, bias - hi, 0.0))
    keep[:feat, :] = rows(0)
    keep[feat:, :] = tail
    far[...] = rows(2)
    send[:feat, :] = rows(1).astype(BF)
    send[feat:, :] = tail.astype(BF)
    send_far[...] = rows(3).astype(BF)


def qkv_grads(meta, x, grads, feat):
    wide = grads[0].shape[1]
    width = x[0].shape[1]
    return meta_call(
        functools.partial(qkv_grads_kernel, n=len(x), feat=feat),
        [meta, *x, *grads],
        [
            jax.ShapeDtypeStruct((feat + 16, wide), F32),
            jax.ShapeDtypeStruct((feat, wide), F32),
            jax.ShapeDtypeStruct((feat + 16, wide), BF),
            jax.ShapeDtypeStruct((feat, wide), BF),
        ],
        "qkv_grads",
        scratch=[pltpu.VMEM((width, wide), F32)],
    )


def spread_kernel(meta, *refs, n):
    pieces, outs = refs[:n], refs[n:]
    hw = pieces[0].shape[1] // 3
    values = [ref[...].astype(F32) for ref in pieces]
    for j in range(n):
        away = meta[3] - j
        away = jnp.where(away < 0, away + n, away)
        value = values[0]
        for k in range(1, n):
            value = jnp.where(away == k, values[k], value)
        for i, out in enumerate(outs):
            out[:, j * hw : (j + 1) * hw] = value[:, i * hw : (i + 1) * hw]


def spread(meta, pieces):
    sub, wide = pieces[0].shape
    width = wide // 3 * len(pieces)
    return meta_call(
        functools.partial(spread_kernel, n=len(pieces)),
        [meta, *pieces],
        [jax.ShapeDtypeStruct((sub, width), F32)] * 3,
        "spread",
    )


def pack_kernel(meta, *refs, n):
    blocks, (down, bias, out, half) = refs[:n], refs[n:]
    units, feat = blocks[0].shape
    size = out.shape[0] // 2
    values = [ref[...].astype(F32) for ref in blocks]
    for owner in range(n):
        value = values[0]
        for k in range(1, n):
            value = jnp.where((meta[1] ^ k) == owner, values[k], value)
        out[:units, owner * feat : (owner + 1) * feat] = value.astype(BF)
    out[units:size, :] = bias[...]
    out[size : size + units, :] = down[...].astype(BF)
    out[size + units :, :] = jnp.zeros((size - units, out.shape[1]), BF)

    @pl.when(meta[4] == 0)
    def _():
        half[...] = out[:size, :]

    @pl.when(meta[4] != 0)
    def _():
        half[...] = out[size:, :]


def pack_weights(meta, blocks, down, bias):
    rows, width = down.shape
    size = rows + bias.shape[0]
    return meta_call(
        functools.partial(pack_kernel, n=len(blocks)),
        [meta, *blocks, down, bias],
        [jax.ShapeDtypeStruct((2 * size, width), BF), jax.ShapeDtypeStruct((size, width), BF)],
        "pack_weights",
    )


CORE = [(0, 1), (1, 0), (2, 3), (3, 2)]
CROSS = [(0, 2), (2, 0), (1, 3), (3, 1)]


def core_swap(x):
    return lax.ppermute(x, "row", CORE)


def cross_swap(x):
    return lax.ppermute(x, "row", CROSS)


def shift_col(x, step):
    n = lax.axis_size("col")
    return lax.ppermute(x, "col", [(i, (i + step) % n) for i in range(n)])


def after(x, *others):
    return lax.optimization_barrier((x,) + others)[0]


def natural_row(blocks):
    r = lax.axis_index("row")
    low = (r & 1) == 0
    b0, b1, b2, b3 = blocks
    left = jnp.where(low, jnp.stack([b0, b1]), jnp.stack([b1, b0]))
    right = jnp.where(low, jnp.stack([b2, b3]), jnp.stack([b3, b2]))
    return jnp.where(r < 2, jnp.concatenate([left, right]), jnp.concatenate([right, left]))


def gather_row_rel(x):
    far = cross_swap(x)
    near = core_swap(x)
    return [x, near, far, core_swap(far)]


def sum_dp(x):
    n = lax.axis_size("dp")
    if n == 2:
        return x + lax.ppermute(x, "dp", [(0, 1), (1, 0)])
    return lax.psum(x, "dp")


def split3(x):
    hi = lax.reduce_precision(x, 8, 7)
    mid = lax.reduce_precision(x - hi, 8, 7)
    low = x - hi - mid
    return hi.astype(BF), mid.astype(BF), low.astype(BF)


def per_device(
    tokens,
    cotangent,
    lengths,
    query_weight,
    key_weight,
    value_weight,
    query_bias,
    value_bias,
    out_weight,
    out_bias,
    norm1_gain,
    norm1_shift,
    up_weight,
    up_bias,
    down_weight,
    down_bias,
    norm2_gain,
    norm2_shift,
):
    rows_n = lax.axis_size("row")
    cols_n = lax.axis_size("col")
    r = lax.axis_index("row")
    z = lax.axis_index("col")
    local, width = tokens.shape
    block_len = local * cols_n
    hw = width // cols_n
    heads = hw // HD
    feat = width // rows_n
    scale = 1.0 / math.sqrt(HD)
    paired = lax.axis_size("dp") == 2
    pair = lax.axis_index("dp") if paired else jnp.zeros((), jnp.int32)
    meta = jnp.stack([lengths[0], r, z * (local * rows_n) + r * local, z, pair]).astype(jnp.int32)

    sub_out = out_weight.shape[0]
    x_blocks = [jnp.concatenate([tokens, out_weight.astype(BF)])]
    x_blocks.append(shift_col(x_blocks[0], 1))

    up_t = up_weight.astype(BF).T
    units = up_t.shape[0] // rows_n
    up_t = up_t.reshape(rows_n, units, feat)
    pieces = [lax.dynamic_index_in_dim(up_t, r ^ k, 0, keepdims=False) for k in range(4)]
    up_blocks = [
        pieces[0],
        core_swap(pieces[1]),
        cross_swap(pieces[2]),
        lax.ppermute(pieces[3], "row", [(i, i ^ 3) for i in range(rows_n)]),
    ]

    qkv = jnp.stack([query_weight, key_weight, value_weight], axis=1).astype(BF)
    sub = qkv.shape[0]
    qkv = qkv.reshape(sub, 3, cols_n, hw).transpose(2, 0, 1, 3).reshape(cols_n, sub, 3 * hw)
    pieces = []
    for k in range(cols_n):
        piece = lax.dynamic_index_in_dim(qkv, (z + k) % cols_n, 0, keepdims=False)
        pieces.append(shift_col(piece, k) if k else piece)
    second, *pieces = lax.optimization_barrier((x_blocks[1], *pieces))
    x_blocks.append(shift_col(second, 1))
    w_blocks = gather_row_rel(jnp.concatenate(pieces))
    for _ in range(3, cols_n):
        x_blocks.append(shift_col(x_blocks[-1], 1))

    bias_mine = lax.dynamic_slice_in_dim(up_bias, r * units, units, 0)
    bias_rows = jnp.pad(jnp.stack(split3(bias_mine)), ((0, 13), (0, width - units)))
    def cross_dp(x):
        return lax.ppermute(x, "dp", [(0, 1), (1, 0)]) if paired else x[:1]

    pack, half = pack_weights(meta, up_blocks, down_weight, bias_rows)
    hops = [shift_col(after(half if paired else pack, x_blocks[-1]), 1)]

    qkv_bias = jnp.concatenate([query_bias, jnp.zeros_like(value_bias), value_bias])
    qkv_bias = jnp.broadcast_to(qkv_bias[None], (8, 3 * hw))
    vecs = jnp.stack([out_bias, norm1_gain, norm1_shift, down_bias, norm2_gain, norm2_shift])
    vecs = jnp.pad(jnp.stack(split3(vecs)), ((0, 1), (0, 2), (0, width - feat))).reshape(32, width)
    early, late = (0, 1), tuple(range(2, cols_n))
    q_a, kv_a = project_qkv(meta, x_blocks[:2], early, cols_n, w_blocks, qkv_bias, local, scale)
    far_a, near_a = cross_swap(kv_a), core_swap(kv_a)
    x_blocks[-1], near_a, pack = lax.optimization_barrier((x_blocks[-1], near_a, pack))
    q_b, kv_b, w_qkv, out_pack = project_qkv(
        meta, x_blocks, late, cols_n, w_blocks, qkv_bias, local, scale, vecs
    )
    far_b, near_b = cross_swap(kv_b), core_swap(kv_b)
    near_b, far_a = lax.optimization_barrier((near_b, far_a))
    sizes = (rows_n, cols_n)
    q_parts = [q_a, q_b]
    acc, stat, k_near, v_near = attn_fwd(
        meta, q_parts, [kv_a, kv_b, near_a, near_b], (0, 1), heads, local, sizes, NEAR_COST
    )
    stat, hops[0] = lax.optimization_barrier((stat, hops[0]))
    hops.append(shift_col(hops[0], 1))
    crossed = [cross_dp(hops[0])]
    stat, far_a, far_b, out_pack = lax.optimization_barrier((stat, far_a, far_b, out_pack))
    out_far, out_near = cross_swap(out_pack), core_swap(out_pack)
    state = (acc, stat)
    far = [far_a, far_b, core_swap(far_a), core_swap(far_b)]
    *mixed_part, qb_rows, k_far, v_far = attn_fwd(
        meta, q_parts, far, (2, 3), heads, local, sizes, 4, state=state
    )
    *mixed_part, second, third, out_far, qb_rows = lax.optimization_barrier(
        (*mixed_part, hops[1], crossed[0], out_far, qb_rows)
    )
    hops[1], crossed[0] = second, third
    crossed.append(cross_dp(hops[1]))
    mixed = [mixed_part[0]] + [shift_col(mixed_part[k], -k) for k in range(1, cols_n)]

    out_packs = [out_pack, out_near, out_far, core_swap(out_far)]
    *mixed, third, crossed[1] = lax.optimization_barrier((*mixed, hops[1], crossed[1]))
    hops.append(shift_col(third, 1))
    crossed.append(cross_dp(hops[2]))
    packs = [pack]
    for hop, other in zip(hops, crossed):
        packs += [hop, other] if paired else [hop]
    hidden, hidden_low, normal1, inv1, out_full, vecs = project(meta, mixed, out_packs, tokens, sub_out)

    h_own, h_far, h_near = hidden_low, cross_swap(hidden_low), core_swap(hidden_low)
    h_near, h_far, packs[-1] = lax.optimization_barrier((h_near, h_far, packs[-1]))
    h_diag = core_swap(h_far)
    keep0, send0, act0, slope0 = ffn_fwd(meta, h_own, h_near, packs, units, units * cols_n)
    keep1, send1, act1, slope1 = ffn_fwd(meta, h_far, h_diag, packs, units, units * cols_n)
    far = (keep1.astype(F32) + core_swap(send1).astype(F32)).astype(BF)
    got_far = cross_swap(far)
    got_near = core_swap(send0)
    output, grad_resid2, grad_branch, sums2 = norm2(
        meta, hidden, keep0, got_near, got_far, cotangent, vecs
    )

    g_own, g_far, g_near = grad_branch, cross_swap(grad_branch), core_swap(grad_branch)
    keep0, send0, pre0 = ffn_bwd(meta, g_own, g_near, packs, slope0, units)
    g_far = after(g_far, send0)
    g_diag = core_swap(g_far)
    keep1, send1, pre1 = ffn_bwd(meta, g_far, g_diag, packs, slope1, units)
    far = (keep1.astype(F32) + core_swap(send1).astype(F32)).astype(BF)
    got_far = cross_swap(far)
    got_near = core_swap(send0)
    g_one, g_two, g_up_bias = ffn_grads(
        meta,
        (act0, act1),
        (pre0, pre1),
        (h_own, h_near, h_far, h_diag),
        (g_own, g_near, g_far, g_diag),
    )
    if paired:
        g_two = lax.ppermute(g_two, "dp", [(0, 1), (1, 0)])
    keep0 = after(keep0, g_one)
    grad_resid1, grad_attended, sums1, grad_mixed = norm1_back(
        keep0, got_near, got_far, grad_resid2, normal1, inv1, vecs, out_full
    )
    grad_mixed = [grad_mixed[0]] + [shift_col(grad_mixed[k], k) for k in range(1, cols_n)]

    out_keep, out_far, out_send, sums = out_grads(
        meta, mixed, grad_attended, sums1, sums2, g_up_bias, sub_out, rows_n
    )
    out_got = core_swap(out_send)
    out_got = after(out_got, grad_mixed[1])
    out_message = far_message(out_far, sums, out_got)
    out_got_far = cross_swap(out_message)
    messages = col_messages(
        g_one, g_two, out_keep, sums, out_got, out_got_far, sub_out, cols_n, paired
    )

    grads = after(grad_rows(mixed_part, grad_mixed, heads), out_message)
    dq = jnp.zeros((block_len, LANES), F32)
    *part3, dq = attn_bwd(1, qb_rows, grads, k_far, v_far, dq, heads, 4)
    got3 = [core_swap(part) for part in part3]
    dq = after(dq, messages[1])
    packed = shift_col(after(messages[1], dq), 1)
    *part2, dq = attn_bwd(0, qb_rows, grads, k_far, v_far, dq, heads, 4)
    far_sum = [(a.astype(F32) + b.astype(F32)).astype(BF) for a, b in zip(part2, got3)]
    far_sum = jnp.concatenate(far_sum)
    far_got = cross_swap(far_sum)
    packed = sum_messages([messages[2], packed])
    dq = after(dq, far_sum, packed)
    packed = shift_col(after(packed, dq), 1)
    *part1, dq = attn_bwd(1, qb_rows, grads, k_near, v_near, dq, heads, 4)
    got1 = [core_swap(part) for part in part1]
    packed = sum_messages([messages[3], packed])
    dq = after(dq, packed)
    packed = shift_col(after(packed, dq), 1)
    *part0, dq = attn_bwd(0, qb_rows, grads, k_near, v_near, dq, heads, C4)

    d_blocks, back = join_grads(part0, got1, far_got, dq, w_qkv, cols_n, scale)
    ring = [shift_col(back[1], 1)]

    d_blocks = [after(d_blocks[0], packed), *d_blocks[1:]]
    own, far, send, send_far = qkv_grads(meta, x_blocks, d_blocks, feat)
    packed = sum_messages([after(messages[0], back[1]), packed])
    got, got_far = core_swap(send), core_swap(send_far)
    ring[0], got, got_far, packed = lax.optimization_barrier((ring[0], got, got_far, packed))
    for step in range(2, cols_n + 1):
        total = back[step % cols_n].astype(F32) + ring[-1].astype(F32)
        if step < cols_n:
            ring.append(shift_col(total.astype(BF), 1))
    grad_tokens = grad_resid1 + total
    if paired:
        other = lax.ppermute(packed, "dp", [(0, 1), (1, 0)])
    else:
        other = lax.psum(packed.astype(F32), "dp") - packed.astype(F32)
    g_bias = own[feat] + own[feat + 1]

    def with_bias(block, bias):
        hi = lax.reduce_precision(bias, 8, 7)
        rows = jnp.pad(jnp.stack([hi, bias - hi]), ((0, 14), (0, 0)))
        return jnp.concatenate([block, rows]).astype(BF)

    def bias_of(got):
        return got[-16].astype(F32) + got[-15].astype(F32)

    g_bias = g_bias + bias_of(got)
    mine = own[:feat] + got[:feat].astype(F32)
    got_x = got = cross_swap(with_bias(far + got_far.astype(F32), g_bias))
    g_bias = g_bias + bias_of(got)
    mine = mine + got[:feat].astype(F32)
    if paired:
        got = lax.ppermute(after(with_bias(mine, g_bias), ring[0]), "dp", [(0, 1), (1, 0)])
        g_bias = g_bias + bias_of(got)
        g_qkv = mine + got[:feat].astype(F32)
    else:
        g_bias, g_qkv = lax.psum((g_bias, mine), "dp")
    g_qkv = g_qkv.astype(BF).reshape(cols_n, sub, 3 * hw)
    pieces = []
    for k in range(cols_n):
        piece = lax.dynamic_index_in_dim(g_qkv, (z + k) % cols_n, 0, keepdims=False)
        pieces.append(shift_col(piece, k) if k else piece)
    g_qkv = spread(meta, pieces)
    other = after(other, ring[1], got_x)
    *g_up, g_down_weight, g_out_weight, sums = finish(
        meta, packed, other, rows_n, units, sub_out, paired
    )
    g_up[1] = core_swap(g_up[1])
    g_up[2] = cross_swap(g_up[2])
    g_up[3] = lax.ppermute(g_up[3], "row", [(i, i ^ 3) for i in range(rows_n)])
    g_up_weight = up_grads(meta, g_up)
    vec_out = lax.dynamic_slice_in_dim(sums[:6], r * feat, feat, 1)
    g_up_bias = lax.dynamic_index_in_dim(sums[8 : 8 + cols_n], z, 0, keepdims=False)

    return (
        output,
        grad_tokens,
        g_qkv[0],
        g_qkv[1],
        g_qkv[2],
        g_bias[:hw],
        g_bias[2 * hw :],
        g_out_weight,
        vec_out[2],
        vec_out[0],
        vec_out[1],
        g_up_weight,
        g_up_bias,
        g_down_weight,
        vec_out[5],
        vec_out[3],
        vec_out[4],
    )


def solution(mesh):
    token_spec = P(("dp", "col", "row"), None)
    placed = (
        token_spec,
        token_spec,
        P("dp"),
        P(("row", "col"), None),
        P(("row", "col"), None),
        P(("row", "col"), None),
        P("col"),
        P("col"),
        P(("col", "row"), None),
        P("row"),
        P("row"),
        P("row"),
        P("row", "col"),
        P("col"),
        P(("col", "row"), None),
        P("row"),
        P("row"),
        P("row"),
    )
    return jax.shard_map(
        per_device,
        mesh=mesh,
        in_specs=placed,
        out_specs=(token_spec, token_spec) + placed[3:],
        check_vma=False,
    )
```
